128 devices in a mesh: bins: 16 (over y, z), chan: 8 (over x, core).
Axes of the slice: x: 4, y: 4, z: 4, core: 2. Of those that a mesh axis runs over, the one named last changes fastest.
Arguments:
- tokens_in: bfloat16 [8192, 2048], P('bins', 'chan'), may hold values from -6 to 6
- filters: bfloat16 [8192, 2048], P('bins', 'chan'), may hold values from -0.0625 to 0.0625
- gate: bfloat16 [8192, 2048], P('bins', 'chan'), may hold values from -6 to 6
- skip: float32 [2048], P('chan'), may hold values from 0.5 to 1.5
- out_grad: bfloat16 [8192, 4096], P('bins', 'chan'), may hold values from -6 to 6
- out_weight: bfloat16 [2048, 4096], P('chan'), may hold values from -0.09375 to 0.09375
- owner: int32 [16, 512], P(None, 'bins'), may hold values from 0 to 15, as said below
- slot: int32 [16, 512], P(None, 'bins'), may hold values from 0 to 1023, as said below
Outputs:
- gate_grad: bfloat16 [16, 512, 2048], P(None, 'bins', 'chan')
- filter_grad: float32 [16, 512, 2048], P(None, 'bins', 'chan')
- grad_rows: bfloat16 [16384, 2048], P('bins', 'chan')
The draws below stay inside these ranges and needn't reach their ends.
Inputs may be any that keep to these rules, and one draw needn't show every extreme that they name: Let the column group j be the entries [i, r] with j * 32 <= r < (j + 1) * 32, all i. Within one column group at most 64 entries name the same owner, and in every draw some owner is named exactly 64 times by every column group. An entry of column group j (as for owner) lies in j * 64 to (j + 1) * 64 - 1; no two tokens share an owner and a slot; in every draw some owner has all 1024 slots used.
All inputs are finite; a program needn't handle non-finite values.
Results may differ from the reference program's by a relative error of at most 0.012.
Values may be sent and summed in bfloat16 or wider, within the bound.
A program may use at most 128 MiB of HBM per device.

```python
import math
import jax
import jax.numpy as jnp

D = 4096
CH = 2048
TOK_DEV = 512
BLOCKS = 16
SEQ = 8192
NFFT = 16384
COLS = 32
SEND = 64
CAP = 1024


def shuffle_one(sub_key):
    return jax.random.permutation(sub_key, TOK_DEV)


def to_grid(held):
    return held.reshape(BLOCKS, BLOCKS, COLS).transpose(1, 0, 2).reshape(BLOCKS, TOK_DEV)


def placement_lists(key):
    base_key = jax.random.fold_in(key, 11)
    key_hot, key_shift, key_order, key_slots = jax.random.split(base_key, 4)
    hot_owner = jax.random.randint(key_hot, (), 0, BLOCKS)
    shifts = jax.random.randint(key_shift, (BLOCKS,), 0, BLOCKS - 1)
    places = jnp.arange(TOK_DEV, dtype=jnp.int32)
    others = (places[None, :] - SEND + shifts[:, None]) % (BLOCKS - 1)
    others = others + (others >= hot_owner).astype(jnp.int32)
    chosen = jnp.where(places[None, :] < SEND, hot_owner, others).astype(jnp.int32)
    shuffles = jax.vmap(shuffle_one)(jax.random.split(key_order, BLOCKS))
    owners_held = jnp.take_along_axis(chosen, shuffles, axis=1)
    one_hot = (owners_held[:, :, None] == jnp.arange(BLOCKS, dtype=jnp.int32)[None, None, :]).astype(jnp.int32)
    earlier = jnp.cumsum(one_hot, axis=1) - one_hot
    ranks = jnp.sum(earlier * one_hot, axis=2)
    scores = jax.random.randint(key_slots, (BLOCKS, BLOCKS, SEND), 0, 2 ** 18) * SEND + jnp.arange(SEND, dtype=jnp.int32)
    orders = jnp.argsort(scores, axis=2).astype(jnp.int32)
    holders = jnp.arange(BLOCKS, dtype=jnp.int32)[:, None]
    positions = orders[holders, owners_held, ranks]
    slots_held = holders * SEND + positions
    return (to_grid(owners_held).astype(jnp.int32), to_grid(slots_held).astype(jnp.int32))


def draw_owner(key, part):
    return placement_lists(key)[0]


def draw_slot(key, part):
    return placement_lists(key)[1]


def block_scale(key, extent, shards, low, largest):
    factor_of, own = 1.0, jax.random.fold_in(key, 6)
    for axis_at, blocks in shards:
        steps = jnp.exp(jax.random.uniform(jax.random.fold_in(own, axis_at), (blocks,), jnp.float32, low / len(shards), largest / len(shards)))
        factor_of = factor_of * jnp.repeat(steps, extent[axis_at] // blocks).reshape([-1 if axis == axis_at else 1 for axis in range(len(extent))])
    return factor_of


def noise(key, extent, scale, reach, cuts=(), held_as=jnp.bfloat16):
    gain = block_scale(key, extent, cuts, -0.22, 0.18) if cuts else 1.0
    entries = jax.random.normal(key, extent, jnp.float32) * scale * gain
    return jnp.minimum(jnp.maximum(entries, -reach), reach).astype(held_as)


def setup_inputs(seed: int = 0) -> dict:
    key_list = jax.random.split(jax.random.key(seed), 9)
    return {
        "tokens_in": noise(key_list[0], (SEQ, CH), 1.0, 6.0, ((0, 16), (1, 8))),
        "filters": noise(key_list[1], (SEQ, CH), SEQ ** -0.5, 0.0625, ((0, 16), (1, 8))),
        "gate": noise(key_list[2], (SEQ, CH), 1.0, 6.0, ((0, 16), (1, 8))),
        "skip": jnp.clip(0.5 + 1.0 * jax.random.uniform(key_list[3], (CH,), jnp.float32) ** block_scale(key_list[3], (CH,), ((0, 8),), -0.2, 0.2), 0.5, 1.5),
        "out_grad": noise(key_list[4], (SEQ, D), 1.0, 6.0, ((0, 16), (1, 8))),
        "out_weight": noise(key_list[5], (CH, D), D ** -0.5, 0.09375, ((0, 8),)),
        "owner": draw_owner(jax.random.fold_in(key_list[8], 71), 0),
        "slot": draw_slot(jax.random.fold_in(key_list[8], 71), 0),
    }


def reference(tokens_in, filters, gate, skip, out_grad, out_weight, owner, slot):
    g_rounded = jnp.dot(out_grad, out_weight.T, preferred_element_type=jnp.float32).astype(jnp.bfloat16)
    grad_in = (g_rounded.astype(jnp.float32) * gate.astype(jnp.float32)).astype(jnp.bfloat16)
    tok_real = tokens_in.astype(jnp.float32)
    spec_x = jnp.fft.rfft(tok_real, n=NFFT, axis=0)
    spec_h = jnp.fft.rfft(filters.astype(jnp.float32), n=NFFT, axis=0)
    spec_y = jnp.fft.rfft(grad_in.astype(jnp.float32), n=NFFT, axis=0)

    def inverse(spectrum):
        return jnp.fft.irfft(spectrum, n=NFFT, axis=0)[:SEQ]
    conv = inverse(spec_x * spec_h)
    gate_grad = (g_rounded.astype(jnp.float32) * (conv + skip * tok_real)).astype(jnp.bfloat16)
    token_grad = (inverse(jnp.conj(spec_h) * spec_y) + skip * grad_in.astype(jnp.float32)).astype(jnp.bfloat16)
    filter_grad = inverse(spec_y * jnp.conj(spec_x)) / math.sqrt(SEQ)
    targets = owner.reshape(-1) * CAP + slot.reshape(-1)
    grad_rows = jnp.zeros((BLOCKS * CAP, CH), jnp.bfloat16).at[targets].set(token_grad)
    return (gate_grad.reshape(BLOCKS, TOK_DEV, CH), filter_grad.reshape(BLOCKS, TOK_DEV, CH), grad_rows)
```

```python
import functools
import math

import jax
import jax.numpy as jnp
import numpy as np
from jax import lax
from jax.experimental import pallas as pl
from jax.experimental.pallas import tpu as pltpu
from jax.sharding import PartitionSpec as P

BLOCKS = 16
HELD = 16
ROWS = 512
HALF = BLOCKS + 1
LENGTH = 2 * BLOCKS * ROWS


def tables():
    k1 = np.arange(HALF)
    i = np.arange(BLOCKS)
    ang = 2.0 * np.pi * np.outer(k1, i) / (2 * BLOCKS)
    eye = np.eye(HELD)
    ahead = np.concatenate([np.kron(np.cos(ang), eye), np.kron(-np.sin(ang), eye)], axis=0)
    weight = np.where((k1 == 0) | (k1 == BLOCKS), 1.0, 2.0)[None, :] / LENGTH
    back_re = np.kron(weight * np.cos(ang).T, eye)
    back_im = np.kron(-(weight * np.sin(ang).T)[:, 1:BLOCKS], eye)
    back = np.concatenate([back_re, back_im], axis=1)
    r = np.arange(ROWS)
    twist = 2.0 * np.pi * np.outer(k1, r) / LENGTH
    inner = 2.0 * np.pi * (np.outer(r, r) % ROWS) / ROWS
    return (
        jnp.asarray(ahead, jnp.bfloat16),
        jnp.asarray(back, jnp.bfloat16),
        jnp.asarray(np.cos(twist)[:, None, :], jnp.float32),
        jnp.asarray(np.sin(twist)[:, None, :], jnp.float32),
        jnp.asarray(np.cos(inner), jnp.bfloat16),
        jnp.asarray(np.sin(inner), jnp.bfloat16),
    )


def mm(a, b):
    return jnp.dot(a, b, preferred_element_type=jnp.float32)


def stage_rows(value):
    return value.reshape(HALF, HELD, ROWS)


def flat(value):
    return value.reshape(HALF * HELD, ROWS)


def forward(value, ahead, tw_cos, tw_sin, in_cos, in_sin):
    part = mm(ahead, value)
    n = HALF * HELD
    re, im = stage_rows(part[:n]), stage_rows(part[n:])
    z_re = flat(re * tw_cos + im * tw_sin)
    z_im = flat(im * tw_cos - re * tw_sin)
    z = jnp.concatenate([z_re, z_im], axis=0).astype(jnp.bfloat16)
    by_cos, by_sin = mm(z, in_cos), mm(z, in_sin)
    return by_cos[:n] + by_sin[n:], by_cos[n:] - by_sin[:n]


def inverse(s_re, s_im, back, tw_cos, tw_sin, in_cos, in_sin):
    n = HALF * HELD
    q = jnp.concatenate([s_re, s_im], axis=0).astype(jnp.bfloat16)
    by_cos, by_sin = mm(q, in_cos), mm(q, in_sin)
    re, im = stage_rows(by_cos[:n] - by_sin[n:]), stage_rows(by_cos[n:] + by_sin[:n])
    t_re = flat(re * tw_cos - im * tw_sin)
    t_im = flat(im * tw_cos + re * tw_sin)[HELD : BLOCKS * HELD]
    t = jnp.concatenate([t_re, t_im], axis=0).astype(jnp.bfloat16)
    return mm(back, t)


def to_columns(value):
    group = lax.broadcasted_iota(jnp.int32, (HELD, 128), 1) // 32
    out = [[None] * 4 for _ in range(BLOCKS)]
    for i_hi in range(4):
        for j_hi in range(4):
            tiles = [
                value[(4 * i_hi + i_lo) * HELD : (4 * i_hi + i_lo + 1) * HELD, 128 * j_hi : 128 * (j_hi + 1)]
                for i_lo in range(4)
            ]
            for j_lo in range(4):
                acc = None
                for i_lo in range(4):
                    shift = (32 * (i_lo - j_lo)) % 128
                    turned = pltpu.roll(tiles[i_lo], shift, 1) if shift else tiles[i_lo]
                    acc = turned if acc is None else jnp.where(group == i_lo, turned, acc)
                out[4 * j_hi + j_lo][i_hi] = acc
    return jnp.concatenate([jnp.concatenate(row, axis=1) for row in out], axis=0)


def transform_kernel(
    x_ref, h_ref, gate_ref, g_ref, skip_ref, ahead, back, tw_cos, tw_sin, in_cos, in_sin, out_ref
):
    f32 = jnp.float32
    forward_tables = (ahead[...], tw_cos[...], tw_sin[...], in_cos[...], in_sin[...])
    inverse_tables = (back[...], tw_cos[...], tw_sin[...], in_cos[...], in_sin[...])
    x = x_ref[...]
    skip = skip_ref[...]
    x_re, x_im = forward(x, *forward_tables)
    h_re, h_im = forward(h_ref[...], *forward_tables)
    conv = inverse(x_re * h_re - x_im * h_im, x_re * h_im + x_im * h_re, *inverse_tables)
    g = g_ref[...].astype(f32)
    out_ref[0] = to_columns(g * (conv + skip * x.astype(f32))).astype(jnp.bfloat16)
    dy = (g * gate_ref[...].astype(f32)).astype(jnp.bfloat16)
    y_re, y_im = forward(dy, *forward_tables)
    grad = inverse(h_re * y_re + h_im * y_im, h_re * y_im - h_im * y_re, *inverse_tables)
    out_ref[1] = to_columns(grad + skip * dy.astype(f32)).astype(jnp.bfloat16)
    lag = inverse(y_re * x_re + y_im * x_im, y_im * x_re - y_re * x_im, *inverse_tables)
    out_ref[2] = to_columns(lag * (1.0 / math.sqrt(BLOCKS * ROWS))).astype(jnp.bfloat16)


def transform(x, h, gate, g, skip):
    return pl.pallas_call(
        transform_kernel,
        out_shape=jax.ShapeDtypeStruct((3, BLOCKS * HELD, ROWS), jnp.bfloat16),
        compiler_params=pltpu.CompilerParams(vmem_limit_bytes=48 << 20),
    )(x, h, gate, g, skip, *tables())


def shards(tokens_in, filters, gate, skip, out_grad, out_weight, owner, slot):
    my_index = lax.axis_index("bins")
    channels = tokens_in.shape[1]

    def spread(value):
        return lax.all_to_all(value, "bins", split_axis=0, concat_axis=0, tiled=True)

    early = jnp.stack([v.T.reshape(BLOCKS, HELD, ROWS) for v in (tokens_in, filters, gate)], axis=1)
    early = spread(early)
    upstream = lax.dot_general(
        out_weight,
        lax.all_gather(out_grad, "chan", axis=1, tiled=True),
        (((1,), (1,)), ((), ())),
        preferred_element_type=jnp.float32,
    ).astype(jnp.bfloat16)
    g = spread(upstream.reshape(BLOCKS, HELD, ROWS)).reshape(BLOCKS * HELD, ROWS)
    x, h, gates = (early[:, n].reshape(BLOCKS * HELD, ROWS) for n in range(3))
    own_skip = jnp.tile(lax.dynamic_slice_in_dim(skip, my_index * HELD, HELD), BLOCKS)[:, None]
    done = transform(x, h, gates, g, own_skip)
    done = spread(done.reshape(3, BLOCKS, HELD, ROWS).transpose(1, 0, 2, 3))
    gate_grad, token_grad, filter_grad = (done[:, n].reshape(channels, ROWS) for n in range(3))
    gate_grad = gate_grad.T.reshape(BLOCKS, ROWS // BLOCKS, channels)
    filter_grad = filter_grad.T.reshape(BLOCKS, ROWS // BLOCKS, channels).astype(jnp.float32)
    send_rows = 2 * ROWS // BLOCKS
    targets = owner.reshape(1, -1) * send_rows + slot.reshape(1, -1) - my_index * send_rows
    places = lax.broadcasted_iota(jnp.int32, (BLOCKS * send_rows, ROWS), 0)
    chosen = (places == targets).astype(jnp.bfloat16)
    outbox = lax.dot_general(
        chosen, token_grad, (((1,), (1,)), ((), ())), preferred_element_type=jnp.float32
    ).astype(jnp.bfloat16)
    inbox = spread(outbox.reshape(BLOCKS, send_rows, channels))
    return (gate_grad, filter_grad, inbox.reshape(BLOCKS * send_rows, channels))


def solution(mesh):
    return jax.shard_map(
        shards,
        mesh=mesh,
        in_specs=(
            P("bins", "chan"),
            P("bins", "chan"),
            P("bins", "chan"),
            P("chan"),
            P("bins", "chan"),
            P("chan", None),
            P(None, "bins"),
            P(None, "bins"),
        ),
        out_specs=(P(None, "bins", "chan"), P(None, "bins", "chan"), P("bins", "chan")),
        check_vma=False,
    )
```

```python
import functools
import math

import jax
import jax.numpy as jnp
import numpy as np
from jax import lax
from jax.experimental import pallas as pl
from jax.experimental.pallas import tpu as pltpu
from jax.sharding import PartitionSpec as P

BLOCKS = 16
HELD = 16
ROWS = 512
HALF = BLOCKS + 1
LENGTH = 2 * BLOCKS * ROWS


def tables():
    k1 = np.arange(HALF)
    i = np.arange(BLOCKS)
    ang = 2.0 * np.pi * np.outer(k1, i) / (2 * BLOCKS)
    eye = np.eye(HELD)
    ahead = np.concatenate([np.kron(np.cos(ang), eye), np.kron(-np.sin(ang), eye)], axis=0)
    weight = np.where((k1 == 0) | (k1 == BLOCKS), 1.0, 2.0)[None, :] / LENGTH
    back_re = np.kron(weight * np.cos(ang).T, eye)
    back_im = np.kron(-(weight * np.sin(ang).T)[:, 1:BLOCKS], eye)
    back = np.concatenate([back_re, back_im], axis=1)
    r = np.arange(ROWS)
    twist = 2.0 * np.pi * np.outer(k1, r) / LENGTH
    inner = 2.0 * np.pi * (np.outer(r, r) % ROWS) / ROWS
    return (
        jnp.asarray(ahead, jnp.bfloat16),
        jnp.asarray(back, jnp.bfloat16),
        jnp.asarray(np.cos(twist)[:, None, :], jnp.float32),
        jnp.asarray(np.sin(twist)[:, None, :], jnp.float32),
        jnp.asarray(np.cos(inner), jnp.bfloat16),
        jnp.asarray(np.sin(inner), jnp.bfloat16),
    )


def mm(a, b):
    return jnp.dot(a, b, preferred_element_type=jnp.float32)


def stage_rows(value):
    return value.reshape(HALF, HELD, ROWS)


def flat(value):
    return value.reshape(HALF * HELD, ROWS)


def forward(value, ahead, tw_cos, tw_sin, in_cos, in_sin):
    part = mm(ahead, value)
    n = HALF * HELD
    re, im = stage_rows(part[:n]), stage_rows(part[n:])
    z_re = flat(re * tw_cos + im * tw_sin)
    z_im = flat(im * tw_cos - re * tw_sin)
    z = jnp.concatenate([z_re, z_im], axis=0).astype(jnp.bfloat16)
    by_cos, by_sin = mm(z, in_cos), mm(z, in_sin)
    return by_cos[:n] + by_sin[n:], by_cos[n:] - by_sin[:n]


def inverse(s_re, s_im, back, tw_cos, tw_sin, in_cos, in_sin):
    n = HALF * HELD
    q = jnp.concatenate([s_re, s_im], axis=0).astype(jnp.bfloat16)
    by_cos, by_sin = mm(q, in_cos), mm(q, in_sin)
    re, im = stage_rows(by_cos[:n] - by_sin[n:]), stage_rows(by_cos[n:] + by_sin[:n])
    t_re = flat(re * tw_cos - im * tw_sin)
    t_im = flat(im * tw_cos + re * tw_sin)[HELD : BLOCKS * HELD]
    t = jnp.concatenate([t_re, t_im], axis=0).astype(jnp.bfloat16)
    return mm(back, t)


def to_columns(value):
    group = lax.broadcasted_iota(jnp.int32, (HELD, 128), 1) // 32
    out = [[None] * 4 for _ in range(BLOCKS)]
    for i_hi in range(4):
        for j_hi in range(4):
            tiles = [
                value[(4 * i_hi + i_lo) * HELD : (4 * i_hi + i_lo + 1) * HELD, 128 * j_hi : 128 * (j_hi + 1)]
                for i_lo in range(4)
            ]
            for j_lo in range(4):
                acc = None
                for i_lo in range(4):
                    shift = (32 * (i_lo - j_lo)) % 128
                    turned = pltpu.roll(tiles[i_lo], shift, 1) if shift else tiles[i_lo]
                    acc = turned if acc is None else jnp.where(group == i_lo, turned, acc)
                out[4 * j_hi + j_lo][i_hi] = acc
    return jnp.concatenate([jnp.concatenate(row, axis=1) for row in out], axis=0)


def transform_kernel(early_ref, g_ref, skip_ref, ahead, back, tw_cos, tw_sin, in_cos, in_sin, out_ref):
    f32 = jnp.float32
    forward_tables = (ahead[...], tw_cos[...], tw_sin[...], in_cos[...], in_sin[...])
    inverse_tables = (back[...], tw_cos[...], tw_sin[...], in_cos[...], in_sin[...])
    rows = BLOCKS * HELD
    x = early_ref[:, 0].reshape(rows, ROWS)
    skip = skip_ref[...]
    x_re, x_im = forward(x, *forward_tables)
    h_re, h_im = forward(early_ref[:, 1].reshape(rows, ROWS), *forward_tables)
    conv = inverse(x_re * h_re - x_im * h_im, x_re * h_im + x_im * h_re, *inverse_tables)
    g = jnp.concatenate([g_ref[0].reshape(rows, ROWS // 2), g_ref[1].reshape(rows, ROWS // 2)], axis=1)
    g = g.astype(f32)
    gate = early_ref[:, 2].reshape(rows, ROWS).astype(f32)

    def put(n, value):
        out_ref[n] = to_columns(value).astype(jnp.bfloat16).reshape(BLOCKS, HELD, ROWS)

    put(2, g * (conv + skip * x.astype(f32)))
    dy = (g * gate).astype(jnp.bfloat16)
    y_re, y_im = forward(dy, *forward_tables)
    grad = inverse(h_re * y_re + h_im * y_im, h_re * y_im - h_im * y_re, *inverse_tables)
    put(0, grad + skip * dy.astype(f32))
    lag = inverse(y_re * x_re + y_im * x_im, y_im * x_re - y_re * x_im, *inverse_tables)
    put(1, lag * (1.0 / math.sqrt(BLOCKS * ROWS)))


def transform(early, g, skip):
    return pl.pallas_call(
        transform_kernel,
        out_shape=jax.ShapeDtypeStruct((3, BLOCKS, HELD, ROWS), jnp.bfloat16),
        compiler_params=pltpu.CompilerParams(vmem_limit_bytes=48 << 20),
    )(early, g, skip, *tables())


def remote(src, dst, send, recv, bins, chan):
    return pltpu.make_async_remote_copy(
        src_ref=src,
        dst_ref=dst,
        send_sem=send,
        recv_sem=recv,
        device_id=(bins, chan),
        device_id_type=pl.DeviceIdType.MESH,
    )


def each(first, last, body):
    def step(p, carry):
        body(p)
        return carry

    lax.fori_loop(first, last, step, 0)


def front_kernel(
    x_ref, h_ref, gate_ref, og_hbm, w_hbm, early_out, g_out,
    w_all, og_all, acc, early_src, g_src,
    local_sem, w_sem, mate_sem, side_send, side_recv, far_send, far_recv, early_send, early_recv, g_send, g_recv,
):
    b = lax.axis_index("bins")
    k = lax.axis_index("chan")
    chip, core = lax.div(k, 2), lax.rem(k, 2)
    right, left, across = lax.rem(chip + 1, 4), lax.rem(chip + 3, 4), lax.rem(chip + 2, 4)
    mate = 2 * chip + 1 - core

    own_w = pltpu.make_async_copy(w_hbm, w_all.at[core], local_sem.at[0])
    own_w.start()
    own_og = pltpu.make_async_copy(og_hbm.at[core], og_all.at[k], local_sem.at[1])
    own_og.start()

    barrier = pltpu.get_barrier_semaphore()

    def greet(bins, chan):
        pl.semaphore_signal(barrier, inc=1, device_id=(bins, chan), device_id_type=pl.DeviceIdType.MESH)

    each(1, BLOCKS, lambda p: greet(lax.rem(b + p, BLOCKS), k))
    each(0, BLOCKS, lambda p: greet(lax.rem(b + p, BLOCKS), mate))
    for side in (right, left):
        for c in range(2):
            greet(b, 2 * side + c)
    pl.semaphore_wait(barrier, 2 * BLOCKS - 1 + 4)

    def side_copy(way, part, c):
        to = (right, left)[way]
        return remote(
            og_hbm.at[c, part], og_all.at[k, part],
            side_send.at[way, part, c], side_recv.at[way, part, core], b, 2 * to + c,
        )

    for turn in range(2):
        for c in range(2):
            side_copy(0, turn, c).start()
            side_copy(1, 1 - turn, c).start()
    mate_og = remote(og_hbm.at[1 - core], og_all.at[k], mate_sem.at[0], mate_sem.at[1], b, mate)
    mate_og.start()
    mate_w = remote(w_hbm, w_all.at[core], w_sem.at[0], w_sem.at[1], b, mate)
    mate_w.start()

    for n, ref in enumerate((x_ref, h_ref, gate_ref)):
        early_src[:, n] = ref[...].T.reshape(BLOCKS, HELD, ROWS)

    def early_copy(p):
        to = lax.rem(b + p, BLOCKS)
        return remote(early_src.at[to], early_out.at[b], early_send.at[p], early_recv.at[p], to, k)

    each(1, BLOCKS, lambda p: early_copy(p).start())
    own_early = pltpu.make_async_copy(early_src.at[b], early_out.at[b], local_sem.at[2])
    own_early.start()

    def side_arrived(way, part, c):
        src = 2 * (left, right)[way] + c
        return remote(
            og_hbm.at[c, part], og_all.at[src, part],
            side_send.at[way, part, c], side_recv.at[way, part, c], b, mate,
        )

    def far_copy(way, c):
        src = 2 * (left, right)[way] + c
        to = (right, left)[way]
        return remote(
            og_all.at[src, way], og_all.at[src, way],
            far_send.at[way, c], far_recv.at[way, c], b, 2 * to + core,
        )

    for c in range(2):
        for way in range(2):
            side_arrived(way, way, c).wait_recv()
            far_copy(way, c).start()

    def gather(source, first=False):
        columns = pl.ds(pl.multiple_of(source * ROWS, ROWS), ROWS)
        weights = w_all[:, :, columns].reshape(2 * BLOCKS * HELD, ROWS)
        term = lax.dot_general(
            weights, og_all[source].reshape(ROWS // 2, ROWS), (((1,), (1,)), ((), ())),
            preferred_element_type=jnp.float32,
        )
        acc[...] = term if first else acc[...] + term

    own_w.wait()
    own_og.wait()
    mate_w.wait()
    mate_og.wait()
    gather(k, True)
    gather(mate)
    for c in range(2):
        for way in range(2):
            side_arrived(way, 1 - way, c).wait_recv()
            gather(2 * (left, right)[way] + c)
    for c in range(2):
        for way in range(2):
            far_copy(way, c).wait_recv()
        gather(2 * across + c)
    g_src[...] = acc[...].astype(jnp.bfloat16).reshape(2, BLOCKS, HELD, ROWS // 2)

    def g_copy(p, c):
        to = lax.rem(b + p, BLOCKS)
        hand = lax.rem(core + c, 2)
        return remote(
            g_src.at[hand, to], g_out.at[core, b], g_send.at[c, p], g_recv.at[c, p], to, 2 * chip + hand
        )

    each(1, BLOCKS, lambda p: g_copy(p, 0).start())
    each(0, BLOCKS, lambda p: g_copy(p, 1).start())
    own_g = pltpu.make_async_copy(g_src.at[core, b], g_out.at[core, b], local_sem.at[3])
    own_g.start()

    each(1, BLOCKS, lambda p: early_copy(p).wait())
    own_early.wait()
    each(1, BLOCKS, lambda p: g_copy(p, 0).wait())
    each(0, BLOCKS, lambda p: g_copy(p, 1).wait())
    own_g.wait()
    for c in range(2):
        for way in range(2):
            far_copy(way, c).wait_send()
            for part in range(2):
                side_copy(way, part, c).wait_send()


def front(x, h, gate, out_grad, out_weight):
    half = ROWS // 2
    dma = pltpu.SemaphoreType.DMA
    vmem, hbm = pl.BlockSpec(memory_space=pltpu.VMEM), pl.BlockSpec(memory_space=pl.ANY)
    bf16 = jnp.bfloat16
    return pl.pallas_call(
        front_kernel,
        out_shape=(
            jax.ShapeDtypeStruct((BLOCKS, 3, HELD, ROWS), bf16),
            jax.ShapeDtypeStruct((2, BLOCKS, HELD, half), bf16),
        ),
        in_specs=[vmem, vmem, vmem, hbm, hbm],
        out_specs=(vmem, vmem),
        scratch_shapes=[
            pltpu.VMEM((2, BLOCKS * HELD, 8 * ROWS), bf16),
            pltpu.VMEM((8, 2, half // 2, ROWS), bf16),
            pltpu.VMEM((2 * BLOCKS * HELD, half), jnp.float32),
            pltpu.VMEM((BLOCKS, 3, HELD, ROWS), bf16),
            pltpu.VMEM((2, BLOCKS, HELD, half), bf16),
            dma((4,)), dma((2,)), dma((2,)), dma((2, 2, 2)), dma((2, 2, 2)), dma((2, 2)), dma((2, 2)),
            dma((BLOCKS,)), dma((BLOCKS,)), dma((2, BLOCKS)), dma((2, BLOCKS)),
        ],
        compiler_params=pltpu.CompilerParams(
            collective_id=0, has_side_effects=True, vmem_limit_bytes=48 << 20
        ),
    )(x, h, gate, out_grad.reshape(2, 2, half // 2, ROWS), out_weight)


def tail_kernel(
    done_ref, target_ref, gate_out, filter_out, rows_out, came, outbox, local_sem, done_send, done_recv, box_send, box_recv
):
    b = lax.axis_index("bins")
    k = lax.axis_index("chan")
    send_rows = 2 * ROWS // BLOCKS
    barrier = pltpu.get_barrier_semaphore()

    def greet(p):
        pl.semaphore_signal(
            barrier, inc=1, device_id=(lax.rem(b + p, BLOCKS), k), device_id_type=pl.DeviceIdType.MESH
        )

    each(1, BLOCKS, greet)
    pl.semaphore_wait(barrier, BLOCKS - 1)

    def done_copy(n, p):
        to = lax.rem(b + p, BLOCKS)
        return remote(done_ref.at[n, to], came.at[n, b], done_send.at[n, p], done_recv.at[n, p], to, k)

    own_done = [pltpu.make_async_copy(done_ref.at[n, b], came.at[n, b], local_sem.at[n]) for n in range(3)]
    for n in range(3):
        each(1, BLOCKS, lambda p, n=n: done_copy(n, p).start())
        own_done[n].start()
    places = lax.broadcasted_iota(jnp.int32, (BLOCKS * send_rows, ROWS), 0)
    chosen = jnp.where(places == target_ref[...], 1.0, 0.0).astype(jnp.bfloat16)

    def arrived(n):
        each(1, BLOCKS, lambda p: done_copy(n, p).wait())
        own_done[n].wait()
        return came[n].reshape(BLOCKS * HELD, ROWS)

    box = lax.dot_general(
        chosen, arrived(0), (((1,), (1,)), ((), ())), preferred_element_type=jnp.float32
    ).astype(jnp.bfloat16)
    outbox[...] = box.reshape(BLOCKS, send_rows, BLOCKS * HELD)

    def box_copy(p):
        to = lax.rem(b + p, BLOCKS)
        return remote(outbox.at[to], rows_out.at[b], box_send.at[p], box_recv.at[p], to, k)

    each(1, BLOCKS, lambda p: box_copy(p).start())
    own_box = pltpu.make_async_copy(outbox.at[b], rows_out.at[b], local_sem.at[3])
    own_box.start()
    gate_out[...] = arrived(2).T
    filter_out[...] = arrived(1).T.astype(jnp.float32)
    each(1, BLOCKS, lambda p: box_copy(p).wait())
    own_box.wait()


def tail(done, targets):
    dma = pltpu.SemaphoreType.DMA
    vmem = pl.BlockSpec(memory_space=pltpu.VMEM)
    bf16 = jnp.bfloat16
    channels, send_rows = BLOCKS * HELD, 2 * ROWS // BLOCKS
    return pl.pallas_call(
        tail_kernel,
        out_shape=(
            jax.ShapeDtypeStruct((ROWS, channels), bf16),
            jax.ShapeDtypeStruct((ROWS, channels), jnp.float32),
            jax.ShapeDtypeStruct((BLOCKS, send_rows, channels), bf16),
        ),
        in_specs=[vmem, vmem],
        out_specs=(vmem, vmem, vmem),
        scratch_shapes=[
            pltpu.VMEM((3, BLOCKS, HELD, ROWS), bf16),
            pltpu.VMEM((BLOCKS, send_rows, channels), bf16),
            dma((4,)), dma((3, BLOCKS)), dma((3, BLOCKS)), dma((BLOCKS,)), dma((BLOCKS,)),
        ],
        compiler_params=pltpu.CompilerParams(
            collective_id=1, has_side_effects=True, vmem_limit_bytes=48 << 20
        ),
    )(done, targets)


def shards(tokens_in, filters, gate, skip, out_grad, out_weight, owner, slot):
    my_index = lax.axis_index("bins")
    channels = tokens_in.shape[1]
    send_rows = 2 * ROWS // BLOCKS
    early, g = front(tokens_in, filters, gate, out_grad, out_weight)
    own_skip = jnp.tile(lax.dynamic_slice_in_dim(skip, my_index * HELD, HELD), BLOCKS)[:, None]
    done = transform(early, g, own_skip)
    targets = owner.reshape(1, -1) * send_rows + slot.reshape(1, -1) - my_index * send_rows
    gate_grad, filter_grad, grad_rows = tail(done, targets)
    grid = (BLOCKS, ROWS // BLOCKS, channels)
    return (gate_grad.reshape(grid), filter_grad.reshape(grid), grad_rows.reshape(BLOCKS * send_rows, channels))


def solution(mesh):
    return jax.shard_map(
        shards,
        mesh=mesh,
        in_specs=(
            P("bins", "chan"),
            P("bins", "chan"),
            P("bins", "chan"),
            P("chan"),
            P("bins", "chan"),
            P("chan", None),
            P(None, "bins"),
            P(None, "bins"),
        ),
        out_specs=(P(None, "bins", "chan"), P(None, "bins", "chan"), P("bins", "chan")),
        check_vma=False,
    )
```

```python
import math

import jax
import jax.numpy as jnp
import numpy as np
from jax import lax
from jax.experimental import pallas as pl
from jax.experimental.pallas import tpu as pltpu
from jax.sharding import PartitionSpec as P

BLOCKS = 16
HELD = 16
ROWS = 512
HALF = BLOCKS + 1
LENGTH = 2 * BLOCKS * ROWS


def tables():
    k1 = np.arange(HALF)
    i = np.arange(BLOCKS)
    ang = 2.0 * np.pi * np.outer(k1, i) / (2 * BLOCKS)
    eye = np.eye(HELD)
    ahead = np.concatenate([np.kron(np.cos(ang), eye), np.kron(-np.sin(ang), eye)], axis=0)
    weight = np.where((k1 == 0) | (k1 == BLOCKS), 1.0, 2.0)[None, :] / LENGTH
    back_re = np.kron(weight * np.cos(ang).T, eye)
    back_im = np.kron(-(weight * np.sin(ang).T)[:, 1:BLOCKS], eye)
    back = np.concatenate([back_re, back_im], axis=1)
    r = np.arange(ROWS)
    twist = 2.0 * np.pi * np.outer(k1, r) / LENGTH
    inner = 2.0 * np.pi * (np.outer(r, r) % ROWS) / ROWS
    return (
        jnp.asarray(ahead, jnp.bfloat16),
        jnp.asarray(back, jnp.bfloat16),
        jnp.asarray(np.cos(twist)[:, None, :], jnp.float32),
        jnp.asarray(np.sin(twist)[:, None, :], jnp.float32),
        jnp.asarray(np.cos(inner), jnp.bfloat16),
        jnp.asarray(np.sin(inner), jnp.bfloat16),
    )


def mm(a, b):
    return jnp.dot(a, b, preferred_element_type=jnp.float32)


def stage_rows(value):
    return value.reshape(HALF, HELD, ROWS)


def flat(value):
    return value.reshape(HALF * HELD, ROWS)


def forward(value, ahead, tw_cos, tw_sin, in_cos, in_sin):
    part = mm(ahead, value)
    n = HALF * HELD
    re, im = stage_rows(part[:n]), stage_rows(part[n:])
    z_re = flat(re * tw_cos + im * tw_sin)
    z_im = flat(im * tw_cos - re * tw_sin)
    z = jnp.concatenate([z_re, z_im], axis=0).astype(jnp.bfloat16)
    by_cos, by_sin = mm(z, in_cos), mm(z, in_sin)
    return by_cos[:n] + by_sin[n:], by_cos[n:] - by_sin[:n]


def inverse(s_re, s_im, back, tw_cos, tw_sin, in_cos, in_sin):
    n = HALF * HELD
    q = jnp.concatenate([s_re, s_im], axis=0).astype(jnp.bfloat16)
    by_cos, by_sin = mm(q, in_cos), mm(q, in_sin)
    re, im = stage_rows(by_cos[:n] - by_sin[n:]), stage_rows(by_cos[n:] + by_sin[:n])
    t_re = flat(re * tw_cos - im * tw_sin)
    t_im = flat(im * tw_cos + re * tw_sin)[HELD : BLOCKS * HELD]
    t = jnp.concatenate([t_re, t_im], axis=0).astype(jnp.bfloat16)
    return mm(back, t)


def to_columns(value):
    group = lax.broadcasted_iota(jnp.int32, (HELD, 128), 1) // 32
    out = [[None] * 4 for _ in range(BLOCKS)]
    for i_hi in range(4):
        for j_hi in range(4):
            tiles = [
                value[(4 * i_hi + i_lo) * HELD : (4 * i_hi + i_lo + 1) * HELD, 128 * j_hi : 128 * (j_hi + 1)]
                for i_lo in range(4)
            ]
            for j_lo in range(4):
                acc = None
                for i_lo in range(4):
                    shift = (32 * (i_lo - j_lo)) % 128
                    turned = pltpu.roll(tiles[i_lo], shift, 1) if shift else tiles[i_lo]
                    acc = turned if acc is None else jnp.where(group == i_lo, turned, acc)
                out[4 * j_hi + j_lo][i_hi] = acc
    return jnp.concatenate([jnp.concatenate(row, axis=1) for row in out], axis=0)


def remote(src, dst, send, recv, bins, chan):
    return pltpu.make_async_remote_copy(
        src_ref=src,
        dst_ref=dst,
        send_sem=send,
        recv_sem=recv,
        device_id=(bins, chan),
        device_id_type=pl.DeviceIdType.MESH,
    )


def kernel(
    x_hbm, h_hbm, gate_hbm, skip_hbm, og_hbm, w_hbm, owner_hbm, slot_hbm, *rest
):
    tables_hbm, rest = rest[:TABLES], rest[TABLES:]
    gate_out, filter_out, rows_out = rest[:3]
    (
        raw, skip_ref, owner_ref, slot_ref, *rest
    ) = rest[3:]
    tables_ref, rest = rest[:TABLES], rest[TABLES:]
    (
        w_all, og_all, acc, early_src, early, g_src, g_came, done, came, outbox, chosen,
        local_sem, w_sem, mate_sem, side_send, side_recv, far_send, far_recv,
        early_send, early_recv, g_send, g_recv, done_send, done_recv, box_send, box_recv,
    ) = rest
    f32, bf16 = jnp.float32, jnp.bfloat16
    rows = BLOCKS * HELD
    send_rows = 2 * ROWS // BLOCKS
    b = lax.axis_index("bins")
    k = lax.axis_index("chan")
    b_y, b_z = lax.div(b, 4), lax.rem(b, 4)
    chip, core = lax.div(k, 2), lax.rem(k, 2)
    right, left, across = lax.rem(chip + 1, 4), lax.rem(chip + 3, 4), lax.rem(chip + 2, 4)
    mate = 2 * chip + 1 - core

    def peer(p):
        return 4 * lax.rem(b_y + p // 4, 4) + lax.rem(b_z + p % 4, 4)

    local = []

    def bring(src, dst):
        copy = pltpu.make_async_copy(src, dst, local_sem.at[len(local)])
        copy.start()
        local.append(copy)
        return copy

    own_raw = [bring(ref, raw.at[n]) for n, ref in enumerate((x_hbm, h_hbm, gate_hbm))]
    own_og = bring(og_hbm.at[core], og_all.at[k])
    own_w = bring(w_hbm, w_all.at[core])
    own_small = [bring(*pair) for pair in ((skip_hbm, skip_ref), (owner_hbm, owner_ref), (slot_hbm, slot_ref))]
    own_tables = [bring(*pair) for pair in zip(tables_hbm, tables_ref)]

    barrier = pltpu.get_barrier_semaphore()

    def greet(bins, chan):
        pl.semaphore_signal(barrier, inc=1, device_id=(bins, chan), device_id_type=pl.DeviceIdType.MESH)

    for p in ORDER:
        greet(peer(p), k)
        greet(peer(p), mate)
    greet(b, mate)
    for side in (right, left):
        for c in range(2):
            greet(b, 2 * side + c)
    pl.semaphore_wait(barrier, 2 * BLOCKS - 1 + 4)

    def side_copy(way, part, c):
        to = (right, left)[way]
        return remote(
            og_hbm.at[c, part], og_all.at[k, part],
            side_send.at[way, part, c], side_recv.at[way, part, core], b, 2 * to + c,
        )

    for turn in range(2):
        for c in range(2):
            side_copy(0, turn, c).start()
            side_copy(1, 1 - turn, c).start()
    mate_og = remote(og_hbm.at[1 - core], og_all.at[k], mate_sem.at[0], mate_sem.at[1], b, mate)
    mate_og.start()
    mate_w = remote(w_hbm, w_all.at[core], w_sem.at[0], w_sem.at[1], b, mate)
    mate_w.start()

    for n in range(3):
        own_raw[n].wait()
        early_src[:, n] = raw[n].T.reshape(BLOCKS, HELD, ROWS)

    def early_copy(p):
        to = peer(p)
        return remote(early_src.at[to], early.at[b], early_send.at[p], early_recv.at[p], to, k)

    for p in ORDER:
        early_copy(p).start()
    own_early = bring(early_src.at[b], early.at[b])

    def side_arrived(way, part, c):
        src = 2 * (left, right)[way] + c
        return remote(
            og_hbm.at[c, part], og_all.at[src, part],
            side_send.at[way, part, c], side_recv.at[way, part, c], b, mate,
        )

    def far_copy(way, c):
        src = 2 * (left, right)[way] + c
        to = (right, left)[way]
        return remote(
            og_all.at[src, way], og_all.at[src, way],
            far_send.at[way, c], far_recv.at[way, c], b, 2 * to + core,
        )

    for c in range(2):
        for way in range(2):
            side_arrived(way, way, c).wait_recv()
            far_copy(way, c).start()

    def gather(source, first=False):
        columns = pl.ds(pl.multiple_of(source * ROWS, ROWS), ROWS)
        weights = w_all[:, :, columns].reshape(2 * rows, ROWS)
        term = lax.dot_general(
            weights, og_all[source].reshape(ROWS // 2, ROWS), (((1,), (1,)), ((), ())), preferred_element_type=f32
        )
        acc[...] = term if first else acc[...] + term

    own_w.wait()
    own_og.wait()
    mate_w.wait()
    mate_og.wait()
    gather(k, True)
    gather(mate)
    for c in range(2):
        for way in range(2):
            side_arrived(way, 1 - way, c).wait_recv()
            gather(2 * (left, right)[way] + c)
    for copy in own_small + own_tables:
        copy.wait()
    for c in range(2):
        for way in range(2):
            far_copy(way, c).wait_recv()
        gather(2 * across + c)
    g_src[...] = acc[...].astype(bf16).reshape(2, BLOCKS, HELD, ROWS // 2)

    def g_copy(p, c):
        to = peer(p)
        hand = lax.rem(core + c, 2)
        return remote(
            g_src.at[hand, to], g_came.at[core, b], g_send.at[c, p], g_recv.at[c, p], to, 2 * chip + hand
        )

    for p in ORDER:
        g_copy(p, 0).start()
        g_copy(p, 1).start()
    g_copy(0, 1).start()
    own_g = bring(g_src.at[core, b], g_came.at[core, b])

    for p in ORDER:
        early_copy(p).wait()
    own_early.wait()
    ahead, back, tw_cos, tw_sin, in_cos, in_sin = (ref[...] for ref in tables_ref)
    forward_tables = (ahead, tw_cos, tw_sin, in_cos, in_sin)
    inverse_tables = (back, tw_cos, tw_sin, in_cos, in_sin)
    x = early[:, 0].reshape(rows, ROWS)
    x_re, x_im = forward(x, *forward_tables)
    h_re, h_im = forward(early[:, 1].reshape(rows, ROWS), *forward_tables)
    conv = inverse(x_re * h_re - x_im * h_im, x_re * h_im + x_im * h_re, *inverse_tables)
    lanes = lax.broadcasted_iota(jnp.int32, (rows, rows), 1)
    held = lax.rem(lax.broadcasted_iota(jnp.int32, (rows, rows), 0), HELD)
    skip = jnp.sum(jnp.where(lanes == held + HELD * b, skip_ref[...], 0.0), axis=1, keepdims=True)
    with_skip = conv + skip * x.astype(f32)
    target = owner_ref[...] * send_rows + slot_ref[...] - b * send_rows
    target = jnp.concatenate([target[i : i + 1] for i in range(BLOCKS)], axis=1)
    places = lax.broadcasted_iota(jnp.int32, (BLOCKS * send_rows, ROWS), 0)
    chosen[...] = jnp.where(places == target, 1.0, 0.0).astype(bf16)

    for p in ORDER:
        g_copy(p, 0).wait()
        g_copy(p, 1).wait()
    g_copy(0, 1).wait()
    own_g.wait()
    g = jnp.concatenate([g_came[0].reshape(rows, ROWS // 2), g_came[1].reshape(rows, ROWS // 2)], axis=1)
    g = g.astype(f32)
    dy = (g * early[:, 2].reshape(rows, ROWS).astype(f32)).astype(bf16)
    y_re, y_im = forward(dy, *forward_tables)

    def done_copy(n, p):
        to = peer(p)
        return remote(done.at[n, to], came.at[n, b], done_send.at[n, p], done_recv.at[n, p], to, k)

    own_done = []

    def put(n, value):
        done[n] = to_columns(value).astype(bf16).reshape(BLOCKS, HELD, ROWS)
        for p in ORDER:
            done_copy(n, p).start()
        own_done.append(bring(done.at[n, b], came.at[n, b]))

    grad = inverse(h_re * y_re + h_im * y_im, h_re * y_im - h_im * y_re, *inverse_tables)
    put(0, grad + skip * dy.astype(f32))
    lag = inverse(y_re * x_re + y_im * x_im, y_im * x_re - y_re * x_im, *inverse_tables)
    put(1, lag * (1.0 / math.sqrt(BLOCKS * ROWS)))
    put(2, g * with_skip)

    def arrived(n):
        for p in ORDER:
            done_copy(n, p).wait()
        own_done[n].wait()
        return came[n].reshape(rows, ROWS)

    box = lax.dot_general(chosen[...], arrived(0), (((1,), (1,)), ((), ())), preferred_element_type=f32)
    outbox[...] = box.astype(bf16).reshape(BLOCKS, send_rows, rows)

    def box_copy(p):
        to = peer(p)
        return remote(outbox.at[to], rows_out.at[b], box_send.at[p], box_recv.at[p], to, k)

    for p in ORDER:
        box_copy(p).start()
    own_box = bring(outbox.at[b], rows_out.at[b])
    filter_out[...] = arrived(1).T.astype(f32)
    gate_out[...] = arrived(2).T
    for c in range(2):
        for way in range(2):
            far_copy(way, c).wait_send()
            for part in range(2):
                side_copy(way, part, c).wait_send()
    for p in ORDER:
        box_copy(p).wait()
    own_box.wait()


ORDER = sorted(range(1, BLOCKS), key=lambda p: -(min(p // 4, 4 - p // 4) + min(p % 4, 4 - p % 4)))
TABLES = 6


def shards(tokens_in, filters, gate, skip, out_grad, out_weight, owner, slot):
    channels = tokens_in.shape[1]
    send_rows = 2 * ROWS // BLOCKS
    half = ROWS // 2
    dma = pltpu.SemaphoreType.DMA
    vmem, hbm = pl.BlockSpec(memory_space=pltpu.VMEM), pl.BlockSpec(memory_space=pl.ANY)
    f32, bf16 = jnp.float32, jnp.bfloat16
    constants = tables()
    operands = (
        tokens_in, filters, gate, skip.reshape(1, channels), out_grad.reshape(2, 2, half // 2, ROWS), out_weight,
        owner, slot, *constants,
    )
    gate_grad, filter_grad, grad_rows = pl.pallas_call(
        kernel,
        out_shape=(
            jax.ShapeDtypeStruct((ROWS, channels), bf16),
            jax.ShapeDtypeStruct((ROWS, channels), f32),
            jax.ShapeDtypeStruct((BLOCKS, send_rows, channels), bf16),
        ),
        in_specs=[hbm] * len(operands),
        out_specs=(vmem, vmem, vmem),
        scratch_shapes=[
            pltpu.VMEM((3, ROWS, channels), bf16),
            pltpu.VMEM((1, channels), f32),
            pltpu.VMEM(owner.shape, jnp.int32),
            pltpu.VMEM(slot.shape, jnp.int32),
            *(pltpu.VMEM(c.shape, c.dtype) for c in constants),
            pltpu.VMEM((2, channels, 8 * ROWS), bf16),
            pltpu.VMEM((8, 2, half // 2, ROWS), bf16),
            pltpu.VMEM((2 * channels, half), f32),
            pltpu.VMEM((BLOCKS, 3, HELD, ROWS), bf16),
            pltpu.VMEM((BLOCKS, 3, HELD, ROWS), bf16),
            pltpu.VMEM((2, BLOCKS, HELD, half), bf16),
            pltpu.VMEM((2, BLOCKS, HELD, half), bf16),
            pltpu.VMEM((3, BLOCKS, HELD, ROWS), bf16),
            pltpu.VMEM((3, BLOCKS, HELD, ROWS), bf16),
            pltpu.VMEM((BLOCKS, send_rows, channels), bf16),
            pltpu.VMEM((BLOCKS * send_rows, ROWS), bf16),
            dma((24,)), dma((2,)), dma((2,)), dma((2, 2, 2)), dma((2, 2, 2)), dma((2, 2)), dma((2, 2)),
            dma((BLOCKS,)), dma((BLOCKS,)), dma((2, BLOCKS)), dma((2, BLOCKS)),
            dma((3, BLOCKS)), dma((3, BLOCKS)), dma((BLOCKS,)), dma((BLOCKS,)),
        ],
        compiler_params=pltpu.CompilerParams(
            collective_id=0, has_side_effects=True, vmem_limit_bytes=67043328
        ),
    )(*operands)
    grid = (BLOCKS, ROWS // BLOCKS, channels)
    return (gate_grad.reshape(grid), filter_grad.reshape(grid), grad_rows.reshape(BLOCKS * send_rows, channels))


def solution(mesh):
    return jax.shard_map(
        shards,
        mesh=mesh,
        in_specs=(
            P("bins", "chan"),
            P("bins", "chan"),
            P("bins", "chan"),
            P("chan"),
            P("bins", "chan"),
            P("chan", None),
            P(None, "bins"),
            P(None, "bins"),
        ),
        out_specs=(P(None, "bins", "chan"), P(None, "bins", "chan"), P("bins", "chan")),
        check_vma=False,
    )
```

```python
import math

import jax
import jax.numpy as jnp
import numpy as np
from jax import lax
from jax.experimental import pallas as pl
from jax.experimental.pallas import tpu as pltpu
from jax.sharding import PartitionSpec as P

BLOCKS = 16
HELD = 16
ROWS = 512
HALF = BLOCKS + 1
LENGTH = 2 * BLOCKS * ROWS


def tables():
    k1 = np.arange(HALF)
    i = np.arange(BLOCKS)
    ang = 2.0 * np.pi * np.outer(k1, i) / (2 * BLOCKS)
    eye = np.eye(HELD)
    ahead = np.concatenate([np.kron(np.cos(ang), eye), np.kron(-np.sin(ang), eye)], axis=0)
    weight = np.where((k1 == 0) | (k1 == BLOCKS), 1.0, 2.0)[None, :] / LENGTH
    back_re = np.kron(weight * np.cos(ang).T, eye)
    back_im = np.kron(-(weight * np.sin(ang).T)[:, 1:BLOCKS], eye)
    back = np.concatenate([back_re, back_im], axis=1)
    r = np.arange(ROWS)
    twist = 2.0 * np.pi * np.outer(k1, r) / LENGTH
    inner = 2.0 * np.pi * (np.outer(r, r) % ROWS) / ROWS
    return (
        jnp.asarray(ahead, jnp.bfloat16),
        jnp.asarray(back, jnp.bfloat16),
        jnp.asarray(np.cos(twist)[:, None, :], jnp.float32),
        jnp.asarray(np.sin(twist)[:, None, :], jnp.float32),
        jnp.asarray(np.cos(inner), jnp.bfloat16),
        jnp.asarray(np.sin(inner), jnp.bfloat16),
    )


def mm(a, b):
    return jnp.dot(a, b, preferred_element_type=jnp.float32)


def stage_rows(value):
    return value.reshape(HALF, HELD, ROWS)


def flat(value):
    return value.reshape(HALF * HELD, ROWS)


def forward(value, ahead, tw_cos, tw_sin, in_cos, in_sin):
    part = mm(ahead, value)
    n = HALF * HELD
    re, im = stage_rows(part[:n]), stage_rows(part[n:])
    z_re = flat(re * tw_cos + im * tw_sin)
    z_im = flat(im * tw_cos - re * tw_sin)
    z = jnp.concatenate([z_re, z_im], axis=0).astype(jnp.bfloat16)
    by_cos, by_sin = mm(z, in_cos), mm(z, in_sin)
    return by_cos[:n] + by_sin[n:], by_cos[n:] - by_sin[:n]


def inverse(s_re, s_im, back, tw_cos, tw_sin, in_cos, in_sin):
    n = HALF * HELD
    q = jnp.concatenate([s_re, s_im], axis=0).astype(jnp.bfloat16)
    by_cos, by_sin = mm(q, in_cos), mm(q, in_sin)
    re, im = stage_rows(by_cos[:n] - by_sin[n:]), stage_rows(by_cos[n:] + by_sin[:n])
    t_re = flat(re * tw_cos - im * tw_sin)
    t_im = flat(im * tw_cos + re * tw_sin)[HELD : BLOCKS * HELD]
    t = jnp.concatenate([t_re, t_im], axis=0).astype(jnp.bfloat16)
    return mm(back, t)


def to_columns(value):
    group = lax.broadcasted_iota(jnp.int32, (HELD, 128), 1) // 32
    out = [[None] * 4 for _ in range(BLOCKS)]
    for i_hi in range(4):
        for j_hi in range(4):
            tiles = [
                value[(4 * i_hi + i_lo) * HELD : (4 * i_hi + i_lo + 1) * HELD, 128 * j_hi : 128 * (j_hi + 1)]
                for i_lo in range(4)
            ]
            for j_lo in range(4):
                acc = None
                for i_lo in range(4):
                    shift = (32 * (i_lo - j_lo)) % 128
                    turned = pltpu.roll(tiles[i_lo], shift, 1) if shift else tiles[i_lo]
                    acc = turned if acc is None else jnp.where(group == i_lo, turned, acc)
                out[4 * j_hi + j_lo][i_hi] = acc
    return jnp.concatenate([jnp.concatenate(row, axis=1) for row in out], axis=0)


def remote(src, dst, send, recv, bins, chan):
    return pltpu.make_async_remote_copy(
        src_ref=src,
        dst_ref=dst,
        send_sem=send,
        recv_sem=recv,
        device_id=(bins, chan),
        device_id_type=pl.DeviceIdType.MESH,
    )


def kernel(
    x_hbm, h_hbm, gate_hbm, skip_hbm, og_hbm, w_hbm, owner_hbm, slot_hbm, *rest
):
    tables_hbm, rest = rest[:TABLES], rest[TABLES:]
    gate_out, filter_out, rows_out = rest[:3]
    (
        raw, skip_ref, owner_ref, slot_ref, *rest
    ) = rest[3:]
    tables_ref, rest = rest[:TABLES], rest[TABLES:]
    (
        w_all, og_all, acc, early_src, early, g_src, g_came, done, came, outbox, chosen, turned,
        local_sem, w_sem, mate_sem, side_send, side_recv, far_send, far_recv,
        early_send, early_recv, g_send, g_recv, done_send, done_recv, box_send, box_recv,
    ) = rest
    f32, bf16 = jnp.float32, jnp.bfloat16
    rows = BLOCKS * HELD
    send_rows = 2 * ROWS // BLOCKS
    b = lax.axis_index("bins")
    k = lax.axis_index("chan")
    b_y, b_z = lax.div(b, 4), lax.rem(b, 4)
    chip, core = lax.div(k, 2), lax.rem(k, 2)
    right, left, across = lax.rem(chip + 1, 4), lax.rem(chip + 3, 4), lax.rem(chip + 2, 4)
    mate = 2 * chip + 1 - core

    def peer(p):
        return 4 * lax.rem(b_y + p // 4, 4) + lax.rem(b_z + p % 4, 4)

    local = []

    def bring(src, dst):
        copy = pltpu.make_async_copy(src, dst, local_sem.at[len(local)])
        copy.start()
        local.append(copy)
        return copy

    own_raw = [bring(ref, raw.at[n]) for n, ref in enumerate((x_hbm, h_hbm, gate_hbm))]
    own_og = bring(og_hbm.at[core], og_all.at[k])
    own_w = bring(w_hbm, w_all.at[core])
    own_small = [bring(*pair) for pair in ((skip_hbm, skip_ref), (owner_hbm, owner_ref), (slot_hbm, slot_ref))]
    own_tables = [bring(*pair) for pair in zip(tables_hbm, tables_ref)]

    barrier = pltpu.get_barrier_semaphore()

    def greet(bins, chan):
        pl.semaphore_signal(barrier, inc=1, device_id=(bins, chan), device_id_type=pl.DeviceIdType.MESH)

    for p in ORDER:
        greet(peer(p), k)
        greet(peer(p), mate)
    greet(b, mate)
    for side in (right, left):
        for c in range(2):
            greet(b, 2 * side + c)
    pl.semaphore_wait(barrier, 2 * BLOCKS - 1 + 4)

    def side_copy(way, part, c):
        to = (right, left)[way]
        return remote(
            og_hbm.at[c, part], og_all.at[k, part],
            side_send.at[way, part, c], side_recv.at[way, part, core], b, 2 * to + c,
        )

    for turn in range(2):
        for c in range(2):
            side_copy(0, turn, c).start()
            side_copy(1, 1 - turn, c).start()
    mate_og = remote(og_hbm.at[1 - core], og_all.at[k], mate_sem.at[0], mate_sem.at[1], b, mate)
    mate_og.start()
    mate_w = remote(w_hbm, w_all.at[core], w_sem.at[0], w_sem.at[1], b, mate)
    mate_w.start()

    for n in range(3):
        own_raw[n].wait()
        early_src[:, n] = raw[n].T.reshape(BLOCKS, HELD, ROWS)

    def early_copy(p):
        to = peer(p)
        return remote(early_src.at[to], early.at[b], early_send.at[p], early_recv.at[p], to, k)

    for p in ORDER:
        early_copy(p).start()
    own_early = bring(early_src.at[b], early.at[b])

    def side_arrived(way, part, c):
        src = 2 * (left, right)[way] + c
        return remote(
            og_hbm.at[c, part], og_all.at[src, part],
            side_send.at[way, part, c], side_recv.at[way, part, c], b, mate,
        )

    def far_copy(way, c):
        src = 2 * (left, right)[way] + c
        to = (right, left)[way]
        return remote(
            og_all.at[src, way], og_all.at[src, way],
            far_send.at[way, c], far_recv.at[way, c], b, 2 * to + core,
        )

    for c in range(2):
        for way in range(2):
            side_arrived(way, way, c).wait_recv()
            far_copy(way, c).start()

    def gather(source, first=False):
        columns = pl.ds(pl.multiple_of(source * ROWS, ROWS), ROWS)
        weights = w_all[:, :, columns].reshape(2 * rows, ROWS)
        term = lax.dot_general(
            weights, og_all[source].reshape(ROWS // 2, ROWS), (((1,), (1,)), ((), ())), preferred_element_type=f32
        )
        acc[...] = term if first else acc[...] + term

    own_w.wait()
    own_og.wait()
    mate_w.wait()
    mate_og.wait()
    gather(k, True)
    gather(mate)
    for c in range(2):
        for way in range(2):
            side_arrived(way, 1 - way, c).wait_recv()
            gather(2 * (left, right)[way] + c)
    for copy in own_small + own_tables:
        copy.wait()
    for p in ORDER:
        early_copy(p).wait()
    own_early.wait()
    ahead, back, tw_cos, tw_sin, in_cos, in_sin = (ref[...] for ref in tables_ref)
    forward_tables = (ahead, tw_cos, tw_sin, in_cos, in_sin)
    inverse_tables = (back, tw_cos, tw_sin, in_cos, in_sin)
    x = early[:, 0].reshape(rows, ROWS)
    x_re, x_im = forward(x, *forward_tables)
    h_re, h_im = forward(early[:, 1].reshape(rows, ROWS), *forward_tables)
    conv = inverse(x_re * h_re - x_im * h_im, x_re * h_im + x_im * h_re, *inverse_tables)
    lanes = lax.broadcasted_iota(jnp.int32, (rows, rows), 1)
    held = lax.rem(lax.broadcasted_iota(jnp.int32, (rows, rows), 0), HELD)
    skip = jnp.sum(jnp.where(lanes == held + HELD * b, skip_ref[...], 0.0), axis=1, keepdims=True)
    with_skip = conv + skip * x.astype(f32)
    target = owner_ref[...] * send_rows + slot_ref[...] - b * send_rows
    target = jnp.concatenate([target[i : i + 1] for i in range(BLOCKS)], axis=1)
    places = lax.broadcasted_iota(jnp.int32, (BLOCKS * send_rows, ROWS), 0)
    chosen[...] = jnp.where(places == target, 1.0, 0.0).astype(bf16)

    for c in range(2):
        for way in range(2):
            far_copy(way, c).wait_recv()
        gather(2 * across + c)
    g_src[...] = acc[...].astype(bf16).reshape(2, BLOCKS, HELD, ROWS // 2)

    def g_copy(p, c):
        to = peer(p)
        hand = lax.rem(core + c, 2)
        return remote(
            g_src.at[hand, to], g_came.at[core, b], g_send.at[c, p], g_recv.at[c, p], to, 2 * chip + hand
        )

    for p in ORDER:
        g_copy(p, 0).start()
        g_copy(p, 1).start()
    g_copy(0, 1).start()
    own_g = bring(g_src.at[core, b], g_came.at[core, b])

    for p in ORDER:
        g_copy(p, 0).wait()
        g_copy(p, 1).wait()
    g_copy(0, 1).wait()
    own_g.wait()
    g = jnp.concatenate([g_came[0].reshape(rows, ROWS // 2), g_came[1].reshape(rows, ROWS // 2)], axis=1)
    g = g.astype(f32)
    def done_copy(n, p):
        to = peer(p)
        return remote(done.at[n, to], came.at[n, b], done_send.at[n, p], done_recv.at[n, p], to, k)

    own_done = {}

    def put(n, value):
        done[n] = to_columns(value).astype(bf16).reshape(BLOCKS, HELD, ROWS)
        for p in ORDER:
            done_copy(n, p).start()
        own_done[n] = bring(done.at[n, b], came.at[n, b])

    put(2, g * with_skip)
    dy = (g * early[:, 2].reshape(rows, ROWS).astype(f32)).astype(bf16)
    y_re, y_im = forward(dy, *forward_tables)

    grad = inverse(h_re * y_re + h_im * y_im, h_re * y_im - h_im * y_re, *inverse_tables)
    put(0, grad + skip * dy.astype(f32))
    lag = inverse(y_re * x_re + y_im * x_im, y_im * x_re - y_re * x_im, *inverse_tables)
    put(1, lag * (1.0 / math.sqrt(BLOCKS * ROWS)))

    def arrived(n):
        for p in ORDER:
            done_copy(n, p).wait()
        own_done[n].wait()
        return came[n].reshape(rows, ROWS)

    box = lax.dot_general(chosen[...], arrived(0), (((1,), (1,)), ((), ())), preferred_element_type=f32)
    outbox[...] = box.astype(bf16).reshape(BLOCKS, send_rows, rows)

    def box_copy(p):
        to = peer(p)
        return remote(outbox.at[to], rows_out.at[b], box_send.at[p], box_recv.at[p], to, k)

    for p in ORDER:
        box_copy(p).start()
    own_box = bring(outbox.at[b], rows_out.at[b])
    results = []
    for n, out in ((2, gate_out), (1, filter_out)):
        turned[n - 1] = arrived(n).T
        results.append(bring(turned.at[n - 1], out))
    for c in range(2):
        for way in range(2):
            far_copy(way, c).wait_send()
            for part in range(2):
                side_copy(way, part, c).wait_send()
    for p in ORDER:
        box_copy(p).wait()
    own_box.wait()
    for copy in results:
        copy.wait()


ORDER = sorted(range(1, BLOCKS), key=lambda p: -(min(p // 4, 4 - p // 4) + min(p % 4, 4 - p % 4)))
TABLES = 6


def finish_kernel(gate_hbm, filter_hbm, rows_hbm, gate_out, filter_out, rows_out, gate, taps, wide, moved, sem):
    pieces = 2
    half, part = ROWS // pieces, BLOCKS // pieces
    steps = []
    for n in range(pieces):
        some, blocks = pl.ds(n * half, half), pl.ds(n * part, part)
        steps += [
            (filter_hbm.at[some], taps.at[some], wide.at[some], filter_out.at[some], some),
            (rows_hbm.at[blocks], moved.at[blocks], moved.at[blocks], rows_out.at[blocks], None),
            (gate_hbm.at[some], gate.at[some], gate.at[some], gate_out.at[some], None),
        ]
    reads = [pltpu.make_async_copy(src, held, sem.at[0, n]) for n, (src, held, _, _, _) in enumerate(steps)]
    writes = [pltpu.make_async_copy(held, dst, sem.at[1, n]) for n, (_, _, held, dst, _) in enumerate(steps)]
    for read in reads:
        read.start()
    for read, write, step in zip(reads, writes, steps):
        read.wait()
        if step[4] is not None:
            wide[step[4]] = taps[step[4]].astype(jnp.float32)
        write.start()
    for write in writes:
        write.wait()


def finish(gate_grad, filter_grad, grad_rows):
    f32 = jnp.float32
    return pl.pallas_call(
        finish_kernel,
        out_shape=(
            jax.ShapeDtypeStruct(gate_grad.shape, gate_grad.dtype),
            jax.ShapeDtypeStruct(filter_grad.shape, f32),
            jax.ShapeDtypeStruct(grad_rows.shape, grad_rows.dtype),
        ),
        in_specs=[pl.BlockSpec(memory_space=pl.ANY)] * 3,
        out_specs=(pl.BlockSpec(memory_space=pl.ANY),) * 3,
        scratch_shapes=[
            pltpu.VMEM(gate_grad.shape, gate_grad.dtype),
            pltpu.VMEM(filter_grad.shape, filter_grad.dtype),
            pltpu.VMEM(filter_grad.shape, f32),
            pltpu.VMEM(grad_rows.shape, grad_rows.dtype),
            pltpu.SemaphoreType.DMA((2, 6)),
        ],
        compiler_params=pltpu.CompilerParams(vmem_limit_bytes=67043328),
    )(gate_grad, filter_grad, grad_rows)


def shards(tokens_in, filters, gate, skip, out_grad, out_weight, owner, slot):
    channels = tokens_in.shape[1]
    send_rows = 2 * ROWS // BLOCKS
    half = ROWS // 2
    dma = pltpu.SemaphoreType.DMA
    hbm = pl.BlockSpec(memory_space=pl.ANY)
    f32, bf16 = jnp.float32, jnp.bfloat16
    constants = tables()
    operands = (
        tokens_in, filters, gate, skip.reshape(1, channels), out_grad.reshape(2, 2, half // 2, ROWS), out_weight,
        owner, slot, *constants,
    )
    gate_grad, filter_grad, grad_rows = pl.pallas_call(
        kernel,
        out_shape=(
            jax.ShapeDtypeStruct((ROWS, channels), bf16),
            jax.ShapeDtypeStruct((ROWS, channels), bf16),
            jax.ShapeDtypeStruct((BLOCKS, send_rows, channels), bf16),
        ),
        in_specs=[hbm] * len(operands),
        out_specs=(hbm, hbm, hbm),
        scratch_shapes=[
            pltpu.VMEM((3, ROWS, channels), bf16),
            pltpu.VMEM((1, channels), f32),
            pltpu.VMEM(owner.shape, jnp.int32),
            pltpu.VMEM(slot.shape, jnp.int32),
            *(pltpu.VMEM(c.shape, c.dtype) for c in constants),
            pltpu.VMEM((2, channels, 8 * ROWS), bf16),
            pltpu.VMEM((8, 2, half // 2, ROWS), bf16),
            pltpu.VMEM((2 * channels, half), f32),
            pltpu.VMEM((BLOCKS, 3, HELD, ROWS), bf16),
            pltpu.VMEM((BLOCKS, 3, HELD, ROWS), bf16),
            pltpu.VMEM((2, BLOCKS, HELD, half), bf16),
            pltpu.VMEM((2, BLOCKS, HELD, half), bf16),
            pltpu.VMEM((3, BLOCKS, HELD, ROWS), bf16),
            pltpu.VMEM((3, BLOCKS, HELD, ROWS), bf16),
            pltpu.VMEM((BLOCKS, send_rows, channels), bf16),
            pltpu.VMEM((BLOCKS * send_rows, ROWS), bf16),
            pltpu.VMEM((2, ROWS, channels), bf16),
            dma((24,)), dma((2,)), dma((2,)), dma((2, 2, 2)), dma((2, 2, 2)), dma((2, 2)), dma((2, 2)),
            dma((BLOCKS,)), dma((BLOCKS,)), dma((2, BLOCKS)), dma((2, BLOCKS)),
            dma((3, BLOCKS)), dma((3, BLOCKS)), dma((BLOCKS,)), dma((BLOCKS,)),
        ],
        compiler_params=pltpu.CompilerParams(
            collective_id=0, has_side_effects=True, vmem_limit_bytes=67043328
        ),
    )(*operands)
    gate_grad, filter_grad, grad_rows = finish(gate_grad, filter_grad, grad_rows)
    grid = (BLOCKS, ROWS // BLOCKS, channels)
    return (gate_grad.reshape(grid), filter_grad.reshape(grid), grad_rows.reshape(BLOCKS * send_rows, channels))


def solution(mesh):
    return jax.shard_map(
        shards,
        mesh=mesh,
        in_specs=(
            P("bins", "chan"),
            P("bins", "chan"),
            P("bins", "chan"),
            P("chan"),
            P("bins", "chan"),
            P("chan", None),
            P(None, "bins"),
            P(None, "bins"),
        ),
        out_specs=(P(None, "bins", "chan"), P(None, "bins", "chan"), P("bins", "chan")),
        check_vma=False,
    )
```

```python
import math

import jax
import jax.numpy as jnp
import numpy as np
from jax import lax
from jax.experimental import pallas as pl
from jax.experimental.pallas import tpu as pltpu
from jax.sharding import PartitionSpec as P

BLOCKS = 16
HELD = 16
ROWS = 512
HALF = BLOCKS + 1
LENGTH = 2 * BLOCKS * ROWS


def tables():
    k1 = np.arange(HALF)
    i = np.arange(BLOCKS)
    ang = 2.0 * np.pi * np.outer(k1, i) / (2 * BLOCKS)
    eye = np.eye(HELD)
    ahead = np.concatenate([np.kron(np.cos(ang), eye), np.kron(-np.sin(ang), eye)], axis=0)
    weight = np.where((k1 == 0) | (k1 == BLOCKS), 1.0, 2.0)[None, :] / LENGTH
    back_re = np.kron(weight * np.cos(ang).T, eye)
    back_im = np.kron(-(weight * np.sin(ang).T)[:, 1:BLOCKS], eye)
    back = np.concatenate([back_re, back_im], axis=1)
    r = np.arange(ROWS)
    twist = 2.0 * np.pi * np.outer(k1, r) / LENGTH
    inner = 2.0 * np.pi * (np.outer(r, r) % ROWS) / ROWS
    return (
        jnp.asarray(ahead, jnp.bfloat16),
        jnp.asarray(back, jnp.bfloat16),
        jnp.asarray(np.cos(twist)[:, None, :], jnp.float32),
        jnp.asarray(np.sin(twist)[:, None, :], jnp.float32),
        jnp.asarray(np.cos(inner), jnp.bfloat16),
        jnp.asarray(np.sin(inner), jnp.bfloat16),
    )


def mm(a, b):
    return jnp.dot(a, b, preferred_element_type=jnp.float32)


def stage_rows(value):
    return value.reshape(HALF, HELD, ROWS)


def flat(value):
    return value.reshape(HALF * HELD, ROWS)


def forward(value, ahead, tw_cos, tw_sin, in_cos, in_sin):
    part = mm(ahead, value)
    n = HALF * HELD
    re, im = stage_rows(part[:n]), stage_rows(part[n:])
    z_re = flat(re * tw_cos + im * tw_sin)
    z_im = flat(im * tw_cos - re * tw_sin)
    z = jnp.concatenate([z_re, z_im], axis=0).astype(jnp.bfloat16)
    by_cos, by_sin = mm(z, in_cos), mm(z, in_sin)
    return by_cos[:n] + by_sin[n:], by_cos[n:] - by_sin[:n]


def inverse(s_re, s_im, back, tw_cos, tw_sin, in_cos, in_sin):
    n = HALF * HELD
    q = jnp.concatenate([s_re, s_im], axis=0).astype(jnp.bfloat16)
    by_cos, by_sin = mm(q, in_cos), mm(q, in_sin)
    re, im = stage_rows(by_cos[:n] - by_sin[n:]), stage_rows(by_cos[n:] + by_sin[:n])
    t_re = flat(re * tw_cos - im * tw_sin)
    t_im = flat(im * tw_cos + re * tw_sin)[HELD : BLOCKS * HELD]
    t = jnp.concatenate([t_re, t_im], axis=0).astype(jnp.bfloat16)
    return mm(back, t)


def to_columns(value):
    group = lax.broadcasted_iota(jnp.int32, (HELD, 128), 1) // 32
    out = [[None] * 4 for _ in range(BLOCKS)]
    for i_hi in range(4):
        for j_hi in range(4):
            tiles = [
                value[(4 * i_hi + i_lo) * HELD : (4 * i_hi + i_lo + 1) * HELD, 128 * j_hi : 128 * (j_hi + 1)]
                for i_lo in range(4)
            ]
            for j_lo in range(4):
                acc = None
                for i_lo in range(4):
                    shift = (32 * (i_lo - j_lo)) % 128
                    turned = pltpu.roll(tiles[i_lo], shift, 1) if shift else tiles[i_lo]
                    acc = turned if acc is None else jnp.where(group == i_lo, turned, acc)
                out[4 * j_hi + j_lo][i_hi] = acc
    return jnp.concatenate([jnp.concatenate(row, axis=1) for row in out], axis=0)


def remote(src, dst, send, recv, bins, chan):
    return pltpu.make_async_remote_copy(
        src_ref=src,
        dst_ref=dst,
        send_sem=send,
        recv_sem=recv,
        device_id=(bins, chan),
        device_id_type=pl.DeviceIdType.MESH,
    )


def kernel(
    x_hbm, h_hbm, gate_hbm, skip_hbm, og_hbm, w_hbm, owner_hbm, slot_hbm, *rest
):
    tables_hbm, rest = rest[:TABLES], rest[TABLES:]
    gate_out, filter_out, rows_out = rest[:3]
    (
        raw, skip_ref, owner_ref, slot_ref, *rest
    ) = rest[3:]
    tables_ref, rest = rest[:TABLES], rest[TABLES:]
    (
        w_all, og_all, acc, early_src, early, g_src, g_came, done, came, outbox, map_src, maps, turned,
        local_sem, w_sem, mate_sem, side_send, side_recv, far_send, far_recv,
        early_send, early_recv, g_send, g_recv, done_send, done_recv, box_send, box_recv, map_send, map_recv,
    ) = rest
    f32, bf16 = jnp.float32, jnp.bfloat16
    rows = BLOCKS * HELD
    send_rows = 2 * ROWS // BLOCKS
    b = lax.axis_index("bins")
    k = lax.axis_index("chan")
    b_y, b_z = lax.div(b, 4), lax.rem(b, 4)
    chip, core = lax.div(k, 2), lax.rem(k, 2)
    right, left, across = lax.rem(chip + 1, 4), lax.rem(chip + 3, 4), lax.rem(chip + 2, 4)
    mate = 2 * chip + 1 - core

    def peer(p):
        return 4 * lax.rem(b_y + p // 4, 4) + lax.rem(b_z + p % 4, 4)

    local = []

    def bring(src, dst):
        copy = pltpu.make_async_copy(src, dst, local_sem.at[len(local)])
        copy.start()
        local.append(copy)
        return copy

    own_raw = [bring(ref, raw.at[n]) for n, ref in enumerate((x_hbm, h_hbm, gate_hbm))]
    own_og = bring(og_hbm.at[core], og_all.at[k])
    own_w = bring(w_hbm, w_all.at[core])
    own_small = [bring(*pair) for pair in ((skip_hbm, skip_ref), (owner_hbm, owner_ref), (slot_hbm, slot_ref))]
    own_tables = [bring(*pair) for pair in zip(tables_hbm, tables_ref)]

    barrier = pltpu.get_barrier_semaphore()

    def greet(bins, chan):
        pl.semaphore_signal(barrier, inc=1, device_id=(bins, chan), device_id_type=pl.DeviceIdType.MESH)

    for p in ORDER:
        greet(peer(p), k)
        greet(peer(p), mate)
    greet(b, mate)
    for side in (right, left):
        for c in range(2):
            greet(b, 2 * side + c)
    pl.semaphore_wait(barrier, 2 * BLOCKS - 1 + 4)

    def side_copy(way, part, c):
        to = (right, left)[way]
        return remote(
            og_hbm.at[c, part], og_all.at[k, part],
            side_send.at[way, part, c], side_recv.at[way, part, core], b, 2 * to + c,
        )

    for turn in range(2):
        for c in range(2):
            side_copy(0, turn, c).start()
            side_copy(1, 1 - turn, c).start()
    mate_og = remote(og_hbm.at[1 - core], og_all.at[k], mate_sem.at[0], mate_sem.at[1], b, mate)
    mate_og.start()
    mate_w = remote(w_hbm, w_all.at[core], w_sem.at[0], w_sem.at[1], b, mate)
    mate_w.start()

    for n in range(3):
        own_raw[n].wait()
        early_src[:, n] = raw[n].T.reshape(BLOCKS, HELD, ROWS)

    def early_copy(p):
        to = peer(p)
        return remote(early_src.at[to], early.at[b], early_send.at[p], early_recv.at[p], to, k)

    for p in ORDER:
        early_copy(p).start()
    own_early = bring(early_src.at[b], early.at[b])

    def side_arrived(way, part, c):
        src = 2 * (left, right)[way] + c
        return remote(
            og_hbm.at[c, part], og_all.at[src, part],
            side_send.at[way, part, c], side_recv.at[way, part, c], b, mate,
        )

    def far_copy(way, c):
        src = 2 * (left, right)[way] + c
        to = (right, left)[way]
        return remote(
            og_all.at[src, way], og_all.at[src, way],
            far_send.at[way, c], far_recv.at[way, c], b, 2 * to + core,
        )

    for c in range(2):
        for way in range(2):
            side_arrived(way, way, c).wait_recv()
            far_copy(way, c).start()

    def gather(source, first=False):
        columns = pl.ds(pl.multiple_of(source * ROWS, ROWS), ROWS)
        weights = w_all[:, :, columns].reshape(2 * rows, ROWS)
        term = lax.dot_general(
            weights, og_all[source].reshape(ROWS // 2, ROWS), (((1,), (1,)), ((), ())), preferred_element_type=f32
        )
        acc[...] = term if first else acc[...] + term

    own_w.wait()
    own_og.wait()
    mate_w.wait()
    mate_og.wait()
    gather(k, True)
    gather(mate)
    for c in range(2):
        for way in range(2):
            side_arrived(way, 1 - way, c).wait_recv()
            gather(2 * (left, right)[way] + c)
    for copy in own_small + own_tables:
        copy.wait()
    for p in ORDER:
        early_copy(p).wait()
    own_early.wait()
    ahead, back, tw_cos, tw_sin, in_cos, in_sin = (ref[...] for ref in tables_ref)
    forward_tables = (ahead, tw_cos, tw_sin, in_cos, in_sin)
    inverse_tables = (back, tw_cos, tw_sin, in_cos, in_sin)
    x = early[:, 0].reshape(rows, ROWS)
    x_re, x_im = forward(x, *forward_tables)
    h_re, h_im = forward(early[:, 1].reshape(rows, ROWS), *forward_tables)
    conv = inverse(x_re * h_re - x_im * h_im, x_re * h_im + x_im * h_re, *inverse_tables)
    lanes = lax.broadcasted_iota(jnp.int32, (rows, rows), 1)
    held = lax.rem(lax.broadcasted_iota(jnp.int32, (rows, rows), 0), HELD)
    skip = jnp.sum(jnp.where(lanes == held + HELD * b, skip_ref[...], 0.0), axis=1, keepdims=True)
    with_skip = conv + skip * x.astype(f32)
    odd = lax.rem(b, 2)
    target = (owner_ref[...] + odd * (1 - 2 * lax.rem(owner_ref[...], 2))) * send_rows + slot_ref[...] - b * send_rows
    target = jnp.concatenate([target[i : i + 1] for i in range(BLOCKS)], axis=1)
    places = lax.broadcasted_iota(jnp.int32, (BLOCKS * send_rows, ROWS), 0)
    chosen = jnp.where(places == target, 1.0, 0.0).astype(bf16)
    token = lax.broadcasted_iota(jnp.int32, (16, ROWS), 1)
    which = lax.broadcasted_iota(jnp.int32, (16, ROWS), 0)
    digits = jnp.where(which == 0, lax.rem(token, 128), jnp.where(which == 1, lax.div(token, 128) + 1, 0))
    digits = lax.dot_general(
        digits.astype(f32).astype(bf16), chosen, (((1,), (1,)), ((), ())), preferred_element_type=f32
    )
    origin = (digits[0:1] + 128.0 * digits[1:2]).astype(jnp.int32)
    map_src[...] = jnp.concatenate([origin[:, 128 * n : 128 * (n + 1)] for n in range(8)], axis=0)

    def map_copy(p):
        to = peer(p)
        return remote(map_src, maps.at[b], map_send.at[p], map_recv.at[p], to, k)

    for p in ORDER:
        map_copy(p).start()
    own_map = bring(map_src, maps.at[b])
    for c in range(2):
        for way in range(2):
            far_copy(way, c).wait_recv()
        gather(2 * across + c)
    g_src[...] = acc[...].astype(bf16).reshape(2, BLOCKS, HELD, ROWS // 2)

    def g_copy(p, c):
        to = peer(p)
        hand = lax.rem(core + c, 2)
        return remote(
            g_src.at[hand, to], g_came.at[core, b], g_send.at[c, p], g_recv.at[c, p], to, 2 * chip + hand
        )

    for p in ORDER:
        g_copy(p, 0).start()
        g_copy(p, 1).start()
    g_copy(0, 1).start()
    own_g = bring(g_src.at[core, b], g_came.at[core, b])

    for p in ORDER:
        g_copy(p, 0).wait()
        g_copy(p, 1).wait()
    g_copy(0, 1).wait()
    own_g.wait()
    g = jnp.concatenate([g_came[0].reshape(rows, ROWS // 2), g_came[1].reshape(rows, ROWS // 2)], axis=1)
    g = g.astype(f32)
    def done_copy(n, p):
        to = peer(p)
        return remote(done.at[n, to], came.at[n, b], done_send.at[n, p], done_recv.at[n, p], to, k)

    own_done = {}

    def put(n, value):
        done[n] = to_columns(value).astype(bf16).reshape(BLOCKS, HELD, ROWS)
        for p in ORDER:
            done_copy(n, p).start()
        own_done[n] = bring(done.at[n, b], came.at[n, b])

    put(0, g * with_skip)
    dy = (g * early[:, 2].reshape(rows, ROWS).astype(f32)).astype(bf16)
    y_re, y_im = forward(dy, *forward_tables)

    lag = inverse(y_re * x_re + y_im * x_im, y_im * x_re - y_re * x_im, *inverse_tables)
    put(1, lag * (1.0 / math.sqrt(BLOCKS * ROWS)))
    grad = inverse(h_re * y_re + h_im * y_im, h_re * y_im - h_im * y_re, *inverse_tables)
    columns = to_columns(grad + skip * dy.astype(f32))
    for p in ORDER:
        map_copy(p).wait()
    own_map.wait()
    low_half = lax.broadcasted_iota(jnp.int32, (HELD, 128), 1) < 64
    for m in range(BLOCKS // 2):
        picked = []
        for j in (2 * m, 2 * m + 1):
            held = columns[j * HELD : (j + 1) * HELD]
            lane, tile = lax.rem(maps[j], 128), lax.div(maps[j], 128)
            tiles = []
            for n in range(8):
                at = jnp.broadcast_to(lane[n : n + 1], (HELD, 128))
                which = jnp.broadcast_to(tile[n : n + 1], (HELD, 128))
                value = jnp.zeros((HELD, 128), f32)
                for t in range(4):
                    found = jnp.take_along_axis(held[:, 128 * t : 128 * (t + 1)], at, axis=1)
                    value = jnp.where(which == t + 1, found, value)
                tiles.append(value)
            picked.append(tiles)
        for n in range(8):
            even, other = picked[0][n], picked[1][n]
            outbox[2 * n, :, 128 * m : 128 * (m + 1)] = jnp.where(low_half, even, other).astype(bf16)
            outbox[2 * n + 1, :, 128 * m : 128 * (m + 1)] = jnp.where(low_half, other, even).astype(bf16)

    def box_copy(p):
        to = peer(p)
        return remote(outbox.at[to], rows_out.at[b], box_send.at[p], box_recv.at[p], to, k)

    for p in ORDER:
        box_copy(p).start()
    own_box = bring(outbox.at[b], rows_out.at[b])

    def arrived(n):
        for p in ORDER:
            done_copy(n, p).wait()
        own_done[n].wait()
        return came[n].reshape(rows, ROWS)

    results = []
    for n, out in enumerate((gate_out, filter_out)):
        turned[n] = arrived(n).T
        results.append(bring(turned.at[n], out))
    for c in range(2):
        for way in range(2):
            far_copy(way, c).wait_send()
            for part in range(2):
                side_copy(way, part, c).wait_send()
    for p in ORDER:
        box_copy(p).wait()
    own_box.wait()
    for copy in results:
        copy.wait()


ORDER = sorted(range(1, BLOCKS), key=lambda p: -(min(p // 4, 4 - p // 4) + min(p % 4, 4 - p % 4)))
TABLES = 6


def finish_kernel(gate_hbm, filter_hbm, rows_hbm, gate_out, filter_out, rows_out, gate, taps, wide, moved, ranked, sem):
    odd = lax.rem(lax.axis_index("bins"), 2)
    span = 256
    parts = rows_hbm.shape[1] // span
    reads, writes = [], []

    def read(src, held):
        reads.append(pltpu.make_async_copy(src, held, sem.at[len(reads)]))
        reads[-1].start()
        return reads[-1]

    def write(held, dst):
        writes.append(pltpu.make_async_copy(held, dst, sem.at[8 + len(writes)]))
        writes[-1].start()

    taps_in = read(filter_hbm, taps)
    rows_in = [read(rows_hbm.at[:, pl.ds(n * span, span)], moved.at[n]) for n in range(parts)]
    gate_in = read(gate_hbm, gate)
    taps_in.wait()
    wide[...] = taps[...].astype(jnp.float32)
    write(wide, filter_out)
    for n in range(parts):
        rows_in[n].wait()
        ranked[n] = moved[n].T.reshape(span // 64, 64, 256)
        for q in range(span // 64):
            group = n * (span // 64) + q
            group = group + odd * (1 - 2 * (q % 2))
            write(ranked.at[n, q], rows_out.at[pl.ds(group * 64, 64)])
    gate_in.wait()
    write(gate, gate_out)
    for copy in writes:
        copy.wait()


def finish(gate_grad, filter_grad, grad_rows):
    f32 = jnp.float32
    channels, count = grad_rows.shape
    return pl.pallas_call(
        finish_kernel,
        out_shape=(
            jax.ShapeDtypeStruct(gate_grad.shape, gate_grad.dtype),
            jax.ShapeDtypeStruct(filter_grad.shape, f32),
            jax.ShapeDtypeStruct((count, channels), grad_rows.dtype),
        ),
        in_specs=[pl.BlockSpec(memory_space=pl.ANY)] * 3,
        out_specs=(pl.BlockSpec(memory_space=pl.ANY),) * 3,
        scratch_shapes=[
            pltpu.VMEM(gate_grad.shape, gate_grad.dtype),
            pltpu.VMEM(filter_grad.shape, filter_grad.dtype),
            pltpu.VMEM(filter_grad.shape, f32),
            pltpu.VMEM((count // 256, channels, 256), grad_rows.dtype),
            pltpu.VMEM((count // 256, 4, 64, channels), grad_rows.dtype),
            pltpu.SemaphoreType.DMA((32,)),
        ],
        compiler_params=pltpu.CompilerParams(vmem_limit_bytes=67043328),
    )(gate_grad, filter_grad, grad_rows)


def shards(tokens_in, filters, gate, skip, out_grad, out_weight, owner, slot):
    channels = tokens_in.shape[1]
    send_rows = 2 * ROWS // BLOCKS
    half = ROWS // 2
    dma = pltpu.SemaphoreType.DMA
    hbm = pl.BlockSpec(memory_space=pl.ANY)
    f32, bf16 = jnp.float32, jnp.bfloat16
    constants = tables()
    operands = (
        tokens_in, filters, gate, skip.reshape(1, channels), out_grad.reshape(2, 2, half // 2, ROWS), out_weight,
        owner, slot, *constants,
    )
    gate_grad, filter_grad, grad_rows = pl.pallas_call(
        kernel,
        out_shape=(
            jax.ShapeDtypeStruct((ROWS, channels), bf16),
            jax.ShapeDtypeStruct((ROWS, channels), bf16),
            jax.ShapeDtypeStruct((BLOCKS, HELD, BLOCKS * send_rows), bf16),
        ),
        in_specs=[hbm] * len(operands),
        out_specs=(hbm, hbm, hbm),
        scratch_shapes=[
            pltpu.VMEM((3, ROWS, channels), bf16),
            pltpu.VMEM((1, channels), f32),
            pltpu.VMEM(owner.shape, jnp.int32),
            pltpu.VMEM(slot.shape, jnp.int32),
            *(pltpu.VMEM(c.shape, c.dtype) for c in constants),
            pltpu.VMEM((2, channels, 8 * ROWS), bf16),
            pltpu.VMEM((8, 2, half // 2, ROWS), bf16),
            pltpu.VMEM((2 * channels, half), f32),
            pltpu.VMEM((BLOCKS, 3, HELD, ROWS), bf16),
            pltpu.VMEM((BLOCKS, 3, HELD, ROWS), bf16),
            pltpu.VMEM((2, BLOCKS, HELD, half), bf16),
            pltpu.VMEM((2, BLOCKS, HELD, half), bf16),
            pltpu.VMEM((2, BLOCKS, HELD, ROWS), bf16),
            pltpu.VMEM((2, BLOCKS, HELD, ROWS), bf16),
            pltpu.VMEM((BLOCKS, HELD, BLOCKS * send_rows), bf16),
            pltpu.VMEM((8, 128), jnp.int32),
            pltpu.VMEM((BLOCKS, 8, 128), jnp.int32),
            pltpu.VMEM((2, ROWS, channels), bf16),
            dma((24,)), dma((2,)), dma((2,)), dma((2, 2, 2)), dma((2, 2, 2)), dma((2, 2)), dma((2, 2)),
            dma((BLOCKS,)), dma((BLOCKS,)), dma((2, BLOCKS)), dma((2, BLOCKS)),
            dma((2, BLOCKS)), dma((2, BLOCKS)), dma((BLOCKS,)), dma((BLOCKS,)), dma((BLOCKS,)), dma((BLOCKS,)),
        ],
        compiler_params=pltpu.CompilerParams(
            collective_id=0, has_side_effects=True, vmem_limit_bytes=67043328
        ),
    )(*operands)
    gate_grad, filter_grad, grad_rows = finish(gate_grad, filter_grad, grad_rows.reshape(channels, -1))
    grid = (BLOCKS, ROWS // BLOCKS, channels)
    return (gate_grad.reshape(grid), filter_grad.reshape(grid), grad_rows)


def solution(mesh):
    return jax.shard_map(
        shards,
        mesh=mesh,
        in_specs=(
            P("bins", "chan"),
            P("bins", "chan"),
            P("bins", "chan"),
            P("chan"),
            P("bins", "chan"),
            P("chan", None),
            P(None, "bins"),
            P(None, "bins"),
        ),
        out_specs=(P(None, "bins", "chan"), P(None, "bins", "chan"), P("bins", "chan")),
        check_vma=False,
    )
```

```python
import math

import jax
import jax.numpy as jnp
import numpy as np
from jax import lax
from jax.experimental import pallas as pl
from jax.experimental.pallas import tpu as pltpu
from jax.sharding import PartitionSpec as P

BLOCKS = 16
HELD = 16
ROWS = 512
HALF = BLOCKS + 1
LENGTH = 2 * BLOCKS * ROWS


def tables():
    k1 = np.arange(HALF)
    i = np.arange(BLOCKS)
    ang = 2.0 * np.pi * np.outer(k1, i) / (2 * BLOCKS)
    eye = np.eye(HELD)
    ahead = np.concatenate([np.kron(np.cos(ang), eye), np.kron(-np.sin(ang), eye)], axis=0)
    weight = np.where((k1 == 0) | (k1 == BLOCKS), 1.0, 2.0)[None, :] / LENGTH
    back_re = np.kron(weight * np.cos(ang).T, eye)
    back_im = np.kron(-(weight * np.sin(ang).T)[:, 1:BLOCKS], eye)
    back = np.concatenate([back_re, back_im], axis=1)
    r = np.arange(ROWS)
    twist = 2.0 * np.pi * np.outer(k1, r) / LENGTH
    inner = 2.0 * np.pi * (np.outer(r, r) % ROWS) / ROWS
    return (
        jnp.asarray(ahead, jnp.bfloat16),
        jnp.asarray(back, jnp.bfloat16),
        jnp.asarray(np.cos(twist)[:, None, :], jnp.float32),
        jnp.asarray(np.sin(twist)[:, None, :], jnp.float32),
        jnp.asarray(np.cos(inner), jnp.bfloat16),
        jnp.asarray(np.sin(inner), jnp.bfloat16),
    )


def mm(a, b):
    return jnp.dot(a, b, preferred_element_type=jnp.float32)


def stage_rows(value):
    return value.reshape(HALF, HELD, ROWS)


def flat(value):
    return value.reshape(HALF * HELD, ROWS)


def forward(value, ahead, tw_cos, tw_sin, in_cos, in_sin):
    part = mm(ahead, value)
    n = HALF * HELD
    re, im = stage_rows(part[:n]), stage_rows(part[n:])
    z_re = flat(re * tw_cos + im * tw_sin)
    z_im = flat(im * tw_cos - re * tw_sin)
    z = jnp.concatenate([z_re, z_im], axis=0).astype(jnp.bfloat16)
    by_cos, by_sin = mm(z, in_cos), mm(z, in_sin)
    return by_cos[:n] + by_sin[n:], by_cos[n:] - by_sin[:n]


def inverse(s_re, s_im, back, tw_cos, tw_sin, in_cos, in_sin):
    n = HALF * HELD
    q = jnp.concatenate([s_re, s_im], axis=0).astype(jnp.bfloat16)
    by_cos, by_sin = mm(q, in_cos), mm(q, in_sin)
    re, im = stage_rows(by_cos[:n] - by_sin[n:]), stage_rows(by_cos[n:] + by_sin[:n])
    t_re = flat(re * tw_cos - im * tw_sin)
    t_im = flat(im * tw_cos + re * tw_sin)[HELD : BLOCKS * HELD]
    t = jnp.concatenate([t_re, t_im], axis=0).astype(jnp.bfloat16)
    return mm(back, t)


def to_columns(value):
    group = lax.broadcasted_iota(jnp.int32, (HELD, 128), 1) // 32
    out = [[None] * 4 for _ in range(BLOCKS)]
    for i_hi in range(4):
        for j_hi in range(4):
            tiles = [
                value[(4 * i_hi + i_lo) * HELD : (4 * i_hi + i_lo + 1) * HELD, 128 * j_hi : 128 * (j_hi + 1)]
                for i_lo in range(4)
            ]
            for j_lo in range(4):
                acc = None
                for i_lo in range(4):
                    shift = (32 * (i_lo - j_lo)) % 128
                    turned = pltpu.roll(tiles[i_lo], shift, 1) if shift else tiles[i_lo]
                    acc = turned if acc is None else jnp.where(group == i_lo, turned, acc)
                out[4 * j_hi + j_lo][i_hi] = acc
    return jnp.concatenate([jnp.concatenate(row, axis=1) for row in out], axis=0)


def remote(src, dst, send, recv, bins, chan):
    return pltpu.make_async_remote_copy(
        src_ref=src,
        dst_ref=dst,
        send_sem=send,
        recv_sem=recv,
        device_id=(bins, chan),
        device_id_type=pl.DeviceIdType.MESH,
    )


def kernel(
    x_hbm, h_hbm, gate_hbm, skip_hbm, og_hbm, w_hbm, owner_hbm, slot_hbm, *rest
):
    tables_hbm, rest = rest[:TABLES], rest[TABLES:]
    gate_out, filter_out, rows_out = rest[:3]
    (
        raw, skip_ref, owner_ref, slot_ref, *rest
    ) = rest[3:]
    tables_ref, rest = rest[:TABLES], rest[TABLES:]
    (
        w_all, og_all, acc, pair_src, pair, gate_src, gate_came, mix_src, mix, g_src, g_came, gated_src,
        done, came, outbox, map_src, maps, turned,
        local_sem, w_sem, mate_sem, side_send, side_recv, far_send, far_recv,
        pair_send, pair_recv, gate_send, gate_recv, mix_send, mix_recv, g_send, g_recv, gated_send, gated_recv,
        done_send, done_recv, box_send, box_recv, map_send, map_recv,
    ) = rest
    f32, bf16 = jnp.float32, jnp.bfloat16
    rows = BLOCKS * HELD
    send_rows = 2 * ROWS // BLOCKS
    b = lax.axis_index("bins")
    k = lax.axis_index("chan")
    b_y, b_z = lax.div(b, 4), lax.rem(b, 4)
    chip, core = lax.div(k, 2), lax.rem(k, 2)
    right, left, across = lax.rem(chip + 1, 4), lax.rem(chip + 3, 4), lax.rem(chip + 2, 4)
    mate = 2 * chip + 1 - core

    def peer(p):
        return 4 * lax.rem(b_y + p // 4, 4) + lax.rem(b_z + p % 4, 4)

    local = []

    def bring(src, dst):
        copy = pltpu.make_async_copy(src, dst, local_sem.at[len(local)])
        copy.start()
        local.append(copy)
        return copy

    own_raw = [bring(ref, raw.at[n]) for n, ref in enumerate((x_hbm, h_hbm, gate_hbm))]
    own_og = bring(og_hbm.at[core], og_all.at[k])
    own_w = bring(w_hbm, w_all.at[core])
    own_small = [bring(*pair) for pair in ((skip_hbm, skip_ref), (owner_hbm, owner_ref), (slot_hbm, slot_ref))]
    own_tables = [bring(*pair) for pair in zip(tables_hbm, tables_ref)]

    barrier = pltpu.get_barrier_semaphore()

    def greet(bins, chan):
        pl.semaphore_signal(barrier, inc=1, device_id=(bins, chan), device_id_type=pl.DeviceIdType.MESH)

    for p in ORDER:
        greet(peer(p), k)
        greet(peer(p), mate)
    greet(b, mate)
    for side in (right, left):
        for c in range(2):
            greet(b, 2 * side + c)
    pl.semaphore_wait(barrier, 2 * BLOCKS - 1 + 4)

    def side_copy(way, part, c):
        to = (right, left)[way]
        return remote(
            og_hbm.at[c, :, part], og_all.at[k, :, part],
            side_send.at[way, part, c], side_recv.at[way, part, core], b, 2 * to + c,
        )

    for turn in range(2):
        for c in range(2):
            side_copy(0, turn, c).start()
            side_copy(1, 1 - turn, c).start()
    mate_og = remote(og_hbm.at[1 - core], og_all.at[k], mate_sem.at[0], mate_sem.at[1], b, mate)
    mate_og.start()
    mate_w = remote(w_hbm, w_all.at[core], w_sem.at[0], w_sem.at[1], b, mate)
    mate_w.start()

    for n in range(2):
        own_raw[n].wait()
        pair_src[:, n] = raw[n].T.reshape(BLOCKS, HELD, ROWS)

    def pair_copy(p):
        to = peer(p)
        return remote(pair_src.at[to], pair.at[b], pair_send.at[p], pair_recv.at[p], to, k)

    for p in ORDER:
        pair_copy(p).start()
    own_pair = bring(pair_src.at[b], pair.at[b])
    own_raw[2].wait()
    gate_src[...] = raw[2].T.reshape(BLOCKS, HELD, ROWS)

    def gate_copy(p):
        to = peer(p)
        return remote(gate_src.at[to], gate_came.at[b], gate_send.at[p], gate_recv.at[p], to, k)

    for p in ORDER:
        gate_copy(p).start()
    own_gate = bring(gate_src.at[b], gate_came.at[b])

    def side_arrived(way, part, c):
        src = 2 * (left, right)[way] + c
        return remote(
            og_hbm.at[c, :, part], og_all.at[src, :, part],
            side_send.at[way, part, c], side_recv.at[way, part, c], b, mate,
        )

    def far_copy(way, c, s):
        src = 2 * (left, right)[way] + c
        to = (right, left)[way]
        return remote(
            og_all.at[src, s, way], og_all.at[src, s, way],
            far_send.at[way, c, s], far_recv.at[way, c, s], b, 2 * to + core,
        )

    for c in range(2):
        for way in range(2):
            side_arrived(way, way, c).wait_recv()
    for s in range(2):
        for c in range(2):
            for way in range(2):
                far_copy(way, c, s).start()

    def term(source, tokens):
        columns = pl.ds(pl.multiple_of(source * ROWS, ROWS), ROWS)
        weights = w_all[:, :, columns].reshape(2 * rows, ROWS)
        return lax.dot_general(weights, tokens, (((1,), (1,)), ((), ())), preferred_element_type=f32)

    def near(source):
        return term(source, og_all[source].reshape(ROWS // 2, ROWS))

    own_w.wait()
    own_og.wait()
    mate_w.wait()
    mate_og.wait()
    acc[...] = near(k) + near(mate)

    for copy in own_small + own_tables:
        copy.wait()
    ahead, back, tw_cos, tw_sin, in_cos, in_sin = (ref[...] for ref in tables_ref)
    forward_tables = (ahead, tw_cos, tw_sin, in_cos, in_sin)
    inverse_tables = (back, tw_cos, tw_sin, in_cos, in_sin)
    lanes = lax.broadcasted_iota(jnp.int32, (rows, rows), 1)
    held = lax.rem(lax.broadcasted_iota(jnp.int32, (rows, rows), 0), HELD)
    skip = jnp.sum(jnp.where(lanes == held + HELD * b, skip_ref[...], 0.0), axis=1, keepdims=True)
    for p in ORDER:
        pair_copy(p).wait()
    own_pair.wait()
    x = pair[:, 0].reshape(rows, ROWS)
    x_re, x_im = forward(x, *forward_tables)
    h_re, h_im = forward(pair[:, 1].reshape(rows, ROWS), *forward_tables)
    conv = inverse(x_re * h_re - x_im * h_im, x_re * h_im + x_im * h_re, *inverse_tables)
    with_skip = (conv + skip * x.astype(f32)).astype(bf16)
    for hand in range(2):
        mix_src[hand] = with_skip[:, rows * hand : rows * (hand + 1)].reshape(BLOCKS, HELD, ROWS // 2)

    def mix_copy(p, c):
        to = peer(p)
        hand = lax.rem(core + c, 2)
        return remote(
            mix_src.at[hand, to], mix.at[core, b], mix_send.at[c, p], mix_recv.at[c, p], to, 2 * chip + hand
        )

    for p in ORDER:
        mix_copy(p, 0).start()
        mix_copy(p, 1).start()
    mix_copy(0, 1).start()
    own_mix = bring(mix_src.at[core, b], mix.at[core, b])

    odd = lax.rem(b, 2)
    target = (owner_ref[...] + odd * (1 - 2 * lax.rem(owner_ref[...], 2))) * send_rows + slot_ref[...] - b * send_rows
    target = jnp.concatenate([target[i : i + 1] for i in range(BLOCKS)], axis=1)
    places = lax.broadcasted_iota(jnp.int32, (BLOCKS * send_rows, ROWS), 0)
    chosen = jnp.where(places == target, 1.0, 0.0).astype(bf16)
    token = lax.broadcasted_iota(jnp.int32, (16, ROWS), 1)
    which = lax.broadcasted_iota(jnp.int32, (16, ROWS), 0)
    digits = jnp.where(which == 0, lax.rem(token, 128), jnp.where(which == 1, lax.div(token, 128) + 1, 0))
    digits = lax.dot_general(
        digits.astype(f32).astype(bf16), chosen, (((1,), (1,)), ((), ())), preferred_element_type=f32
    )
    origin = (digits[0:1] + 128.0 * digits[1:2]).astype(jnp.int32)
    map_src[...] = jnp.concatenate([origin[:, 128 * n : 128 * (n + 1)] for n in range(8)], axis=0)

    def map_copy(p):
        to = peer(p)
        return remote(map_src, maps.at[b], map_send.at[p], map_recv.at[p], to, k)

    for p in ORDER:
        map_copy(p).start()
    own_map = bring(map_src, maps.at[b])

    for c in range(2):
        for way in range(2):
            side_arrived(way, 1 - way, c).wait_recv()
            acc[...] += near(2 * (left, right)[way] + c)

    def g_copy(p, c, s):
        to = peer(p)
        hand = lax.rem(core + c, 2)
        return remote(
            g_src.at[s, hand, to], g_came.at[core, s, b],
            g_send.at[s, c, p], g_recv.at[s, c, p], to, 2 * chip + hand,
        )

    own_g = []
    for s in range(2):
        for c in range(2):
            for way in range(2):
                far_copy(way, c, s).wait_recv()
        part = acc[:, 128 * s : 128 * (s + 1)]
        for c in range(2):
            part = part + term(2 * across + c, og_all[2 * across + c, s].reshape(128, ROWS))
        g_src[s] = part.astype(bf16).reshape(2, BLOCKS, HELD, 128)
        for p in ORDER:
            g_copy(p, 0, s).start()
            g_copy(p, 1, s).start()
        g_copy(0, 1, s).start()
        own_g.append(bring(g_src.at[s, core, b], g_came.at[core, s, b]))

    for p in ORDER:
        mix_copy(p, 0).wait()
        mix_copy(p, 1).wait()
    mix_copy(0, 1).wait()
    own_mix.wait()
    g_block = jnp.concatenate([g_src[s].reshape(2 * rows, 128) for s in range(2)], axis=1).astype(f32)
    gated = (g_block * mix[...].reshape(2 * rows, ROWS // 2).astype(f32)).astype(bf16).T
    for hand in range(2):
        gated_src[hand] = gated[:, rows * hand : rows * (hand + 1)].reshape(8, ROWS // BLOCKS, rows)

    def gated_copy(q, c):
        column = lax.rem(b + q, 8)
        hand = lax.rem(core + c, 2)
        return remote(
            gated_src.at[hand, column], gate_out.at[b],
            gated_send.at[c, q], gated_recv.at[b], 8 * core + column, 2 * chip + hand,
        )

    stays = lax.div(b, 8) == core
    own_gated = pltpu.make_async_copy(gated_src.at[core, lax.rem(b, 8)], gate_out.at[b], gated_recv.at[b])
    for q in range(1, 8):
        gated_copy(q, 0).start()
        gated_copy(q, 1).start()
    gated_copy(0, 1).start()

    @pl.when(stays)
    def _():
        own_gated.start()

    @pl.when(jnp.logical_not(stays))
    def _():
        gated_copy(0, 0).start()

    for p in ORDER:
        gate_copy(p).wait()
    own_gate.wait()
    for p in ORDER:
        for s in range(2):
            g_copy(p, 0, s).wait()
            g_copy(p, 1, s).wait()
    for s in range(2):
        g_copy(0, 1, s).wait()
        own_g[s].wait()
    g = jnp.concatenate([g_came[h, s].reshape(rows, 128) for h in range(2) for s in range(2)], axis=1)
    g = g.astype(f32)
    dy = (g * gate_came[...].reshape(rows, ROWS).astype(f32)).astype(bf16)
    y_re, y_im = forward(dy, *forward_tables)

    def done_copy(p):
        to = peer(p)
        return remote(done.at[to], came.at[b], done_send.at[p], done_recv.at[p], to, k)

    lag = inverse(y_re * x_re + y_im * x_im, y_im * x_re - y_re * x_im, *inverse_tables)
    done[...] = to_columns(lag * (1.0 / math.sqrt(BLOCKS * ROWS))).astype(bf16).reshape(BLOCKS, HELD, ROWS)
    for p in ORDER:
        done_copy(p).start()
    own_done = bring(done.at[b], came.at[b])
    grad = inverse(h_re * y_re + h_im * y_im, h_re * y_im - h_im * y_re, *inverse_tables)
    columns = to_columns(grad + skip * dy.astype(f32))
    for p in ORDER:
        map_copy(p).wait()
    own_map.wait()
    low_half = lax.broadcasted_iota(jnp.int32, (HELD, 128), 1) < 64
    for m in range(BLOCKS // 2):
        picked = []
        for j in (2 * m, 2 * m + 1):
            held = columns[j * HELD : (j + 1) * HELD]
            lane, tile = lax.rem(maps[j], 128), lax.div(maps[j], 128)
            tiles = []
            for n in range(8):
                at = jnp.broadcast_to(lane[n : n + 1], (HELD, 128))
                which = jnp.broadcast_to(tile[n : n + 1], (HELD, 128))
                value = jnp.zeros((HELD, 128), f32)
                for t in range(4):
                    found = jnp.take_along_axis(held[:, 128 * t : 128 * (t + 1)], at, axis=1)
                    value = jnp.where(which == t + 1, found, value)
                tiles.append(value)
            picked.append(tiles)
        for n in range(8):
            even, other = picked[0][n], picked[1][n]
            outbox[2 * n, :, 128 * m : 128 * (m + 1)] = jnp.where(low_half, even, other).astype(bf16)
            outbox[2 * n + 1, :, 128 * m : 128 * (m + 1)] = jnp.where(low_half, other, even).astype(bf16)

    def box_copy(p):
        to = peer(p)
        return remote(outbox.at[to], rows_out.at[b], box_send.at[p], box_recv.at[p], to, k)

    for p in ORDER:
        box_copy(p).start()
    own_box = bring(outbox.at[b], rows_out.at[b])

    for p in ORDER:
        done_copy(p).wait()
    own_done.wait()
    turned[...] = came[...].reshape(rows, ROWS).T
    result = bring(turned, filter_out)
    for c in range(2):
        for way in range(2):
            for part in range(2):
                far_copy(way, c, part).wait_send()
                side_copy(way, part, c).wait_send()

    def gated_arrived(i):
        return remote(gated_src.at[0, 0], gate_out.at[i], gated_send.at[0, 0], gated_recv.at[i], b, mate)

    for p in ORDER:
        gated_arrived(lax.rem(b + p, BLOCKS)).wait_recv()
    for q in range(1, 8):
        gated_copy(q, 0).wait_send()
        gated_copy(q, 1).wait_send()
    gated_copy(0, 1).wait_send()

    @pl.when(stays)
    def _():
        own_gated.wait()

    @pl.when(jnp.logical_not(stays))
    def _():
        gated_copy(0, 0).wait_send()
        gated_arrived(b).wait_recv()

    for p in ORDER:
        box_copy(p).wait()
    own_box.wait()
    result.wait()


ORDER = sorted(range(1, BLOCKS), key=lambda p: -(min(p // 4, 4 - p // 4) + min(p % 4, 4 - p % 4)))
TABLES = 6


def finish_kernel(gate_hbm, filter_hbm, rows_hbm, gate_out, filter_out, rows_out, gate, taps, wide, moved, ranked, sem):
    odd = lax.rem(lax.axis_index("bins"), 2)
    span = 256
    parts = rows_hbm.shape[1] // span
    reads, writes = [], []

    def read(src, held):
        reads.append(pltpu.make_async_copy(src, held, sem.at[len(reads)]))
        reads[-1].start()
        return reads[-1]

    def write(held, dst):
        writes.append(pltpu.make_async_copy(held, dst, sem.at[8 + len(writes)]))
        writes[-1].start()

    taps_in = read(filter_hbm, taps)
    rows_in = [read(rows_hbm.at[:, pl.ds(n * span, span)], moved.at[n]) for n in range(parts)]
    gate_in = read(gate_hbm, gate)
    taps_in.wait()
    wide[...] = taps[...].astype(jnp.float32)
    write(wide, filter_out)
    for n in range(parts):
        rows_in[n].wait()
        ranked[n] = moved[n].T.reshape(span // 64, 64, 256)
        for q in range(span // 64):
            group = n * (span // 64) + q
            group = group + odd * (1 - 2 * (q % 2))
            write(ranked.at[n, q], rows_out.at[pl.ds(group * 64, 64)])
    gate_in.wait()
    write(gate, gate_out)
    for copy in writes:
        copy.wait()


def finish(gate_grad, filter_grad, grad_rows):
    f32 = jnp.float32
    channels, count = grad_rows.shape
    return pl.pallas_call(
        finish_kernel,
        out_shape=(
            jax.ShapeDtypeStruct(gate_grad.shape, gate_grad.dtype),
            jax.ShapeDtypeStruct(filter_grad.shape, f32),
            jax.ShapeDtypeStruct((count, channels), grad_rows.dtype),
        ),
        in_specs=[pl.BlockSpec(memory_space=pl.ANY)] * 3,
        out_specs=(pl.BlockSpec(memory_space=pl.ANY),) * 3,
        scratch_shapes=[
            pltpu.VMEM(gate_grad.shape, gate_grad.dtype),
            pltpu.VMEM(filter_grad.shape, filter_grad.dtype),
            pltpu.VMEM(filter_grad.shape, f32),
            pltpu.VMEM((count // 256, channels, 256), grad_rows.dtype),
            pltpu.VMEM((count // 256, 4, 64, channels), grad_rows.dtype),
            pltpu.SemaphoreType.DMA((32,)),
        ],
        compiler_params=pltpu.CompilerParams(vmem_limit_bytes=67043328),
    )(gate_grad, filter_grad, grad_rows)


def shards(tokens_in, filters, gate, skip, out_grad, out_weight, owner, slot):
    channels = tokens_in.shape[1]
    send_rows = 2 * ROWS // BLOCKS
    half = ROWS // 2
    dma = pltpu.SemaphoreType.DMA
    hbm = pl.BlockSpec(memory_space=pl.ANY)
    f32, bf16 = jnp.float32, jnp.bfloat16
    constants = tables()
    operands = (
        tokens_in, filters, gate, skip.reshape(1, channels), out_grad.reshape(2, 2, 2, 64, ROWS), out_weight,
        owner, slot, *constants,
    )
    gate_grad, filter_grad, grad_rows = pl.pallas_call(
        kernel,
        out_shape=(
            jax.ShapeDtypeStruct((BLOCKS, ROWS // BLOCKS, channels), bf16),
            jax.ShapeDtypeStruct((ROWS, channels), bf16),
            jax.ShapeDtypeStruct((BLOCKS, HELD, BLOCKS * send_rows), bf16),
        ),
        in_specs=[hbm] * len(operands),
        out_specs=(hbm, hbm, hbm),
        scratch_shapes=[
            pltpu.VMEM((3, ROWS, channels), bf16),
            pltpu.VMEM((1, channels), f32),
            pltpu.VMEM(owner.shape, jnp.int32),
            pltpu.VMEM(slot.shape, jnp.int32),
            *(pltpu.VMEM(c.shape, c.dtype) for c in constants),
            pltpu.VMEM((2, channels, 8 * ROWS), bf16),
            pltpu.VMEM((8, 2, 2, 64, ROWS), bf16),
            pltpu.VMEM((2 * channels, half), f32),
            pltpu.VMEM((BLOCKS, 2, HELD, ROWS), bf16),
            pltpu.VMEM((BLOCKS, 2, HELD, ROWS), bf16),
            pltpu.VMEM((BLOCKS, HELD, ROWS), bf16),
            pltpu.VMEM((BLOCKS, HELD, ROWS), bf16),
            pltpu.VMEM((2, BLOCKS, HELD, half), bf16),
            pltpu.VMEM((2, BLOCKS, HELD, half), bf16),
            pltpu.VMEM((2, 2, BLOCKS, HELD, 128), bf16),
            pltpu.VMEM((2, 2, BLOCKS, HELD, 128), bf16),
            pltpu.VMEM((2, 8, ROWS // BLOCKS, channels), bf16),
            pltpu.VMEM((BLOCKS, HELD, ROWS), bf16),
            pltpu.VMEM((BLOCKS, HELD, ROWS), bf16),
            pltpu.VMEM((BLOCKS, HELD, BLOCKS * send_rows), bf16),
            pltpu.VMEM((8, 128), jnp.int32),
            pltpu.VMEM((BLOCKS, 8, 128), jnp.int32),
            pltpu.VMEM((ROWS, channels), bf16),
            dma((24,)), dma((2,)), dma((2,)), dma((2, 2, 2)), dma((2, 2, 2)), dma((2, 2, 2)), dma((2, 2, 2)),
            dma((BLOCKS,)), dma((BLOCKS,)), dma((BLOCKS,)), dma((BLOCKS,)), dma((2, BLOCKS)), dma((2, BLOCKS)),
            dma((2, 2, BLOCKS)), dma((2, 2, BLOCKS)), dma((2, 8)), dma((BLOCKS,)),
            dma((BLOCKS,)), dma((BLOCKS,)), dma((BLOCKS,)), dma((BLOCKS,)), dma((BLOCKS,)), dma((BLOCKS,)),
        ],
        compiler_params=pltpu.CompilerParams(
            collective_id=0, has_side_effects=True, vmem_limit_bytes=67043328
        ),
    )(*operands)
    gate_grad, filter_grad, grad_rows = finish(gate_grad, filter_grad, grad_rows.reshape(channels, -1))
    grid = (BLOCKS, ROWS // BLOCKS, channels)
    return (gate_grad, filter_grad.reshape(grid), grad_rows)


def solution(mesh):
    return jax.shard_map(
        shards,
        mesh=mesh,
        in_specs=(
            P("bins", "chan"),
            P("bins", "chan"),
            P("bins", "chan"),
            P("chan"),
            P("bins", "chan"),
            P("chan", None),
            P(None, "bins"),
            P(None, "bins"),
        ),
        out_specs=(P(None, "bins", "chan"), P(None, "bins", "chan"), P("bins", "chan")),
        check_vma=False,
    )
```

```python
import math

import jax
import jax.numpy as jnp
import numpy as np
from jax import lax
from jax.experimental import pallas as pl
from jax.experimental.pallas import tpu as pltpu
from jax.sharding import PartitionSpec as P

BLOCKS = 16
HELD = 16
ROWS = 512
HALF = BLOCKS + 1
LENGTH = 2 * BLOCKS * ROWS


def tables():
    k1 = np.arange(HALF)
    i = np.arange(BLOCKS)
    ang = 2.0 * np.pi * np.outer(k1, i) / (2 * BLOCKS)
    eye = np.eye(HELD)
    ahead = np.concatenate([np.kron(np.cos(ang), eye), np.kron(-np.sin(ang), eye)], axis=0)
    weight = np.where((k1 == 0) | (k1 == BLOCKS), 1.0, 2.0)[None, :] / LENGTH
    back_re = np.kron(weight * np.cos(ang).T, eye)
    back_im = np.kron(-(weight * np.sin(ang).T)[:, 1:BLOCKS], eye)
    back = np.concatenate([back_re, back_im], axis=1)
    r = np.arange(ROWS)
    twist = 2.0 * np.pi * np.outer(k1, r) / LENGTH
    inner = 2.0 * np.pi * (np.outer(r, r) % ROWS) / ROWS
    return (
        jnp.asarray(ahead, jnp.bfloat16),
        jnp.asarray(back, jnp.bfloat16),
        jnp.asarray(np.cos(twist)[:, None, :], jnp.float32),
        jnp.asarray(np.sin(twist)[:, None, :], jnp.float32),
        jnp.asarray(np.cos(inner), jnp.bfloat16),
        jnp.asarray(np.sin(inner), jnp.bfloat16),
    )


def mm(a, b):
    return jnp.dot(a, b, preferred_element_type=jnp.float32)


def stage_rows(value):
    return value.reshape(HALF, HELD, ROWS)


def flat(value):
    return value.reshape(HALF * HELD, ROWS)


def forward(value, ahead, tw_cos, tw_sin, in_cos, in_sin):
    part = mm(ahead, value)
    n = HALF * HELD
    re, im = stage_rows(part[:n]), stage_rows(part[n:])
    z_re = flat(re * tw_cos + im * tw_sin)
    z_im = flat(im * tw_cos - re * tw_sin)
    z = jnp.concatenate([z_re, z_im], axis=0).astype(jnp.bfloat16)
    by_cos, by_sin = mm(z, in_cos), mm(z, in_sin)
    return by_cos[:n] + by_sin[n:], by_cos[n:] - by_sin[:n]


def inverse(s_re, s_im, back, tw_cos, tw_sin, in_cos, in_sin):
    n = HALF * HELD
    q = jnp.concatenate([s_re, s_im], axis=0).astype(jnp.bfloat16)
    by_cos, by_sin = mm(q, in_cos), mm(q, in_sin)
    re, im = stage_rows(by_cos[:n] - by_sin[n:]), stage_rows(by_cos[n:] + by_sin[:n])
    t_re = flat(re * tw_cos - im * tw_sin)
    t_im = flat(im * tw_cos + re * tw_sin)[HELD : BLOCKS * HELD]
    t = jnp.concatenate([t_re, t_im], axis=0).astype(jnp.bfloat16)
    return mm(back, t)


def to_columns(value):
    group = lax.broadcasted_iota(jnp.int32, (HELD, 128), 1) // 32
    out = [[None] * 4 for _ in range(BLOCKS)]
    for i_hi in range(4):
        for j_hi in range(4):
            tiles = [
                value[(4 * i_hi + i_lo) * HELD : (4 * i_hi + i_lo + 1) * HELD, 128 * j_hi : 128 * (j_hi + 1)]
                for i_lo in range(4)
            ]
            for j_lo in range(4):
                acc = None
                for i_lo in range(4):
                    shift = (32 * (i_lo - j_lo)) % 128
                    turned = pltpu.roll(tiles[i_lo], shift, 1) if shift else tiles[i_lo]
                    acc = turned if acc is None else jnp.where(group == i_lo, turned, acc)
                out[4 * j_hi + j_lo][i_hi] = acc
    return jnp.concatenate([jnp.concatenate(row, axis=1) for row in out], axis=0)


def remote(src, dst, send, recv, bins, chan):
    return pltpu.make_async_remote_copy(
        src_ref=src,
        dst_ref=dst,
        send_sem=send,
        recv_sem=recv,
        device_id=(bins, chan),
        device_id_type=pl.DeviceIdType.MESH,
    )


def drain(ref, sem):
    pltpu.make_async_copy(ref, ref, sem).wait()


def kernel(
    x_hbm, h_hbm, gate_hbm, skip_hbm, og_hbm, w_hbm, owner_hbm, slot_hbm, *rest
):
    tables_hbm, rest = rest[:TABLES], rest[TABLES:]
    gate_out, filter_out, rows_out = rest[:3]
    (
        raw, skip_ref, owner_ref, slot_ref, *rest
    ) = rest[3:]
    tables_ref, rest = rest[:TABLES], rest[TABLES:]
    (
        w_all, og_all, acc, pair_src, pair, gate_src, gate_came, mix_src, mix, g_src, g_came, gated_src,
        done, came, outbox, map_src, maps, turned,
        local_sem, w_sem, mate_sem, side_send, side_recv, far_send, far_recv,
        pair_send, pair_recv, gate_send, gate_recv, mix_send, mix_recv, g_send, g_recv, gated_send, gated_recv,
        done_send, done_recv, box_send, box_recv, map_send, map_recv,
    ) = rest
    f32, bf16 = jnp.float32, jnp.bfloat16
    rows = BLOCKS * HELD
    send_rows = 2 * ROWS // BLOCKS
    b = lax.axis_index("bins")
    k = lax.axis_index("chan")
    b_y, b_z = lax.div(b, 4), lax.rem(b, 4)
    chip, core = lax.div(k, 2), lax.rem(k, 2)
    right, left, across = lax.rem(chip + 1, 4), lax.rem(chip + 3, 4), lax.rem(chip + 2, 4)
    mate = 2 * chip + 1 - core

    def peer(p):
        return 4 * lax.rem(b_y + p // 4, 4) + lax.rem(b_z + p % 4, 4)

    local = []

    def bring(src, dst, sem=None):
        copy = pltpu.make_async_copy(src, dst, local_sem.at[len(local)] if sem is None else sem)
        copy.start()
        if sem is None:
            local.append(copy)
        return copy

    own_raw = [bring(ref, raw.at[n]) for n, ref in enumerate((x_hbm, h_hbm, gate_hbm))]
    own_og = bring(og_hbm.at[core], og_all.at[k])
    own_w = bring(w_hbm, w_all.at[core])
    own_small = [bring(*pair) for pair in ((skip_hbm, skip_ref), (owner_hbm, owner_ref), (slot_hbm, slot_ref))]
    own_tables = [bring(*pair) for pair in zip(tables_hbm, tables_ref)]

    barrier = pltpu.get_barrier_semaphore()

    def greet(bins, chan):
        pl.semaphore_signal(barrier, inc=1, device_id=(bins, chan), device_id_type=pl.DeviceIdType.MESH)

    for p in ORDER:
        greet(peer(p), k)
        greet(peer(p), mate)
    greet(b, mate)
    for side in (right, left):
        for c in range(2):
            greet(b, 2 * side + c)
    pl.semaphore_wait(barrier, 2 * BLOCKS - 1 + 4)

    def side_copy(way, part, c):
        to = (right, left)[way]
        return remote(
            og_hbm.at[c, :, part], og_all.at[k, :, part],
            side_send, side_recv.at[way, part], b, 2 * to + c,
        )

    for turn in range(2):
        for c in range(2):
            side_copy(0, turn, c).start()
            side_copy(1, 1 - turn, c).start()
    mate_og = remote(og_hbm.at[1 - core], og_all.at[k], mate_sem.at[0], mate_sem.at[1], b, mate)
    mate_og.start()
    mate_w = remote(w_hbm, w_all.at[core], w_sem.at[0], w_sem.at[1], b, mate)
    mate_w.start()

    for n in range(2):
        own_raw[n].wait()
        pair_src[:, n] = raw[n].T.reshape(BLOCKS, HELD, ROWS)

    def pair_copy(p):
        to = peer(p)
        return remote(pair_src.at[to], pair.at[b], pair_send, pair_recv, to, k)

    for p in ORDER:
        pair_copy(p).start()
    bring(pair_src.at[b], pair.at[b], pair_recv)
    own_raw[2].wait()
    gate_src[...] = raw[2].T.reshape(BLOCKS, HELD, ROWS)

    def gate_copy(p):
        to = peer(p)
        return remote(gate_src.at[to], gate_came.at[b], gate_send, gate_recv, to, k)

    for p in ORDER:
        gate_copy(p).start()
    bring(gate_src.at[b], gate_came.at[b], gate_recv)

    def side_arrived(way, part):
        src = 2 * (left, right)[way]
        drain(og_all.at[pl.ds(src, 2), :, part], side_recv.at[way, part])

    def far_copy(way, c, s):
        src = 2 * (left, right)[way] + c
        to = (right, left)[way]
        return remote(
            og_all.at[src, s, way], og_all.at[src, s, way],
            far_send, far_recv.at[s], b, 2 * to + core,
        )

    for way in range(2):
        side_arrived(way, way)
    for s in range(2):
        for c in range(2):
            for way in range(2):
                far_copy(way, c, s).start()

    def term(source, tokens):
        columns = pl.ds(pl.multiple_of(source * ROWS, ROWS), ROWS)
        weights = w_all[:, :, columns].reshape(2 * rows, ROWS)
        return lax.dot_general(weights, tokens, (((1,), (1,)), ((), ())), preferred_element_type=f32)

    def near(source):
        return term(source, og_all[source].reshape(ROWS // 2, ROWS))

    own_w.wait()
    own_og.wait()
    mate_w.wait()
    mate_og.wait()
    acc[...] = near(k) + near(mate)

    for copy in own_small + own_tables:
        copy.wait()
    ahead, back, tw_cos, tw_sin, in_cos, in_sin = (ref[...] for ref in tables_ref)
    forward_tables = (ahead, tw_cos, tw_sin, in_cos, in_sin)
    inverse_tables = (back, tw_cos, tw_sin, in_cos, in_sin)
    lanes = lax.broadcasted_iota(jnp.int32, (rows, rows), 1)
    held = lax.rem(lax.broadcasted_iota(jnp.int32, (rows, rows), 0), HELD)
    skip = jnp.sum(jnp.where(lanes == held + HELD * b, skip_ref[...], 0.0), axis=1, keepdims=True)
    drain(pair, pair_recv)
    x = pair[:, 0].reshape(rows, ROWS)
    x_re, x_im = forward(x, *forward_tables)
    h_re, h_im = forward(pair[:, 1].reshape(rows, ROWS), *forward_tables)
    conv = inverse(x_re * h_re - x_im * h_im, x_re * h_im + x_im * h_re, *inverse_tables)
    with_skip = (conv + skip * x.astype(f32)).astype(bf16)
    for hand in range(2):
        mix_src[BLOCKS * hand : BLOCKS * (hand + 1)] = with_skip[:, rows * hand : rows * (hand + 1)].reshape(BLOCKS, HELD, ROWS // 2)

    def mix_copy(p, c):
        to = peer(p)
        hand = lax.rem(core + c, 2)
        return remote(
            mix_src.at[BLOCKS * hand + to], mix.at[core, b], mix_send, mix_recv, to, 2 * chip + hand
        )

    for p in ORDER:
        mix_copy(p, 0).start()
        mix_copy(p, 1).start()
    mix_copy(0, 1).start()
    bring(mix_src.at[BLOCKS * core + b], mix.at[core, b], mix_recv)

    odd = lax.rem(b, 2)
    target = (owner_ref[...] + odd * (1 - 2 * lax.rem(owner_ref[...], 2))) * send_rows + slot_ref[...] - b * send_rows
    target = jnp.concatenate([target[i : i + 1] for i in range(BLOCKS)], axis=1)
    places = lax.broadcasted_iota(jnp.int32, (BLOCKS * send_rows, ROWS), 0)
    chosen = jnp.where(places == target, 1.0, 0.0).astype(bf16)
    token = lax.broadcasted_iota(jnp.int32, (16, ROWS), 1)
    which = lax.broadcasted_iota(jnp.int32, (16, ROWS), 0)
    digits = jnp.where(which == 0, lax.rem(token, 128), jnp.where(which == 1, lax.div(token, 128) + 1, 0))
    digits = lax.dot_general(
        digits.astype(f32).astype(bf16), chosen, (((1,), (1,)), ((), ())), preferred_element_type=f32
    )
    origin = (digits[0:1] + 128.0 * digits[1:2]).astype(jnp.int32)
    map_src[...] = jnp.concatenate([origin[:, 128 * n : 128 * (n + 1)] for n in range(8)], axis=0)

    def map_copy(p):
        to = peer(p)
        return remote(map_src, maps.at[b], map_send, map_recv, to, k)

    for p in ORDER:
        map_copy(p).start()
    bring(map_src, maps.at[b], map_recv)

    for way in range(2):
        side_arrived(way, 1 - way)
        for c in range(2):
            acc[...] += near(2 * (left, right)[way] + c)

    def g_copy(p, c, s):
        to = peer(p)
        hand = lax.rem(core + c, 2)
        return remote(
            g_src.at[s, BLOCKS * hand + to], g_came.at[s, core, b], g_send.at[s], g_recv.at[s], to, 2 * chip + hand
        )

    for s in range(2):
        drain(og_all.at[pl.ds(2 * across, 2), s], far_recv.at[s])
        part = acc[:, 128 * s : 128 * (s + 1)]
        for c in range(2):
            part = part + term(2 * across + c, og_all[2 * across + c, s].reshape(128, ROWS))
        g_src[s] = part.astype(bf16).reshape(2 * BLOCKS, HELD, 128)
        for p in ORDER:
            g_copy(p, 0, s).start()
            g_copy(p, 1, s).start()
        g_copy(0, 1, s).start()
        bring(g_src.at[s, BLOCKS * core + b], g_came.at[s, core, b], g_recv.at[s])

    drain(mix, mix_recv)
    g_block = jnp.concatenate([g_src[s].reshape(2 * rows, 128) for s in range(2)], axis=1).astype(f32)
    gated = (g_block * mix[...].reshape(2 * rows, ROWS // 2).astype(f32)).astype(bf16).T
    for hand in range(2):
        gated_src[8 * hand : 8 * (hand + 1)] = gated[:, rows * hand : rows * (hand + 1)].reshape(8, ROWS // BLOCKS, rows)

    def gated_copy(q, c):
        column = lax.rem(b + q, 8)
        hand = lax.rem(core + c, 2)
        return remote(
            gated_src.at[8 * hand + column], gate_out.at[b],
            gated_send, gated_recv, 8 * core + column, 2 * chip + hand,
        )

    stays = lax.div(b, 8) == core
    own_gated = pltpu.make_async_copy(gated_src.at[8 * core + lax.rem(b, 8)], gate_out.at[b], gated_recv)
    for q in range(1, 8):
        gated_copy(q, 0).start()
        gated_copy(q, 1).start()
    gated_copy(0, 1).start()

    @pl.when(stays)
    def _():
        own_gated.start()

    @pl.when(jnp.logical_not(stays))
    def _():
        gated_copy(0, 0).start()

    drain(gate_came, gate_recv)
    for s in range(2):
        drain(g_came.at[s], g_recv.at[s])
    g = jnp.concatenate([g_came[s, h].reshape(rows, 128) for h in range(2) for s in range(2)], axis=1)
    g = g.astype(f32)
    dy = (g * gate_came[...].reshape(rows, ROWS).astype(f32)).astype(bf16)
    y_re, y_im = forward(dy, *forward_tables)

    def done_copy(p):
        to = peer(p)
        return remote(done.at[to], came.at[b], done_send, done_recv, to, k)

    lag = inverse(y_re * x_re + y_im * x_im, y_im * x_re - y_re * x_im, *inverse_tables)
    done[...] = to_columns(lag * (1.0 / math.sqrt(BLOCKS * ROWS))).astype(bf16).reshape(BLOCKS, HELD, ROWS)
    for p in ORDER:
        done_copy(p).start()
    bring(done.at[b], came.at[b], done_recv)
    grad = inverse(h_re * y_re + h_im * y_im, h_re * y_im - h_im * y_re, *inverse_tables)
    columns = to_columns(grad + skip * dy.astype(f32))
    drain(maps, map_recv)
    low_half = lax.broadcasted_iota(jnp.int32, (HELD, 128), 1) < 64
    for m in range(BLOCKS // 2):
        picked = []
        for j in (2 * m, 2 * m + 1):
            held = columns[j * HELD : (j + 1) * HELD]
            lane, tile = lax.rem(maps[j], 128), lax.div(maps[j], 128)
            tiles = []
            for n in range(8):
                at = jnp.broadcast_to(lane[n : n + 1], (HELD, 128))
                which = jnp.broadcast_to(tile[n : n + 1], (HELD, 128))
                value = jnp.zeros((HELD, 128), f32)
                for t in range(4):
                    found = jnp.take_along_axis(held[:, 128 * t : 128 * (t + 1)], at, axis=1)
                    value = jnp.where(which == t + 1, found, value)
                tiles.append(value)
            picked.append(tiles)
        for n in range(8):
            even, other = picked[0][n], picked[1][n]
            outbox[2 * n, :, 128 * m : 128 * (m + 1)] = jnp.where(low_half, even, other).astype(bf16)
            outbox[2 * n + 1, :, 128 * m : 128 * (m + 1)] = jnp.where(low_half, other, even).astype(bf16)

    def box_copy(p):
        to = peer(p)
        return remote(outbox.at[to], rows_out.at[b], box_send, box_recv, to, k)

    for p in ORDER:
        box_copy(p).start()
    bring(outbox.at[b], rows_out.at[b], box_recv)

    drain(came, done_recv)
    turned[...] = came[...].reshape(rows, ROWS).T
    result = bring(turned, filter_out)
    drain(og_all.at[0:2], far_send)
    drain(og_all.at[0:4], side_send)

    drain(gate_out, gated_recv)

    @pl.when(stays)
    def _():
        drain(gated_src.at[0:15], gated_send)

    @pl.when(jnp.logical_not(stays))
    def _():
        drain(gated_src, gated_send)

    few = BLOCKS - 1
    drain(pair_src.at[0:few], pair_send)
    drain(gate_src.at[0:few], gate_send)
    drain(mix_src.at[0 : BLOCKS + few], mix_send)
    for s in range(2):
        drain(g_src.at[s, 0 : BLOCKS + few], g_send.at[s])
    drain(maps.at[0:few], map_send)
    drain(done.at[0:few], done_send)
    drain(outbox.at[0:few], box_send)
    drain(rows_out, box_recv)
    result.wait()


ORDER = sorted(range(1, BLOCKS), key=lambda p: -(min(p // 4, 4 - p // 4) + min(p % 4, 4 - p % 4)))
TABLES = 6


def finish_kernel(gate_hbm, filter_hbm, rows_hbm, gate_out, filter_out, rows_out, gate, taps, wide, moved, ranked, sem):
    odd = lax.rem(lax.axis_index("bins"), 2)
    span = 256
    parts = rows_hbm.shape[1] // span
    reads = []

    def read(src, held):
        reads.append(pltpu.make_async_copy(src, held, sem.at[len(reads)]))
        reads[-1].start()
        return reads[-1]

    def write(held, dst, at):
        pltpu.make_async_copy(held, dst, sem.at[at]).start()

    taps_in = read(filter_hbm, taps)
    rows_in = [read(rows_hbm.at[:, pl.ds(n * span, span)], moved.at[n]) for n in range(parts)]
    gate_in = read(gate_hbm, gate)
    taps_in.wait()
    wide[...] = taps[...].astype(jnp.float32)
    write(wide, filter_out, 6)
    for n in range(parts):
        rows_in[n].wait()
        ranked[n] = moved[n].T.reshape(span // 64, 64, 256)
        for q in range(span // 64):
            group = n * (span // 64) + q
            group = group + odd * (1 - 2 * (q % 2))
            write(ranked.at[n, q], rows_out.at[pl.ds(group * 64, 64)], 7)
    gate_in.wait()
    write(gate, gate_out, 8)
    for ref, at in ((wide, 6), (ranked, 7), (gate, 8)):
        drain(ref, sem.at[at])


def finish(gate_grad, filter_grad, grad_rows):
    f32 = jnp.float32
    channels, count = grad_rows.shape
    return pl.pallas_call(
        finish_kernel,
        out_shape=(
            jax.ShapeDtypeStruct(gate_grad.shape, gate_grad.dtype),
            jax.ShapeDtypeStruct(filter_grad.shape, f32),
            jax.ShapeDtypeStruct((count, channels), grad_rows.dtype),
        ),
        in_specs=[pl.BlockSpec(memory_space=pl.ANY)] * 3,
        out_specs=(pl.BlockSpec(memory_space=pl.ANY),) * 3,
        scratch_shapes=[
            pltpu.VMEM(gate_grad.shape, gate_grad.dtype),
            pltpu.VMEM(filter_grad.shape, filter_grad.dtype),
            pltpu.VMEM(filter_grad.shape, f32),
            pltpu.VMEM((count // 256, channels, 256), grad_rows.dtype),
            pltpu.VMEM((count // 256, 4, 64, channels), grad_rows.dtype),
            pltpu.SemaphoreType.DMA((9,)),
        ],
        compiler_params=pltpu.CompilerParams(vmem_limit_bytes=67043328),
    )(gate_grad, filter_grad, grad_rows)


def shards(tokens_in, filters, gate, skip, out_grad, out_weight, owner, slot):
    channels = tokens_in.shape[1]
    send_rows = 2 * ROWS // BLOCKS
    half = ROWS // 2
    dma = pltpu.SemaphoreType.DMA
    one = dma(())
    hbm = pl.BlockSpec(memory_space=pl.ANY)
    f32, bf16 = jnp.float32, jnp.bfloat16
    constants = tables()
    operands = (
        tokens_in, filters, gate, skip.reshape(1, channels), out_grad.reshape(2, 2, 2, 64, ROWS), out_weight,
        owner, slot, *constants,
    )
    gate_grad, filter_grad, grad_rows = pl.pallas_call(
        kernel,
        out_shape=(
            jax.ShapeDtypeStruct((BLOCKS, ROWS // BLOCKS, channels), bf16),
            jax.ShapeDtypeStruct((ROWS, channels), bf16),
            jax.ShapeDtypeStruct((BLOCKS, HELD, BLOCKS * send_rows), bf16),
        ),
        in_specs=[hbm] * len(operands),
        out_specs=(hbm, hbm, hbm),
        scratch_shapes=[
            pltpu.VMEM((3, ROWS, channels), bf16),
            pltpu.VMEM((1, channels), f32),
            pltpu.VMEM(owner.shape, jnp.int32),
            pltpu.VMEM(slot.shape, jnp.int32),
            *(pltpu.VMEM(c.shape, c.dtype) for c in constants),
            pltpu.VMEM((2, channels, 8 * ROWS), bf16),
            pltpu.VMEM((8, 2, 2, 64, ROWS), bf16),
            pltpu.VMEM((2 * channels, half), f32),
            pltpu.VMEM((BLOCKS, 2, HELD, ROWS), bf16),
            pltpu.VMEM((BLOCKS, 2, HELD, ROWS), bf16),
            pltpu.VMEM((BLOCKS, HELD, ROWS), bf16),
            pltpu.VMEM((BLOCKS, HELD, ROWS), bf16),
            pltpu.VMEM((2 * BLOCKS, HELD, half), bf16),
            pltpu.VMEM((2, BLOCKS, HELD, half), bf16),
            pltpu.VMEM((2, 2 * BLOCKS, HELD, 128), bf16),
            pltpu.VMEM((2, 2, BLOCKS, HELD, 128), bf16),
            pltpu.VMEM((16, ROWS // BLOCKS, channels), bf16),
            pltpu.VMEM((BLOCKS, HELD, ROWS), bf16),
            pltpu.VMEM((BLOCKS, HELD, ROWS), bf16),
            pltpu.VMEM((BLOCKS, HELD, BLOCKS * send_rows), bf16),
            pltpu.VMEM((8, 128), jnp.int32),
            pltpu.VMEM((BLOCKS, 8, 128), jnp.int32),
            pltpu.VMEM((ROWS, channels), bf16),
            dma((15,)), dma((2,)), dma((2,)), one, dma((2, 2)), one, dma((2,)),
            one, one, one, one, one, one, dma((2,)), dma((2,)), one, one,
            one, one, one, one, one, one,
        ],
        compiler_params=pltpu.CompilerParams(
            collective_id=0, has_side_effects=True, vmem_limit_bytes=67043328
        ),
    )(*operands)
    gate_grad, filter_grad, grad_rows = finish(gate_grad, filter_grad, grad_rows.reshape(channels, -1))
    grid = (BLOCKS, ROWS // BLOCKS, channels)
    return (gate_grad, filter_grad.reshape(grid), grad_rows)


def solution(mesh):
    return jax.shard_map(
        shards,
        mesh=mesh,
        in_specs=(
            P("bins", "chan"),
            P("bins", "chan"),
            P("bins", "chan"),
            P("chan"),
            P("bins", "chan"),
            P("chan", None),
            P(None, "bins"),
            P(None, "bins"),
        ),
        out_specs=(P(None, "bins", "chan"), P(None, "bins", "chan"), P("bins", "chan")),
        check_vma=False,
    )
```

```python
import math

import jax
import jax.numpy as jnp
import numpy as np
from jax import lax
from jax.experimental import pallas as pl
from jax.experimental.pallas import tpu as pltpu
from jax.sharding import PartitionSpec as P

BLOCKS = 16
HELD = 16
ROWS = 512
HALF = BLOCKS + 1
LENGTH = 2 * BLOCKS * ROWS


def tables():
    k1 = np.arange(HALF)
    i = np.arange(BLOCKS)
    ang = 2.0 * np.pi * np.outer(k1, i) / (2 * BLOCKS)
    eye = np.eye(HELD)
    ahead = np.concatenate([np.kron(np.cos(ang), eye), np.kron(-np.sin(ang), eye)], axis=0)
    weight = np.where((k1 == 0) | (k1 == BLOCKS), 1.0, 2.0)[None, :] / LENGTH
    back_re = np.kron(weight * np.cos(ang).T, eye)
    back_im = np.kron(-(weight * np.sin(ang).T)[:, 1:BLOCKS], eye)
    back = np.concatenate([back_re, back_im], axis=1)
    r = np.arange(ROWS)
    twist = 2.0 * np.pi * np.outer(k1, r) / LENGTH
    inner = 2.0 * np.pi * (np.outer(r, r) % ROWS) / ROWS
    return (
        jnp.asarray(ahead, jnp.bfloat16),
        jnp.asarray(back, jnp.bfloat16),
        jnp.asarray(np.cos(twist)[:, None, :], jnp.float32),
        jnp.asarray(np.sin(twist)[:, None, :], jnp.float32),
        jnp.asarray(np.cos(inner), jnp.bfloat16),
        jnp.asarray(np.sin(inner), jnp.bfloat16),
    )


def mm(a, b):
    return jnp.dot(a, b, preferred_element_type=jnp.float32)


def stage_rows(value):
    return value.reshape(HALF, HELD, ROWS)


def flat(value):
    return value.reshape(HALF * HELD, ROWS)


def forward(value, ahead, tw_cos, tw_sin, in_cos, in_sin):
    part = mm(ahead, value)
    n = HALF * HELD
    re, im = stage_rows(part[:n]), stage_rows(part[n:])
    z_re = flat(re * tw_cos + im * tw_sin)
    z_im = flat(im * tw_cos - re * tw_sin)
    z = jnp.concatenate([z_re, z_im], axis=0).astype(jnp.bfloat16)
    by_cos, by_sin = mm(z, in_cos), mm(z, in_sin)
    return by_cos[:n] + by_sin[n:], by_cos[n:] - by_sin[:n]


def inverse(s_re, s_im, back, tw_cos, tw_sin, in_cos, in_sin):
    n = HALF * HELD
    q = jnp.concatenate([s_re, s_im], axis=0).astype(jnp.bfloat16)
    by_cos, by_sin = mm(q, in_cos), mm(q, in_sin)
    re, im = stage_rows(by_cos[:n] - by_sin[n:]), stage_rows(by_cos[n:] + by_sin[:n])
    t_re = flat(re * tw_cos - im * tw_sin)
    t_im = flat(im * tw_cos + re * tw_sin)[HELD : BLOCKS * HELD]
    t = jnp.concatenate([t_re, t_im], axis=0).astype(jnp.bfloat16)
    return mm(back, t)


def to_columns(value):
    group = lax.broadcasted_iota(jnp.int32, (HELD, 128), 1) // 32
    out = [[None] * 4 for _ in range(BLOCKS)]
    for i_hi in range(4):
        for j_hi in range(4):
            tiles = [
                value[(4 * i_hi + i_lo) * HELD : (4 * i_hi + i_lo + 1) * HELD, 128 * j_hi : 128 * (j_hi + 1)]
                for i_lo in range(4)
            ]
            for j_lo in range(4):
                acc = None
                for i_lo in range(4):
                    shift = (32 * (i_lo - j_lo)) % 128
                    turned = pltpu.roll(tiles[i_lo], shift, 1) if shift else tiles[i_lo]
                    acc = turned if acc is None else jnp.where(group == i_lo, turned, acc)
                out[4 * j_hi + j_lo][i_hi] = acc
    return jnp.concatenate([jnp.concatenate(row, axis=1) for row in out], axis=0)


def remote(src, dst, send, recv, bins, chan):
    return pltpu.make_async_remote_copy(
        src_ref=src,
        dst_ref=dst,
        send_sem=send,
        recv_sem=recv,
        device_id=(bins, chan),
        device_id_type=pl.DeviceIdType.MESH,
    )


def drain(ref, sem):
    pltpu.make_async_copy(ref, ref, sem).wait()


def kernel(
    x_hbm, h_hbm, gate_hbm, skip_hbm, og_hbm, w_hbm, owner_hbm, slot_hbm, *rest
):
    tables_hbm, rest = rest[:TABLES], rest[TABLES:]
    gate_out, filter_out, rows_out = rest[:3]
    (
        raw, skip_ref, owner_ref, slot_ref, *rest
    ) = rest[3:]
    tables_ref, rest = rest[:TABLES], rest[TABLES:]
    (
        w_all, og_all, acc, pair_src, pair, gate_src, gate_came, mix_src, mix, g_src, g_came, gated_src,
        done, came, outbox, map_src, maps, turned,
        local_sem, w_sem, mate_sem, side_send, side_recv, far_send, far_recv,
        pair_send, pair_recv, gate_send, gate_recv, mix_send, mix_recv, g_send, g_recv, gated_send, gated_recv,
        done_send, done_recv, box_send, box_recv, map_send, map_recv,
    ) = rest
    f32, bf16 = jnp.float32, jnp.bfloat16
    rows = BLOCKS * HELD
    send_rows = 2 * ROWS // BLOCKS
    b = lax.axis_index("bins")
    k = lax.axis_index("chan")
    b_y, b_z = lax.div(b, 4), lax.rem(b, 4)
    chip, core = lax.div(k, 2), lax.rem(k, 2)
    right, left, across = lax.rem(chip + 1, 4), lax.rem(chip + 3, 4), lax.rem(chip + 2, 4)
    mate = 2 * chip + 1 - core

    along_y = [4 * lax.rem(b_y + n, 4) for n in range(4)]
    along_z = [lax.rem(b_z + n, 4) for n in range(4)]

    def peer(p):
        return along_y[p // 4] + along_z[p % 4]

    barrier = pltpu.get_barrier_semaphore()

    def greet(bins, chan):
        pl.semaphore_signal(barrier, inc=1, device_id=(bins, chan), device_id_type=pl.DeviceIdType.MESH)

    for p in ORDER:
        greet(peer(p), k)
        greet(peer(p), mate)
    greet(b, mate)
    for side in (right, left):
        for c in range(2):
            greet(b, 2 * side + c)

    local = []

    def bring(src, dst, sem=None):
        copy = pltpu.make_async_copy(src, dst, local_sem.at[len(local)] if sem is None else sem)
        copy.start()
        if sem is None:
            local.append(copy)
        return copy

    own_raw = [bring(ref, raw.at[n]) for n, ref in enumerate((x_hbm, h_hbm, gate_hbm))]
    own_og = bring(og_hbm.at[core], og_all.at[k])
    own_w = bring(w_hbm, w_all.at[core])
    own_small = [bring(*pair) for pair in ((skip_hbm, skip_ref), (owner_hbm, owner_ref), (slot_hbm, slot_ref))]
    own_tables = [bring(*pair) for pair in zip(tables_hbm, tables_ref)]

    pl.semaphore_wait(barrier, 2 * BLOCKS - 1 + 4)

    def side_copy(way, part, c):
        to = (right, left)[way]
        return remote(
            og_hbm.at[c, :, part], og_all.at[k, :, part],
            side_send, side_recv.at[way, part], b, 2 * to + c,
        )

    for turn in range(2):
        for c in range(2):
            side_copy(0, turn, c).start()
            side_copy(1, 1 - turn, c).start()
    mate_og = remote(og_hbm.at[1 - core], og_all.at[k], mate_sem.at[0], mate_sem.at[1], b, mate)
    mate_og.start()
    mate_w = remote(w_hbm, w_all.at[core], w_sem.at[0], w_sem.at[1], b, mate)
    mate_w.start()

    for n in range(2):
        own_raw[n].wait()
        pair_src[:, n] = raw[n].T.reshape(BLOCKS, HELD, ROWS)

    def pair_copy(p):
        to = peer(p)
        return remote(pair_src.at[to], pair.at[b], pair_send, pair_recv, to, k)

    for p in ORDER:
        pair_copy(p).start()
    bring(pair_src.at[b], pair.at[b], pair_recv)
    own_raw[2].wait()
    gate_src[...] = raw[2].T.reshape(BLOCKS, HELD, ROWS)

    def gate_copy(p):
        to = peer(p)
        return remote(gate_src.at[to], gate_came.at[b], gate_send, gate_recv, to, k)

    for p in ORDER:
        gate_copy(p).start()
    bring(gate_src.at[b], gate_came.at[b], gate_recv)

    def side_arrived(way, part):
        src = 2 * (left, right)[way]
        drain(og_all.at[pl.ds(src, 2), :, part], side_recv.at[way, part])

    def far_copy(way, c, s):
        src = 2 * (left, right)[way] + c
        to = (right, left)[way]
        return remote(
            og_all.at[src, s, way], og_all.at[src, s, way],
            far_send, far_recv.at[s, c], b, 2 * to + core,
        )

    for way in range(2):
        side_arrived(way, way)
    for s in range(2):
        for c in range(2):
            for way in range(2):
                far_copy(way, c, s).start()

    def term(source, tokens):
        columns = pl.ds(pl.multiple_of(source * ROWS, ROWS), ROWS)
        weights = w_all[:, :, columns].reshape(2 * rows, ROWS)
        return lax.dot_general(weights, tokens, (((1,), (1,)), ((), ())), preferred_element_type=f32)

    def near(source):
        return term(source, og_all[source].reshape(ROWS // 2, ROWS))

    own_w.wait()
    own_og.wait()
    mate_w.wait()
    mate_og.wait()
    acc[...] = near(k) + near(mate)

    for copy in own_small + own_tables:
        copy.wait()
    ahead, back, tw_cos, tw_sin, in_cos, in_sin = (ref[...] for ref in tables_ref)
    forward_tables = (ahead, tw_cos, tw_sin, in_cos, in_sin)
    inverse_tables = (back, tw_cos, tw_sin, in_cos, in_sin)
    lanes = lax.broadcasted_iota(jnp.int32, (rows, rows), 1)
    held = lax.rem(lax.broadcasted_iota(jnp.int32, (rows, rows), 0), HELD)
    skip = jnp.sum(jnp.where(lanes == held + HELD * b, skip_ref[...], 0.0), axis=1, keepdims=True)
    drain(pair, pair_recv)
    x = pair[:, 0].reshape(rows, ROWS)
    x_re, x_im = forward(x, *forward_tables)
    h_re, h_im = forward(pair[:, 1].reshape(rows, ROWS), *forward_tables)
    conv = inverse(x_re * h_re - x_im * h_im, x_re * h_im + x_im * h_re, *inverse_tables)
    with_skip = (conv + skip * x.astype(f32)).astype(bf16)
    for hand in range(2):
        mix_src[BLOCKS * hand : BLOCKS * (hand + 1)] = with_skip[:, rows * hand : rows * (hand + 1)].reshape(BLOCKS, HELD, ROWS // 2)

    def mix_copy(p, c):
        to = peer(p)
        hand = lax.rem(core + c, 2)
        return remote(
            mix_src.at[BLOCKS * hand + to], mix.at[core, b], mix_send, mix_recv, to, 2 * chip + hand
        )

    for p in ORDER:
        mix_copy(p, 0).start()
        mix_copy(p, 1).start()
    mix_copy(0, 1).start()
    bring(mix_src.at[BLOCKS * core + b], mix.at[core, b], mix_recv)

    odd = lax.rem(b, 2)
    target = (owner_ref[...] + odd * (1 - 2 * lax.rem(owner_ref[...], 2))) * send_rows + slot_ref[...] - b * send_rows
    target = jnp.concatenate([target[i : i + 1] for i in range(BLOCKS)], axis=1)
    places = lax.broadcasted_iota(jnp.int32, (BLOCKS * send_rows, ROWS), 0)
    chosen = jnp.where(places == target, 1.0, 0.0).astype(bf16)
    token = lax.broadcasted_iota(jnp.int32, (16, ROWS), 1)
    which = lax.broadcasted_iota(jnp.int32, (16, ROWS), 0)
    digits = jnp.where(which == 0, lax.rem(token, 128), jnp.where(which == 1, lax.div(token, 128) + 1, 0))
    digits = lax.dot_general(
        digits.astype(f32).astype(bf16), chosen, (((1,), (1,)), ((), ())), preferred_element_type=f32
    )
    origin = (digits[0:1] + 128.0 * digits[1:2]).astype(jnp.int32)
    map_src[...] = jnp.concatenate([origin[:, 128 * n : 128 * (n + 1)] for n in range(8)], axis=0)

    def map_copy(p):
        to = peer(p)
        return remote(map_src, maps.at[b], map_send, map_recv, to, k)

    for p in ORDER:
        map_copy(p).start()
    bring(map_src, maps.at[b], map_recv)

    for way in range(2):
        side_arrived(way, 1 - way)
        for c in range(2):
            acc[...] += near(2 * (left, right)[way] + c)

    def g_copy(p, c, s):
        to = peer(p)
        hand = lax.rem(core + c, 2)
        return remote(
            g_src.at[s, BLOCKS * hand + to], g_came.at[s, core, b], g_send.at[s], g_recv.at[s], to, 2 * chip + hand
        )

    for s in range(2):
        part = acc[:, 128 * s : 128 * (s + 1)]
        for c in range(2):
            drain(og_all.at[2 * across + c, s], far_recv.at[s, c])
            part = part + term(2 * across + c, og_all[2 * across + c, s].reshape(128, ROWS))
        g_src[s] = part.astype(bf16).reshape(2 * BLOCKS, HELD, 128)
        for p in ORDER:
            g_copy(p, 0, s).start()
            g_copy(p, 1, s).start()
        g_copy(0, 1, s).start()
        bring(g_src.at[s, BLOCKS * core + b], g_came.at[s, core, b], g_recv.at[s])

    drain(mix, mix_recv)
    g_block = jnp.concatenate([g_src[s].reshape(2 * rows, 128) for s in range(2)], axis=1).astype(f32)
    gated = (g_block * mix[...].reshape(2 * rows, ROWS // 2).astype(f32)).astype(bf16).T
    for hand in range(2):
        gated_src[8 * hand : 8 * (hand + 1)] = gated[:, rows * hand : rows * (hand + 1)].reshape(8, ROWS // BLOCKS, rows)

    def gated_copy(q, c):
        column = lax.rem(b + q, 8)
        hand = lax.rem(core + c, 2)
        return remote(
            gated_src.at[8 * hand + column], gate_out.at[b],
            gated_send, gated_recv, 8 * core + column, 2 * chip + hand,
        )

    stays = lax.div(b, 8) == core
    own_gated = pltpu.make_async_copy(gated_src.at[8 * core + lax.rem(b, 8)], gate_out.at[b], gated_recv)
    for q in range(1, 8):
        gated_copy(q, 0).start()

    @pl.when(stays)
    def _():
        own_gated.start()

    @pl.when(jnp.logical_not(stays))
    def _():
        gated_copy(0, 0).start()

    drain(gate_came, gate_recv)
    for s in range(2):
        drain(g_came.at[s], g_recv.at[s])
    for q in range(8):
        gated_copy(q, 1).start()
    g = jnp.concatenate([g_came[s, h].reshape(rows, 128) for h in range(2) for s in range(2)], axis=1)
    g = g.astype(f32)
    dy = (g * gate_came[...].reshape(rows, ROWS).astype(f32)).astype(bf16)
    y_re, y_im = forward(dy, *forward_tables)

    def done_copy(p):
        to = peer(p)
        return remote(done.at[to], came.at[b], done_send, done_recv, to, k)

    lag = inverse(y_re * x_re + y_im * x_im, y_im * x_re - y_re * x_im, *inverse_tables)
    done[...] = to_columns(lag * (1.0 / math.sqrt(BLOCKS * ROWS))).astype(bf16).reshape(BLOCKS, HELD, ROWS)
    for p in ORDER:
        done_copy(p).start()
    bring(done.at[b], came.at[b], done_recv)
    grad = inverse(h_re * y_re + h_im * y_im, h_re * y_im - h_im * y_re, *inverse_tables)
    columns = to_columns(grad + skip * dy.astype(f32))
    drain(maps, map_recv)
    low_half = lax.broadcasted_iota(jnp.int32, (HELD, 128), 1) < 64
    for m in range(BLOCKS // 2):
        picked = []
        for j in (2 * m, 2 * m + 1):
            held = columns[j * HELD : (j + 1) * HELD]
            lane, tile = lax.rem(maps[j], 128), lax.div(maps[j], 128)
            tiles = []
            for n in range(8):
                at = jnp.broadcast_to(lane[n : n + 1], (HELD, 128))
                which = jnp.broadcast_to(tile[n : n + 1], (HELD, 128))
                value = jnp.zeros((HELD, 128), f32)
                for t in range(4):
                    found = jnp.take_along_axis(held[:, 128 * t : 128 * (t + 1)], at, axis=1)
                    value = jnp.where(which == t + 1, found, value)
                tiles.append(value)
            picked.append(tiles)
        for n in range(8):
            even, other = picked[0][n], picked[1][n]
            outbox[2 * n, :, 128 * m : 128 * (m + 1)] = jnp.where(low_half, even, other).astype(bf16)
            outbox[2 * n + 1, :, 128 * m : 128 * (m + 1)] = jnp.where(low_half, other, even).astype(bf16)

    def box_copy(p):
        to = peer(p)
        return remote(outbox.at[to], rows_out.at[b], box_send, box_recv, to, k)

    for p in ORDER:
        box_copy(p).start()
    bring(outbox.at[b], rows_out.at[b], box_recv)

    drain(came, done_recv)
    turned[...] = came[...].reshape(rows, ROWS).T
    result = bring(turned, filter_out)
    drain(og_all.at[0:2], far_send)
    drain(og_all.at[0:4], side_send)

    drain(gate_out, gated_recv)

    @pl.when(stays)
    def _():
        drain(gated_src.at[0:15], gated_send)

    @pl.when(jnp.logical_not(stays))
    def _():
        drain(gated_src, gated_send)

    few = BLOCKS - 1
    drain(pair_src.at[0:few], pair_send)
    drain(gate_src.at[0:few], gate_send)
    drain(mix_src.at[0 : BLOCKS + few], mix_send)
    for s in range(2):
        drain(g_src.at[s, 0 : BLOCKS + few], g_send.at[s])
    drain(maps.at[0:few], map_send)
    drain(done.at[0:few], done_send)
    drain(outbox.at[0:few], box_send)
    drain(rows_out, box_recv)
    result.wait()


ORDER = sorted(range(1, BLOCKS), key=lambda p: -(min(p // 4, 4 - p // 4) + min(p % 4, 4 - p % 4)))
TABLES = 6


def finish_kernel(gate_hbm, filter_hbm, rows_hbm, gate_out, filter_out, rows_out, gate, taps, wide, moved, ranked, sem):
    odd = lax.rem(lax.axis_index("bins"), 2)
    span = 256
    parts = rows_hbm.shape[1] // span
    reads = []

    def read(src, held):
        reads.append(pltpu.make_async_copy(src, held, sem.at[len(reads)]))
        reads[-1].start()
        return reads[-1]

    def write(held, dst, at):
        pltpu.make_async_copy(held, dst, sem.at[at]).start()

    taps_in = read(filter_hbm, taps)
    rows_in = [read(rows_hbm.at[:, pl.ds(n * span, span)], moved.at[n]) for n in range(parts)]
    gate_in = read(gate_hbm, gate)
    taps_in.wait()
    wide[...] = taps[...].astype(jnp.float32)
    write(wide, filter_out, 6)
    for n in range(parts):
        rows_in[n].wait()
        ranked[n] = moved[n].T.reshape(span // 64, 64, 256)
        for q in range(span // 64):
            group = n * (span // 64) + q
            group = group + odd * (1 - 2 * (q % 2))
            write(ranked.at[n, q], rows_out.at[pl.ds(group * 64, 64)], 7)
    gate_in.wait()
    write(gate, gate_out, 8)
    for ref, at in ((wide, 6), (ranked, 7), (gate, 8)):
        drain(ref, sem.at[at])


def finish(gate_grad, filter_grad, grad_rows):
    f32 = jnp.float32
    channels, count = grad_rows.shape
    return pl.pallas_call(
        finish_kernel,
        out_shape=(
            jax.ShapeDtypeStruct(gate_grad.shape, gate_grad.dtype),
            jax.ShapeDtypeStruct(filter_grad.shape, f32),
            jax.ShapeDtypeStruct((count, channels), grad_rows.dtype),
        ),
        in_specs=[pl.BlockSpec(memory_space=pl.ANY)] * 3,
        out_specs=(pl.BlockSpec(memory_space=pl.ANY),) * 3,
        scratch_shapes=[
            pltpu.VMEM(gate_grad.shape, gate_grad.dtype),
            pltpu.VMEM(filter_grad.shape, filter_grad.dtype),
            pltpu.VMEM(filter_grad.shape, f32),
            pltpu.VMEM((count // 256, channels, 256), grad_rows.dtype),
            pltpu.VMEM((count // 256, 4, 64, channels), grad_rows.dtype),
            pltpu.SemaphoreType.DMA((9,)),
        ],
        compiler_params=pltpu.CompilerParams(vmem_limit_bytes=67043328),
    )(gate_grad, filter_grad, grad_rows)


def shards(tokens_in, filters, gate, skip, out_grad, out_weight, owner, slot):
    channels = tokens_in.shape[1]
    send_rows = 2 * ROWS // BLOCKS
    half = ROWS // 2
    dma = pltpu.SemaphoreType.DMA
    one = dma(())
    hbm = pl.BlockSpec(memory_space=pl.ANY)
    f32, bf16 = jnp.float32, jnp.bfloat16
    constants = tables()
    operands = (
        tokens_in, filters, gate, skip.reshape(1, channels), out_grad.reshape(2, 2, 2, 64, ROWS), out_weight,
        owner, slot, *constants,
    )
    gate_grad, filter_grad, grad_rows = pl.pallas_call(
        kernel,
        out_shape=(
            jax.ShapeDtypeStruct((BLOCKS, ROWS // BLOCKS, channels), bf16),
            jax.ShapeDtypeStruct((ROWS, channels), bf16),
            jax.ShapeDtypeStruct((BLOCKS, HELD, BLOCKS * send_rows), bf16),
        ),
        in_specs=[hbm] * len(operands),
        out_specs=(hbm, hbm, hbm),
        scratch_shapes=[
            pltpu.VMEM((3, ROWS, channels), bf16),
            pltpu.VMEM((1, channels), f32),
            pltpu.VMEM(owner.shape, jnp.int32),
            pltpu.VMEM(slot.shape, jnp.int32),
            *(pltpu.VMEM(c.shape, c.dtype) for c in constants),
            pltpu.VMEM((2, channels, 8 * ROWS), bf16),
            pltpu.VMEM((8, 2, 2, 64, ROWS), bf16),
            pltpu.VMEM((2 * channels, half), f32),
            pltpu.VMEM((BLOCKS, 2, HELD, ROWS), bf16),
            pltpu.VMEM((BLOCKS, 2, HELD, ROWS), bf16),
            pltpu.VMEM((BLOCKS, HELD, ROWS), bf16),
            pltpu.VMEM((BLOCKS, HELD, ROWS), bf16),
            pltpu.VMEM((2 * BLOCKS, HELD, half), bf16),
            pltpu.VMEM((2, BLOCKS, HELD, half), bf16),
            pltpu.VMEM((2, 2 * BLOCKS, HELD, 128), bf16),
            pltpu.VMEM((2, 2, BLOCKS, HELD, 128), bf16),
            pltpu.VMEM((16, ROWS // BLOCKS, channels), bf16),
            pltpu.VMEM((BLOCKS, HELD, ROWS), bf16),
            pltpu.VMEM((BLOCKS, HELD, ROWS), bf16),
            pltpu.VMEM((BLOCKS, HELD, BLOCKS * send_rows), bf16),
            pltpu.VMEM((8, 128), jnp.int32),
            pltpu.VMEM((BLOCKS, 8, 128), jnp.int32),
            pltpu.VMEM((ROWS, channels), bf16),
            dma((15,)), dma((2,)), dma((2,)), one, dma((2, 2)), one, dma((2, 2)),
            one, one, one, one, one, one, dma((2,)), dma((2,)), one, one,
            one, one, one, one, one, one,
        ],
        compiler_params=pltpu.CompilerParams(
            collective_id=0, has_side_effects=True, vmem_limit_bytes=67043328
        ),
    )(*operands)
    gate_grad, filter_grad, grad_rows = finish(gate_grad, filter_grad, grad_rows.reshape(channels, -1))
    grid = (BLOCKS, ROWS // BLOCKS, channels)
    return (gate_grad, filter_grad.reshape(grid), grad_rows)


def solution(mesh):
    return jax.shard_map(
        shards,
        mesh=mesh,
        in_specs=(
            P("bins", "chan"),
            P("bins", "chan"),
            P("bins", "chan"),
            P("chan"),
            P("bins", "chan"),
            P("chan", None),
            P(None, "bins"),
            P(None, "bins"),
        ),
        out_specs=(P(None, "bins", "chan"), P(None, "bins", "chan"), P("bins", "chan")),
        check_vma=False,
    )
```

```python
import math

import jax
import jax.numpy as jnp
import numpy as np
from jax import lax
from jax.experimental import pallas as pl
from jax.experimental.pallas import tpu as pltpu
from jax.sharding import PartitionSpec as P

BLOCKS = 16
HELD = 16
ROWS = 512
HALF = BLOCKS + 1
LENGTH = 2 * BLOCKS * ROWS


def tables():
    k1 = np.arange(HALF)
    i = np.arange(BLOCKS)
    ang = 2.0 * np.pi * np.outer(k1, i) / (2 * BLOCKS)
    eye = np.eye(HELD)
    ahead = np.concatenate([np.kron(np.cos(ang), eye), np.kron(-np.sin(ang), eye)], axis=0)
    weight = np.where((k1 == 0) | (k1 == BLOCKS), 1.0, 2.0)[None, :] / LENGTH
    back_re = np.kron(weight * np.cos(ang).T, eye)
    back_im = np.kron(-(weight * np.sin(ang).T)[:, 1:BLOCKS], eye)
    back = np.concatenate([back_re, back_im], axis=1)
    r = np.arange(ROWS)
    twist = 2.0 * np.pi * np.outer(k1, r) / LENGTH
    m = np.arange(ROWS // 2)
    fold = 2.0 * np.pi * m[None, :] / ROWS
    inner = 2.0 * np.pi * (np.outer(m, m) % (ROWS // 2)) / (ROWS // 2)
    return (
        jnp.asarray(ahead, jnp.bfloat16),
        jnp.asarray(back, jnp.bfloat16),
        jnp.asarray(np.cos(twist)[:, None, :], jnp.float32),
        jnp.asarray(np.sin(twist)[:, None, :], jnp.float32),
        jnp.asarray(np.cos(fold), jnp.float32),
        jnp.asarray(np.sin(fold), jnp.float32),
        jnp.asarray(np.block([[np.cos(inner), -np.sin(inner)], [np.sin(inner), np.cos(inner)]]), jnp.bfloat16),
        jnp.asarray(np.block([[np.cos(inner), np.sin(inner)], [-np.sin(inner), np.cos(inner)]]), jnp.bfloat16),
    )


def mm(a, b):
    return jnp.dot(a, b, preferred_element_type=jnp.float32)


def stage_rows(value):
    return value.reshape(HALF, HELD, ROWS)


def flat(value):
    return value.reshape(HALF * HELD, ROWS)


def forward(value, ahead, tw_cos, tw_sin, fold_cos, fold_sin, inner, inner_back):
    part = mm(ahead, value)
    n = HALF * HELD
    half = ROWS // 2
    re, im = stage_rows(part[:n]), stage_rows(part[n:])
    z_re = flat(re * tw_cos + im * tw_sin)
    z_im = flat(im * tw_cos - re * tw_sin)
    diff_re, diff_im = z_re[:, :half] - z_re[:, half:], z_im[:, :half] - z_im[:, half:]
    even = jnp.concatenate([z_re[:, :half] + z_re[:, half:], z_im[:, :half] + z_im[:, half:]], axis=1)
    odd = jnp.concatenate(
        [diff_re * fold_cos + diff_im * fold_sin, diff_im * fold_cos - diff_re * fold_sin], axis=1
    )
    bins = mm(jnp.concatenate([even, odd], axis=0).astype(jnp.bfloat16), inner)
    return bins[:, :half], bins[:, half:]


def inverse(s_re, s_im, back, tw_cos, tw_sin, fold_cos, fold_sin, inner, inner_back):
    n = HALF * HELD
    half = ROWS // 2
    q = mm(jnp.concatenate([s_re, s_im], axis=1).astype(jnp.bfloat16), inner_back)
    re, im = q[:, :half], q[:, half:]
    odd_re = re[n:] * fold_cos - im[n:] * fold_sin
    odd_im = im[n:] * fold_cos + re[n:] * fold_sin
    re = stage_rows(jnp.concatenate([re[:n] + odd_re, re[:n] - odd_re], axis=1))
    im = stage_rows(jnp.concatenate([im[:n] + odd_im, im[:n] - odd_im], axis=1))
    t_re = flat(re * tw_cos - im * tw_sin)
    t_im = flat(im * tw_cos + re * tw_sin)[HELD : BLOCKS * HELD]
    t = jnp.concatenate([t_re, t_im], axis=0).astype(jnp.bfloat16)
    return mm(back, t)


def to_columns(value):
    group = lax.broadcasted_iota(jnp.int32, (HELD, 128), 1) // 32
    out = [[None] * 4 for _ in range(BLOCKS)]
    for i_hi in range(4):
        for j_hi in range(4):
            tiles = [
                value[(4 * i_hi + i_lo) * HELD : (4 * i_hi + i_lo + 1) * HELD, 128 * j_hi : 128 * (j_hi + 1)]
                for i_lo in range(4)
            ]
            for j_lo in range(4):
                acc = None
                for i_lo in range(4):
                    shift = (32 * (i_lo - j_lo)) % 128
                    turned = pltpu.roll(tiles[i_lo], shift, 1) if shift else tiles[i_lo]
                    acc = turned if acc is None else jnp.where(group == i_lo, turned, acc)
                out[4 * j_hi + j_lo][i_hi] = acc
    return jnp.concatenate([jnp.concatenate(row, axis=1) for row in out], axis=0)


def remote(src, dst, send, recv, bins, chan):
    return pltpu.make_async_remote_copy(
        src_ref=src,
        dst_ref=dst,
        send_sem=send,
        recv_sem=recv,
        device_id=(bins, chan),
        device_id_type=pl.DeviceIdType.MESH,
    )


def drain(ref, sem):
    pltpu.make_async_copy(ref, ref, sem).wait()


def kernel(
    x_hbm, h_hbm, gate_hbm, skip_hbm, og_hbm, w_hbm, owner_hbm, slot_hbm, *rest
):
    tables_hbm, rest = rest[:TABLES], rest[TABLES:]
    gate_out, filter_out, rows_out = rest[:3]
    (
        raw, skip_ref, owner_ref, slot_ref, *rest
    ) = rest[3:]
    tables_ref, rest = rest[:TABLES], rest[TABLES:]
    (
        w_all, og_all, acc, pair_src, pair, gate_src, gate_came, mix_src, mix, g_src, g_came, gated_src,
        done, came, outbox, map_src, maps, turned,
        local_sem, w_sem, mate_sem, side_send, side_recv, far_send, far_recv,
        pair_send, pair_recv, gate_send, gate_recv, mix_send, mix_recv, g_send, g_recv, gated_send, gated_recv,
        done_send, done_recv, box_send, box_recv, map_send, map_recv,
    ) = rest
    f32, bf16 = jnp.float32, jnp.bfloat16
    rows = BLOCKS * HELD
    send_rows = 2 * ROWS // BLOCKS
    b = lax.axis_index("bins")
    k = lax.axis_index("chan")
    b_y, b_z = lax.div(b, 4), lax.rem(b, 4)
    chip, core = lax.div(k, 2), lax.rem(k, 2)
    right, left, across = lax.rem(chip + 1, 4), lax.rem(chip + 3, 4), lax.rem(chip + 2, 4)
    mate = 2 * chip + 1 - core

    along_y = [4 * lax.rem(b_y + n, 4) for n in range(4)]
    along_z = [lax.rem(b_z + n, 4) for n in range(4)]

    def peer(p):
        return along_y[p // 4] + along_z[p % 4]

    barrier = pltpu.get_barrier_semaphore()

    def greet(bins, chan):
        pl.semaphore_signal(barrier, inc=1, device_id=(bins, chan), device_id_type=pl.DeviceIdType.MESH)

    for p in ORDER:
        greet(peer(p), k)
        greet(peer(p), mate)
    greet(b, mate)
    for side in (right, left):
        for c in range(2):
            greet(b, 2 * side + c)

    local = []

    def bring(src, dst, sem=None):
        copy = pltpu.make_async_copy(src, dst, local_sem.at[len(local)] if sem is None else sem)
        copy.start()
        if sem is None:
            local.append(copy)
        return copy

    own_raw = [bring(ref, raw.at[n]) for n, ref in enumerate((x_hbm, h_hbm, gate_hbm))]
    own_og = bring(og_hbm.at[core], og_all.at[k])
    own_w = bring(w_hbm, w_all.at[core])
    own_small = [bring(*pair) for pair in ((skip_hbm, skip_ref), (owner_hbm, owner_ref), (slot_hbm, slot_ref))]
    own_tables = [bring(*pair) for pair in zip(tables_hbm, tables_ref)]

    pl.semaphore_wait(barrier, 2 * BLOCKS - 1 + 4)

    def side_copy(way, part, c):
        to = (right, left)[way]
        return remote(
            og_hbm.at[c, :, part], og_all.at[k, :, part],
            side_send, side_recv.at[way, part], b, 2 * to + c,
        )

    for turn in range(2):
        for c in range(2):
            side_copy(0, turn, c).start()
            side_copy(1, 1 - turn, c).start()
    mate_og = remote(og_hbm.at[1 - core], og_all.at[k], mate_sem.at[0], mate_sem.at[1], b, mate)
    mate_og.start()
    mate_w = remote(w_hbm, w_all.at[core], w_sem.at[0], w_sem.at[1], b, mate)
    mate_w.start()

    for n in range(2):
        own_raw[n].wait()
        pair_src[:, n] = raw[n].T.reshape(BLOCKS, HELD, ROWS)

    def pair_copy(p):
        to = peer(p)
        return remote(pair_src.at[to], pair.at[b], pair_send, pair_recv, to, k)

    for p in ORDER:
        pair_copy(p).start()
    bring(pair_src.at[b], pair.at[b], pair_recv)
    own_raw[2].wait()
    gate_src[...] = raw[2].T.reshape(BLOCKS, HELD, ROWS)

    def gate_copy(p):
        to = peer(p)
        return remote(gate_src.at[to], gate_came.at[b], gate_send, gate_recv, to, k)

    for p in ORDER:
        gate_copy(p).start()
    bring(gate_src.at[b], gate_came.at[b], gate_recv)

    def side_arrived(way, part):
        src = 2 * (left, right)[way]
        drain(og_all.at[pl.ds(src, 2), :, part], side_recv.at[way, part])

    def far_copy(way, c, s):
        src = 2 * (left, right)[way] + c
        to = (right, left)[way]
        return remote(
            og_all.at[src, s, way], og_all.at[src, s, way],
            far_send, far_recv.at[s, c], b, 2 * to + core,
        )

    for way in range(2):
        side_arrived(way, way)
    for s in range(2):
        for c in range(2):
            for way in range(2):
                far_copy(way, c, s).start()

    def term(source, tokens):
        columns = pl.ds(pl.multiple_of(source * ROWS, ROWS), ROWS)
        weights = w_all[:, :, columns].reshape(2 * rows, ROWS)
        return lax.dot_general(weights, tokens, (((1,), (1,)), ((), ())), preferred_element_type=f32)

    def near(source):
        return term(source, og_all[source].reshape(ROWS // 2, ROWS))

    own_w.wait()
    own_og.wait()
    mate_w.wait()
    mate_og.wait()
    acc[...] = near(k) + near(mate)

    for copy in own_small + own_tables:
        copy.wait()
    ahead, back, *shared = (ref[...] for ref in tables_ref)
    forward_tables, inverse_tables = (ahead, *shared), (back, *shared)
    lanes = lax.broadcasted_iota(jnp.int32, (rows, rows), 1)
    held = lax.rem(lax.broadcasted_iota(jnp.int32, (rows, rows), 0), HELD)
    skip = jnp.sum(jnp.where(lanes == held + HELD * b, skip_ref[...], 0.0), axis=1, keepdims=True)
    drain(pair, pair_recv)
    x = pair[:, 0].reshape(rows, ROWS)
    x_re, x_im = forward(x, *forward_tables)
    h_re, h_im = forward(pair[:, 1].reshape(rows, ROWS), *forward_tables)
    conv = inverse(x_re * h_re - x_im * h_im, x_re * h_im + x_im * h_re, *inverse_tables)
    with_skip = (conv + skip * x.astype(f32)).astype(bf16)
    for hand in range(2):
        mix_src[BLOCKS * hand : BLOCKS * (hand + 1)] = with_skip[:, rows * hand : rows * (hand + 1)].reshape(BLOCKS, HELD, ROWS // 2)

    def mix_copy(p, c):
        to = peer(p)
        hand = lax.rem(core + c, 2)
        return remote(
            mix_src.at[BLOCKS * hand + to], mix.at[core, b], mix_send, mix_recv, to, 2 * chip + hand
        )

    for p in ORDER:
        mix_copy(p, 0).start()
        mix_copy(p, 1).start()
    mix_copy(0, 1).start()
    bring(mix_src.at[BLOCKS * core + b], mix.at[core, b], mix_recv)

    odd = lax.rem(b, 2)
    target = (owner_ref[...] + odd * (1 - 2 * lax.rem(owner_ref[...], 2))) * send_rows + slot_ref[...] - b * send_rows
    target = jnp.concatenate([target[i : i + 1] for i in range(BLOCKS)], axis=1)
    places = lax.broadcasted_iota(jnp.int32, (BLOCKS * send_rows, ROWS), 0)
    chosen = jnp.where(places == target, 1.0, 0.0).astype(bf16)
    token = lax.broadcasted_iota(jnp.int32, (16, ROWS), 1)
    which = lax.broadcasted_iota(jnp.int32, (16, ROWS), 0)
    digits = jnp.where(which == 0, lax.rem(token, 128), jnp.where(which == 1, lax.div(token, 128) + 1, 0))
    digits = lax.dot_general(
        digits.astype(f32).astype(bf16), chosen, (((1,), (1,)), ((), ())), preferred_element_type=f32
    )
    origin = (digits[0:1] + 128.0 * digits[1:2]).astype(jnp.int32)
    map_src[...] = jnp.concatenate([origin[:, 128 * n : 128 * (n + 1)] for n in range(8)], axis=0)

    def map_copy(p):
        to = peer(p)
        return remote(map_src, maps.at[b], map_send, map_recv, to, k)

    for p in ORDER:
        map_copy(p).start()
    bring(map_src, maps.at[b], map_recv)

    for way in range(2):
        side_arrived(way, 1 - way)
        for c in range(2):
            acc[...] += near(2 * (left, right)[way] + c)

    def g_copy(p, c, s):
        to = peer(p)
        hand = lax.rem(core + c, 2)
        return remote(
            g_src.at[s, BLOCKS * hand + to], g_came.at[s, core, b], g_send.at[s], g_recv.at[s], to, 2 * chip + hand
        )

    for s in range(2):
        part = acc[:, 128 * s : 128 * (s + 1)]
        for c in range(2):
            drain(og_all.at[2 * across + c, s], far_recv.at[s, c])
            part = part + term(2 * across + c, og_all[2 * across + c, s].reshape(128, ROWS))
        g_src[s] = part.astype(bf16).reshape(2 * BLOCKS, HELD, 128)
        for p in ORDER:
            g_copy(p, 0, s).start()
            g_copy(p, 1, s).start()
        g_copy(0, 1, s).start()
        bring(g_src.at[s, BLOCKS * core + b], g_came.at[s, core, b], g_recv.at[s])

    drain(mix, mix_recv)
    g_block = jnp.concatenate([g_src[s].reshape(2 * rows, 128) for s in range(2)], axis=1).astype(f32)
    gated = (g_block * mix[...].reshape(2 * rows, ROWS // 2).astype(f32)).astype(bf16).T
    for hand in range(2):
        gated_src[8 * hand : 8 * (hand + 1)] = gated[:, rows * hand : rows * (hand + 1)].reshape(8, ROWS // BLOCKS, rows)

    def gated_copy(q, c):
        column = lax.rem(b + q, 8)
        hand = lax.rem(core + c, 2)
        return remote(
            gated_src.at[8 * hand + column], gate_out.at[b],
            gated_send, gated_recv, 8 * core + column, 2 * chip + hand,
        )

    stays = lax.div(b, 8) == core
    own_gated = pltpu.make_async_copy(gated_src.at[8 * core + lax.rem(b, 8)], gate_out.at[b], gated_recv)
    for q in range(1, 8):
        gated_copy(q, 0).start()

    @pl.when(stays)
    def _():
        own_gated.start()

    @pl.when(jnp.logical_not(stays))
    def _():
        gated_copy(0, 0).start()

    drain(gate_came, gate_recv)
    for s in range(2):
        drain(g_came.at[s], g_recv.at[s])
    for q in range(8):
        gated_copy(q, 1).start()
    g = jnp.concatenate([g_came[s, h].reshape(rows, 128) for h in range(2) for s in range(2)], axis=1)
    g = g.astype(f32)
    dy = (g * gate_came[...].reshape(rows, ROWS).astype(f32)).astype(bf16)
    y_re, y_im = forward(dy, *forward_tables)

    def done_copy(p):
        to = peer(p)
        return remote(done.at[to], came.at[b], done_send, done_recv, to, k)

    lag = inverse(y_re * x_re + y_im * x_im, y_im * x_re - y_re * x_im, *inverse_tables)
    done[...] = to_columns(lag * (1.0 / math.sqrt(BLOCKS * ROWS))).astype(bf16).reshape(BLOCKS, HELD, ROWS)
    for p in ORDER:
        done_copy(p).start()
    bring(done.at[b], came.at[b], done_recv)
    grad = inverse(h_re * y_re + h_im * y_im, h_re * y_im - h_im * y_re, *inverse_tables)
    columns = to_columns(grad + skip * dy.astype(f32))
    drain(maps, map_recv)
    low_half = lax.broadcasted_iota(jnp.int32, (HELD, 128), 1) < 64
    for m in range(BLOCKS // 2):
        picked = []
        for j in (2 * m, 2 * m + 1):
            held = columns[j * HELD : (j + 1) * HELD]
            lane, tile = lax.rem(maps[j], 128), lax.div(maps[j], 128)
            tiles = []
            for n in range(8):
                at = jnp.broadcast_to(lane[n : n + 1], (HELD, 128))
                which = jnp.broadcast_to(tile[n : n + 1], (HELD, 128))
                value = jnp.zeros((HELD, 128), f32)
                for t in range(4):
                    found = jnp.take_along_axis(held[:, 128 * t : 128 * (t + 1)], at, axis=1)
                    value = jnp.where(which == t + 1, found, value)
                tiles.append(value)
            picked.append(tiles)
        for n in range(8):
            even, other = picked[0][n], picked[1][n]
            outbox[2 * n, :, 128 * m : 128 * (m + 1)] = jnp.where(low_half, even, other).astype(bf16)
            outbox[2 * n + 1, :, 128 * m : 128 * (m + 1)] = jnp.where(low_half, other, even).astype(bf16)

    def box_copy(p):
        to = peer(p)
        return remote(outbox.at[to], rows_out.at[b], box_send, box_recv, to, k)

    for p in ORDER:
        box_copy(p).start()
    bring(outbox.at[b], rows_out.at[b], box_recv)

    drain(came, done_recv)
    turned[...] = came[...].reshape(rows, ROWS).T
    result = bring(turned, filter_out)
    drain(og_all.at[0:2], far_send)
    drain(og_all.at[0:4], side_send)

    drain(gate_out, gated_recv)

    @pl.when(stays)
    def _():
        drain(gated_src.at[0:15], gated_send)

    @pl.when(jnp.logical_not(stays))
    def _():
        drain(gated_src, gated_send)

    few = BLOCKS - 1
    drain(pair_src.at[0:few], pair_send)
    drain(gate_src.at[0:few], gate_send)
    drain(mix_src.at[0 : BLOCKS + few], mix_send)
    for s in range(2):
        drain(g_src.at[s, 0 : BLOCKS + few], g_send.at[s])
    drain(maps.at[0:few], map_send)
    drain(done.at[0:few], done_send)
    drain(outbox.at[0:few], box_send)
    drain(rows_out, box_recv)
    result.wait()


ORDER = sorted(range(1, BLOCKS), key=lambda p: -(min(p // 4, 4 - p // 4) + min(p % 4, 4 - p % 4)))
TABLES = 8


def finish_kernel(gate_hbm, filter_hbm, rows_hbm, gate_out, filter_out, rows_out, gate, taps, wide, moved, ranked, sem):
    odd = lax.rem(lax.axis_index("bins"), 2)
    span = 256
    parts = rows_hbm.shape[1] // span
    reads = []

    def read(src, held):
        reads.append(pltpu.make_async_copy(src, held, sem.at[len(reads)]))
        reads[-1].start()
        return reads[-1]

    def write(held, dst, at):
        pltpu.make_async_copy(held, dst, sem.at[at]).start()

    taps_in = read(filter_hbm, taps)
    rows_in = [read(rows_hbm.at[:, pl.ds(n * span, span)], moved.at[n]) for n in range(parts)]
    gate_in = read(gate_hbm, gate)
    taps_in.wait()
    wide[...] = taps[...].astype(jnp.float32)
    write(wide, filter_out, 6)
    for n in range(parts):
        rows_in[n].wait()
        ranked[n] = moved[n].T.reshape(span // 64, 64, 256)
        for q in range(span // 64):
            group = n * (span // 64) + q
            group = group + odd * (1 - 2 * (q % 2))
            write(ranked.at[n, q], rows_out.at[pl.ds(group * 64, 64)], 7)
    gate_in.wait()
    write(gate, gate_out, 8)
    for ref, at in ((wide, 6), (ranked, 7), (gate, 8)):
        drain(ref, sem.at[at])


def finish(gate_grad, filter_grad, grad_rows):
    f32 = jnp.float32
    channels, count = grad_rows.shape
    return pl.pallas_call(
        finish_kernel,
        out_shape=(
            jax.ShapeDtypeStruct(gate_grad.shape, gate_grad.dtype),
            jax.ShapeDtypeStruct(filter_grad.shape, f32),
            jax.ShapeDtypeStruct((count, channels), grad_rows.dtype),
        ),
        in_specs=[pl.BlockSpec(memory_space=pl.ANY)] * 3,
        out_specs=(pl.BlockSpec(memory_space=pl.ANY),) * 3,
        scratch_shapes=[
            pltpu.VMEM(gate_grad.shape, gate_grad.dtype),
            pltpu.VMEM(filter_grad.shape, filter_grad.dtype),
            pltpu.VMEM(filter_grad.shape, f32),
            pltpu.VMEM((count // 256, channels, 256), grad_rows.dtype),
            pltpu.VMEM((count // 256, 4, 64, channels), grad_rows.dtype),
            pltpu.SemaphoreType.DMA((9,)),
        ],
        compiler_params=pltpu.CompilerParams(vmem_limit_bytes=67043328),
    )(gate_grad, filter_grad, grad_rows)


def shards(tokens_in, filters, gate, skip, out_grad, out_weight, owner, slot):
    channels = tokens_in.shape[1]
    send_rows = 2 * ROWS // BLOCKS
    half = ROWS // 2
    dma = pltpu.SemaphoreType.DMA
    one = dma(())
    hbm = pl.BlockSpec(memory_space=pl.ANY)
    f32, bf16 = jnp.float32, jnp.bfloat16
    constants = tables()
    operands = (
        tokens_in, filters, gate, skip.reshape(1, channels), out_grad.reshape(2, 2, 2, 64, ROWS), out_weight,
        owner, slot, *constants,
    )
    gate_grad, filter_grad, grad_rows = pl.pallas_call(
        kernel,
        out_shape=(
            jax.ShapeDtypeStruct((BLOCKS, ROWS // BLOCKS, channels), bf16),
            jax.ShapeDtypeStruct((ROWS, channels), bf16),
            jax.ShapeDtypeStruct((BLOCKS, HELD, BLOCKS * send_rows), bf16),
        ),
        in_specs=[hbm] * len(operands),
        out_specs=(hbm, hbm, hbm),
        scratch_shapes=[
            pltpu.VMEM((3, ROWS, channels), bf16),
            pltpu.VMEM((1, channels), f32),
            pltpu.VMEM(owner.shape, jnp.int32),
            pltpu.VMEM(slot.shape, jnp.int32),
            *(pltpu.VMEM(c.shape, c.dtype) for c in constants),
            pltpu.VMEM((2, channels, 8 * ROWS), bf16),
            pltpu.VMEM((8, 2, 2, 64, ROWS), bf16),
            pltpu.VMEM((2 * channels, half), f32),
            pltpu.VMEM((BLOCKS, 2, HELD, ROWS), bf16),
            pltpu.VMEM((BLOCKS, 2, HELD, ROWS), bf16),
            pltpu.VMEM((BLOCKS, HELD, ROWS), bf16),
            pltpu.VMEM((BLOCKS, HELD, ROWS), bf16),
            pltpu.VMEM((2 * BLOCKS, HELD, half), bf16),
            pltpu.VMEM((2, BLOCKS, HELD, half), bf16),
            pltpu.VMEM((2, 2 * BLOCKS, HELD, 128), bf16),
            pltpu.VMEM((2, 2, BLOCKS, HELD, 128), bf16),
            pltpu.VMEM((16, ROWS // BLOCKS, channels), bf16),
            pltpu.VMEM((BLOCKS, HELD, ROWS), bf16),
            pltpu.VMEM((BLOCKS, HELD, ROWS), bf16),
            pltpu.VMEM((BLOCKS, HELD, BLOCKS * send_rows), bf16),
            pltpu.VMEM((8, 128), jnp.int32),
            pltpu.VMEM((BLOCKS, 8, 128), jnp.int32),
            pltpu.VMEM((ROWS, channels), bf16),
            dma((17,)), dma((2,)), dma((2,)), one, dma((2, 2)), one, dma((2, 2)),
            one, one, one, one, one, one, dma((2,)), dma((2,)), one, one,
            one, one, one, one, one, one,
        ],
        compiler_params=pltpu.CompilerParams(
            collective_id=0, has_side_effects=True, vmem_limit_bytes=67043328
        ),
    )(*operands)
    gate_grad, filter_grad, grad_rows = finish(gate_grad, filter_grad, grad_rows.reshape(channels, -1))
    grid = (BLOCKS, ROWS // BLOCKS, channels)
    return (gate_grad, filter_grad.reshape(grid), grad_rows)


def solution(mesh):
    return jax.shard_map(
        shards,
        mesh=mesh,
        in_specs=(
            P("bins", "chan"),
            P("bins", "chan"),
            P("bins", "chan"),
            P("chan"),
            P("bins", "chan"),
            P("chan", None),
            P(None, "bins"),
            P(None, "bins"),
        ),
        out_specs=(P(None, "bins", "chan"), P(None, "bins", "chan"), P("bins", "chan")),
        check_vma=False,
    )
```

```python
import math

import jax
import jax.numpy as jnp
import numpy as np
from jax import lax
from jax.experimental import pallas as pl
from jax.experimental.pallas import tpu as pltpu
from jax.sharding import PartitionSpec as P

BLOCKS = 16
HELD = 16
ROWS = 512
HALF = BLOCKS + 1
LENGTH = 2 * BLOCKS * ROWS


def tables():
    k1 = np.arange(HALF)
    i = np.arange(BLOCKS)
    ang = 2.0 * np.pi * np.outer(k1, i) / (2 * BLOCKS)
    eye = np.eye(HELD)
    ahead = np.concatenate([np.kron(np.cos(ang), eye), np.kron(-np.sin(ang), eye)], axis=0)
    weight = np.where((k1 == 0) | (k1 == BLOCKS), 1.0, 2.0)[None, :] / LENGTH
    back_re = np.kron(weight * np.cos(ang).T, eye)
    back_im = np.kron(-(weight * np.sin(ang).T)[:, 1:BLOCKS], eye)
    back = np.concatenate([back_re, back_im], axis=1)
    r = np.arange(ROWS)
    twist = 2.0 * np.pi * np.outer(k1, r) / LENGTH
    m = np.arange(ROWS // 2)
    fold = 2.0 * np.pi * m[None, :] / ROWS
    inner = 2.0 * np.pi * (np.outer(m, m) % (ROWS // 2)) / (ROWS // 2)
    return (
        jnp.asarray(ahead, jnp.bfloat16),
        jnp.asarray(back, jnp.bfloat16),
        jnp.asarray(np.cos(twist)[:, None, :], jnp.float32),
        jnp.asarray(np.sin(twist)[:, None, :], jnp.float32),
        jnp.asarray(np.cos(fold), jnp.float32),
        jnp.asarray(np.sin(fold), jnp.float32),
        jnp.asarray(np.block([[np.cos(inner), -np.sin(inner)], [np.sin(inner), np.cos(inner)]]), jnp.bfloat16),
        jnp.asarray(np.block([[np.cos(inner), np.sin(inner)], [-np.sin(inner), np.cos(inner)]]), jnp.bfloat16),
    )


def mm(a, b):
    return jnp.dot(a, b, preferred_element_type=jnp.float32)


def stage_rows(value):
    return value.reshape(HALF, HELD, ROWS)


def flat(value):
    return value.reshape(HALF * HELD, ROWS)


def chunk_of(value, s):
    at, half = 128 * s, ROWS // 2
    return jnp.concatenate([value[..., at : at + 128], value[..., half + at : half + at + 128]], axis=-1)


def folded(value, s, ahead, tw_cos, tw_sin, fold_cos, fold_sin, inner, inner_back):
    part = mm(ahead, value)
    n = HALF * HELD
    grid, plain = (HALF, HELD, 256), (n, 256)
    re, im = part[:n].reshape(grid), part[n:].reshape(grid)
    tw_cos, tw_sin = chunk_of(tw_cos, s), chunk_of(tw_sin, s)
    z_re = (re * tw_cos + im * tw_sin).reshape(plain)
    z_im = (im * tw_cos - re * tw_sin).reshape(plain)
    fold_cos, fold_sin = fold_cos[:, 128 * s : 128 * (s + 1)], fold_sin[:, 128 * s : 128 * (s + 1)]
    diff_re, diff_im = z_re[:, :128] - z_re[:, 128:], z_im[:, :128] - z_im[:, 128:]
    re = jnp.concatenate([z_re[:, :128] + z_re[:, 128:], diff_re * fold_cos + diff_im * fold_sin], axis=0)
    im = jnp.concatenate([z_im[:, :128] + z_im[:, 128:], diff_im * fold_cos - diff_re * fold_sin], axis=0)
    return re.astype(jnp.bfloat16), im.astype(jnp.bfloat16)


def binned(first, second, inner):
    bins = mm(jnp.concatenate([first[0], second[0], first[1], second[1]], axis=1), inner)
    half = ROWS // 2
    return bins[:, :half], bins[:, half:]


def forward(value, *forward_tables):
    chunks = [folded(chunk_of(value, s), s, *forward_tables) for s in range(2)]
    return binned(*chunks, forward_tables[-2])


def inverse(s_re, s_im, back, tw_cos, tw_sin, fold_cos, fold_sin, inner, inner_back):
    n = HALF * HELD
    half = ROWS // 2
    q = mm(jnp.concatenate([s_re, s_im], axis=1).astype(jnp.bfloat16), inner_back)
    re, im = q[:, :half], q[:, half:]
    odd_re = re[n:] * fold_cos - im[n:] * fold_sin
    odd_im = im[n:] * fold_cos + re[n:] * fold_sin
    re = stage_rows(jnp.concatenate([re[:n] + odd_re, re[:n] - odd_re], axis=1))
    im = stage_rows(jnp.concatenate([im[:n] + odd_im, im[:n] - odd_im], axis=1))
    t_re = flat(re * tw_cos - im * tw_sin)
    t_im = flat(im * tw_cos + re * tw_sin)[HELD : BLOCKS * HELD]
    t = jnp.concatenate([t_re, t_im], axis=0).astype(jnp.bfloat16)
    return mm(back, t)


def to_columns(value):
    group = lax.broadcasted_iota(jnp.int32, (HELD, 128), 1) // 32
    out = [[None] * 4 for _ in range(BLOCKS)]
    for i_hi in range(4):
        for j_hi in range(4):
            tiles = [
                value[(4 * i_hi + i_lo) * HELD : (4 * i_hi + i_lo + 1) * HELD, 128 * j_hi : 128 * (j_hi + 1)]
                for i_lo in range(4)
            ]
            for j_lo in range(4):
                acc = None
                for i_lo in range(4):
                    shift = (32 * (i_lo - j_lo)) % 128
                    turned = pltpu.roll(tiles[i_lo], shift, 1) if shift else tiles[i_lo]
                    acc = turned if acc is None else jnp.where(group == i_lo, turned, acc)
                out[4 * j_hi + j_lo][i_hi] = acc
    return jnp.concatenate([jnp.concatenate(row, axis=1) for row in out], axis=0)


def remote(src, dst, send, recv, bins, chan):
    return pltpu.make_async_remote_copy(
        src_ref=src,
        dst_ref=dst,
        send_sem=send,
        recv_sem=recv,
        device_id=(bins, chan),
        device_id_type=pl.DeviceIdType.MESH,
    )


def drain(ref, sem):
    pltpu.make_async_copy(ref, ref, sem).wait()


def kernel(
    x_hbm, h_hbm, gate_hbm, skip_hbm, og_hbm, w_hbm, owner_hbm, slot_hbm, *rest
):
    tables_hbm, rest = rest[:TABLES], rest[TABLES:]
    gate_out, filter_out, rows_out = rest[:3]
    (
        raw, skip_ref, owner_ref, slot_ref, *rest
    ) = rest[3:]
    tables_ref, rest = rest[:TABLES], rest[TABLES:]
    (
        w_all, og_all, acc, pair_src, pair, gate_src, gate_came, mix_src, mix, g_src, g_came, gated_src,
        done, came, outbox, map_src, maps, turned,
        local_sem, w_sem, mate_sem, side_send, side_recv, far_send, far_recv,
        pair_send, pair_recv, gate_send, gate_recv, mix_send, mix_recv, g_send, g_recv, gated_send, gated_recv,
        done_send, done_recv, box_send, box_recv, map_send, map_recv,
    ) = rest
    f32, bf16 = jnp.float32, jnp.bfloat16
    rows = BLOCKS * HELD
    send_rows = 2 * ROWS // BLOCKS
    b = lax.axis_index("bins")
    k = lax.axis_index("chan")
    b_y, b_z = lax.div(b, 4), lax.rem(b, 4)
    chip, core = lax.div(k, 2), lax.rem(k, 2)
    right, left, across = lax.rem(chip + 1, 4), lax.rem(chip + 3, 4), lax.rem(chip + 2, 4)
    mate = 2 * chip + 1 - core

    along_y = [4 * lax.rem(b_y + n, 4) for n in range(4)]
    along_z = [lax.rem(b_z + n, 4) for n in range(4)]

    def peer(p):
        return along_y[p // 4] + along_z[p % 4]

    barrier = pltpu.get_barrier_semaphore()

    def greet(bins, chan):
        pl.semaphore_signal(barrier, inc=1, device_id=(bins, chan), device_id_type=pl.DeviceIdType.MESH)

    for p in ORDER:
        greet(peer(p), k)
        greet(peer(p), mate)
    greet(b, mate)
    for side in (right, left):
        for c in range(2):
            greet(b, 2 * side + c)

    local = []

    def bring(src, dst, sem=None):
        copy = pltpu.make_async_copy(src, dst, local_sem.at[len(local)] if sem is None else sem)
        copy.start()
        if sem is None:
            local.append(copy)
        return copy

    own_raw = [bring(ref, raw.at[n]) for n, ref in enumerate((x_hbm, h_hbm, gate_hbm))]
    own_og = bring(og_hbm.at[core], og_all.at[k])
    own_w = bring(w_hbm, w_all.at[core])
    own_small = [bring(*pair) for pair in ((skip_hbm, skip_ref), (owner_hbm, owner_ref), (slot_hbm, slot_ref))]
    own_tables = [bring(*pair) for pair in zip(tables_hbm, tables_ref)]

    pl.semaphore_wait(barrier, 2 * BLOCKS - 1 + 4)

    def side_copy(way, part, c):
        to = (right, left)[way]
        return remote(
            og_hbm.at[c, :, part], og_all.at[k, :, part],
            side_send, side_recv.at[way, part], b, 2 * to + c,
        )

    for turn in range(2):
        for c in range(2):
            side_copy(0, turn, c).start()
            side_copy(1, 1 - turn, c).start()
    mate_og = remote(og_hbm.at[1 - core], og_all.at[k], mate_sem.at[0], mate_sem.at[1], b, mate)
    mate_og.start()
    mate_w = remote(w_hbm, w_all.at[core], w_sem.at[0], w_sem.at[1], b, mate)
    mate_w.start()

    for n in range(2):
        own_raw[n].wait()
        pair_src[:, n] = raw[n].T.reshape(BLOCKS, HELD, ROWS)

    def pair_copy(p):
        to = peer(p)
        return remote(pair_src.at[to], pair.at[b], pair_send, pair_recv, to, k)

    for p in ORDER:
        pair_copy(p).start()
    bring(pair_src.at[b], pair.at[b], pair_recv)
    own_raw[2].wait()
    gate_src[...] = raw[2].T.reshape(BLOCKS, HELD, ROWS)

    def gate_copy(p):
        to = peer(p)
        return remote(gate_src.at[to], gate_came.at[b], gate_send, gate_recv, to, k)

    for p in ORDER:
        gate_copy(p).start()
    bring(gate_src.at[b], gate_came.at[b], gate_recv)

    def side_arrived(way, part):
        src = 2 * (left, right)[way]
        drain(og_all.at[pl.ds(src, 2), :, part], side_recv.at[way, part])

    def far_copy(way, c, s):
        src = 2 * (left, right)[way] + c
        to = (right, left)[way]
        return remote(
            og_all.at[src, s, way], og_all.at[src, s, way],
            far_send, far_recv.at[s, c], b, 2 * to + core,
        )

    for way in range(2):
        side_arrived(way, way)
    for s in range(2):
        for c in range(2):
            for way in range(2):
                far_copy(way, c, s).start()

    def term(source, tokens):
        columns = pl.ds(pl.multiple_of(source * ROWS, ROWS), ROWS)
        weights = w_all[:, :, columns].reshape(2 * rows, ROWS)
        return lax.dot_general(weights, tokens, (((1,), (1,)), ((), ())), preferred_element_type=f32)

    def near(source):
        return term(source, og_all[source].reshape(ROWS // 2, ROWS))

    own_w.wait()
    own_og.wait()
    mate_w.wait()
    mate_og.wait()
    acc[...] = near(k) + near(mate)

    for copy in own_small + own_tables:
        copy.wait()
    ahead, back, *shared = (ref[...] for ref in tables_ref)
    forward_tables, inverse_tables = (ahead, *shared), (back, *shared)
    lanes = lax.broadcasted_iota(jnp.int32, (rows, rows), 1)
    held = lax.rem(lax.broadcasted_iota(jnp.int32, (rows, rows), 0), HELD)
    skip = jnp.sum(jnp.where(lanes == held + HELD * b, skip_ref[...], 0.0), axis=1, keepdims=True)
    drain(pair, pair_recv)
    x = pair[:, 0].reshape(rows, ROWS)
    x_re, x_im = forward(x, *forward_tables)
    h_re, h_im = forward(pair[:, 1].reshape(rows, ROWS), *forward_tables)
    conv = inverse(x_re * h_re - x_im * h_im, x_re * h_im + x_im * h_re, *inverse_tables)
    with_skip = (conv + skip * x.astype(f32)).astype(bf16)
    for hand in range(2):
        mix_src[BLOCKS * hand : BLOCKS * (hand + 1)] = with_skip[:, rows * hand : rows * (hand + 1)].reshape(BLOCKS, HELD, ROWS // 2)

    def mix_copy(p, c):
        to = peer(p)
        hand = lax.rem(core + c, 2)
        return remote(
            mix_src.at[BLOCKS * hand + to], mix.at[core, b], mix_send, mix_recv, to, 2 * chip + hand
        )

    for p in ORDER:
        mix_copy(p, 0).start()
        mix_copy(p, 1).start()
    mix_copy(0, 1).start()
    bring(mix_src.at[BLOCKS * core + b], mix.at[core, b], mix_recv)

    odd = lax.rem(b, 2)
    target = (owner_ref[...] + odd * (1 - 2 * lax.rem(owner_ref[...], 2))) * send_rows + slot_ref[...] - b * send_rows
    target = jnp.concatenate([target[i : i + 1] for i in range(BLOCKS)], axis=1)
    places = lax.broadcasted_iota(jnp.int32, (BLOCKS * send_rows, ROWS), 0)
    chosen = jnp.where(places == target, 1.0, 0.0).astype(bf16)
    token = lax.broadcasted_iota(jnp.int32, (16, ROWS), 1)
    which = lax.broadcasted_iota(jnp.int32, (16, ROWS), 0)
    digits = jnp.where(which == 0, lax.rem(token, 128), jnp.where(which == 1, lax.div(token, 128) + 1, 0))
    digits = lax.dot_general(
        digits.astype(f32).astype(bf16), chosen, (((1,), (1,)), ((), ())), preferred_element_type=f32
    )
    origin = (digits[0:1] + 128.0 * digits[1:2]).astype(jnp.int32)
    map_src[...] = jnp.concatenate([origin[:, 128 * n : 128 * (n + 1)] for n in range(8)], axis=0)

    def map_copy(p):
        to = peer(p)
        return remote(map_src, maps.at[b], map_send, map_recv, to, k)

    for p in ORDER:
        map_copy(p).start()
    bring(map_src, maps.at[b], map_recv)

    for way in range(2):
        side_arrived(way, 1 - way)
        for c in range(2):
            acc[...] += near(2 * (left, right)[way] + c)

    def g_copy(p, c, s):
        to = peer(p)
        hand = lax.rem(core + c, 2)
        return remote(
            g_src.at[s, BLOCKS * hand + to], g_came.at[s, core, b], g_send.at[s], g_recv.at[s], to, 2 * chip + hand
        )

    for s in range(2):
        part = acc[:, 128 * s : 128 * (s + 1)]
        for c in range(2):
            drain(og_all.at[2 * across + c, s], far_recv.at[s, c])
            part = part + term(2 * across + c, og_all[2 * across + c, s].reshape(128, ROWS))
        g_src[s] = part.astype(bf16).reshape(2 * BLOCKS, HELD, 128)
        for p in ORDER:
            g_copy(p, 0, s).start()
            g_copy(p, 1, s).start()
        g_copy(0, 1, s).start()
        bring(g_src.at[s, BLOCKS * core + b], g_came.at[s, core, b], g_recv.at[s])

    drain(mix, mix_recv)
    g_block = jnp.concatenate([g_src[s].reshape(2 * rows, 128) for s in range(2)], axis=1).astype(f32)
    gated = (g_block * mix[...].reshape(2 * rows, ROWS // 2).astype(f32)).astype(bf16).T
    for hand in range(2):
        gated_src[8 * hand : 8 * (hand + 1)] = gated[:, rows * hand : rows * (hand + 1)].reshape(8, ROWS // BLOCKS, rows)

    def gated_copy(q, c):
        column = lax.rem(b + q, 8)
        hand = lax.rem(core + c, 2)
        return remote(
            gated_src.at[8 * hand + column], gate_out.at[b],
            gated_send, gated_recv, 8 * core + column, 2 * chip + hand,
        )

    stays = lax.div(b, 8) == core
    own_gated = pltpu.make_async_copy(gated_src.at[8 * core + lax.rem(b, 8)], gate_out.at[b], gated_recv)
    for q in range(1, 8):
        gated_copy(q, 0).start()
        gated_copy(q, 1).start()
    gated_copy(0, 1).start()

    @pl.when(stays)
    def _():
        own_gated.start()

    @pl.when(jnp.logical_not(stays))
    def _():
        gated_copy(0, 0).start()

    drain(gate_came, gate_recv)
    gate_rows = gate_came[...].reshape(rows, ROWS)
    chunks, dys = [], []
    for s in range(2):
        drain(g_came.at[s], g_recv.at[s])
        g = jnp.concatenate([g_came[s, h].reshape(rows, 128) for h in range(2)], axis=1).astype(f32)
        dys.append((g * chunk_of(gate_rows, s).astype(f32)).astype(bf16))
        chunks.append(folded(dys[s], s, *forward_tables))
    y_re, y_im = binned(*chunks, forward_tables[-2])
    dy = jnp.concatenate([dys[s][:, 128 * h : 128 * (h + 1)] for h in range(2) for s in range(2)], axis=1)

    def done_copy(p):
        to = peer(p)
        return remote(done.at[to], came.at[b], done_send, done_recv, to, k)

    lag = inverse(y_re * x_re + y_im * x_im, y_im * x_re - y_re * x_im, *inverse_tables)
    done[...] = to_columns(lag * (1.0 / math.sqrt(BLOCKS * ROWS))).astype(bf16).reshape(BLOCKS, HELD, ROWS)
    for p in ORDER:
        done_copy(p).start()
    bring(done.at[b], came.at[b], done_recv)
    grad = inverse(h_re * y_re + h_im * y_im, h_re * y_im - h_im * y_re, *inverse_tables)
    columns = to_columns(grad + skip * dy.astype(f32))
    drain(maps, map_recv)
    low_half = lax.broadcasted_iota(jnp.int32, (HELD, 128), 1) < 64
    for m in range(BLOCKS // 2):
        picked = []
        for j in (2 * m, 2 * m + 1):
            held = columns[j * HELD : (j + 1) * HELD]
            lane, tile = lax.rem(maps[j], 128), lax.div(maps[j], 128)
            tiles = []
            for n in range(8):
                at = jnp.broadcast_to(lane[n : n + 1], (HELD, 128))
                which = jnp.broadcast_to(tile[n : n + 1], (HELD, 128))
                value = jnp.zeros((HELD, 128), f32)
                for t in range(4):
                    found = jnp.take_along_axis(held[:, 128 * t : 128 * (t + 1)], at, axis=1)
                    value = jnp.where(which == t + 1, found, value)
                tiles.append(value)
            picked.append(tiles)
        for n in range(8):
            even, other = picked[0][n], picked[1][n]
            outbox[2 * n, :, 128 * m : 128 * (m + 1)] = jnp.where(low_half, even, other).astype(bf16)
            outbox[2 * n + 1, :, 128 * m : 128 * (m + 1)] = jnp.where(low_half, other, even).astype(bf16)

    def box_copy(p):
        to = peer(p)
        return remote(outbox.at[to], rows_out.at[b], box_send, box_recv, to, k)

    for p in ORDER:
        box_copy(p).start()
    bring(outbox.at[b], rows_out.at[b], box_recv)

    drain(came, done_recv)
    turned[...] = came[...].reshape(rows, ROWS).T
    result = bring(turned, filter_out)
    drain(og_all.at[0:2], far_send)
    drain(og_all.at[0:4], side_send)

    drain(gate_out, gated_recv)

    @pl.when(stays)
    def _():
        drain(gated_src.at[0:15], gated_send)

    @pl.when(jnp.logical_not(stays))
    def _():
        drain(gated_src, gated_send)

    few = BLOCKS - 1
    drain(pair_src.at[0:few], pair_send)
    drain(gate_src.at[0:few], gate_send)
    drain(mix_src.at[0 : BLOCKS + few], mix_send)
    for s in range(2):
        drain(g_src.at[s, 0 : BLOCKS + few], g_send.at[s])
    drain(maps.at[0:few], map_send)
    drain(done.at[0:few], done_send)
    drain(outbox.at[0:few], box_send)
    drain(rows_out, box_recv)
    result.wait()


ORDER = sorted(range(1, BLOCKS), key=lambda p: -(min(p // 4, 4 - p // 4) + min(p % 4, 4 - p % 4)))
TABLES = 8


def finish_kernel(gate_hbm, filter_hbm, rows_hbm, gate_out, filter_out, rows_out, gate, taps, wide, moved, ranked, sem):
    odd = lax.rem(lax.axis_index("bins"), 2)
    span = 256
    parts = rows_hbm.shape[1] // span
    reads = []

    def read(src, held):
        reads.append(pltpu.make_async_copy(src, held, sem.at[len(reads)]))
        reads[-1].start()
        return reads[-1]

    def write(held, dst, at):
        pltpu.make_async_copy(held, dst, sem.at[at]).start()

    taps_in = read(filter_hbm, taps)
    rows_in = [read(rows_hbm.at[:, pl.ds(n * span, span)], moved.at[n]) for n in range(parts)]
    gate_in = read(gate_hbm, gate)
    taps_in.wait()
    wide[...] = taps[...].astype(jnp.float32)
    write(wide, filter_out, 6)
    for n in range(parts):
        rows_in[n].wait()
        ranked[n] = moved[n].T.reshape(span // 64, 64, 256)
        for q in range(span // 64):
            group = n * (span // 64) + q
            group = group + odd * (1 - 2 * (q % 2))
            write(ranked.at[n, q], rows_out.at[pl.ds(group * 64, 64)], 7)
    gate_in.wait()
    write(gate, gate_out, 8)
    for ref, at in ((wide, 6), (ranked, 7), (gate, 8)):
        drain(ref, sem.at[at])


def finish(gate_grad, filter_grad, grad_rows):
    f32 = jnp.float32
    channels, count = grad_rows.shape
    return pl.pallas_call(
        finish_kernel,
        out_shape=(
            jax.ShapeDtypeStruct(gate_grad.shape, gate_grad.dtype),
            jax.ShapeDtypeStruct(filter_grad.shape, f32),
            jax.ShapeDtypeStruct((count, channels), grad_rows.dtype),
        ),
        in_specs=[pl.BlockSpec(memory_space=pl.ANY)] * 3,
        out_specs=(pl.BlockSpec(memory_space=pl.ANY),) * 3,
        scratch_shapes=[
            pltpu.VMEM(gate_grad.shape, gate_grad.dtype),
            pltpu.VMEM(filter_grad.shape, filter_grad.dtype),
            pltpu.VMEM(filter_grad.shape, f32),
            pltpu.VMEM((count // 256, channels, 256), grad_rows.dtype),
            pltpu.VMEM((count // 256, 4, 64, channels), grad_rows.dtype),
            pltpu.SemaphoreType.DMA((9,)),
        ],
        compiler_params=pltpu.CompilerParams(vmem_limit_bytes=67043328),
    )(gate_grad, filter_grad, grad_rows)


def shards(tokens_in, filters, gate, skip, out_grad, out_weight, owner, slot):
    channels = tokens_in.shape[1]
    send_rows = 2 * ROWS // BLOCKS
    half = ROWS // 2
    dma = pltpu.SemaphoreType.DMA
    one = dma(())
    hbm = pl.BlockSpec(memory_space=pl.ANY)
    f32, bf16 = jnp.float32, jnp.bfloat16
    constants = tables()
    operands = (
        tokens_in, filters, gate, skip.reshape(1, channels), out_grad.reshape(2, 2, 2, 64, ROWS), out_weight,
        owner, slot, *constants,
    )
    gate_grad, filter_grad, grad_rows = pl.pallas_call(
        kernel,
        out_shape=(
            jax.ShapeDtypeStruct((BLOCKS, ROWS // BLOCKS, channels), bf16),
            jax.ShapeDtypeStruct((ROWS, channels), bf16),
            jax.ShapeDtypeStruct((BLOCKS, HELD, BLOCKS * send_rows), bf16),
        ),
        in_specs=[hbm] * len(operands),
        out_specs=(hbm, hbm, hbm),
        scratch_shapes=[
            pltpu.VMEM((3, ROWS, channels), bf16),
            pltpu.VMEM((1, channels), f32),
            pltpu.VMEM(owner.shape, jnp.int32),
            pltpu.VMEM(slot.shape, jnp.int32),
            *(pltpu.VMEM(c.shape, c.dtype) for c in constants),
            pltpu.VMEM((2, channels, 8 * ROWS), bf16),
            pltpu.VMEM((8, 2, 2, 64, ROWS), bf16),
            pltpu.VMEM((2 * channels, half), f32),
            pltpu.VMEM((BLOCKS, 2, HELD, ROWS), bf16),
            pltpu.VMEM((BLOCKS, 2, HELD, ROWS), bf16),
            pltpu.VMEM((BLOCKS, HELD, ROWS), bf16),
            pltpu.VMEM((BLOCKS, HELD, ROWS), bf16),
            pltpu.VMEM((2 * BLOCKS, HELD, half), bf16),
            pltpu.VMEM((2, BLOCKS, HELD, half), bf16),
            pltpu.VMEM((2, 2 * BLOCKS, HELD, 128), bf16),
            pltpu.VMEM((2, 2, BLOCKS, HELD, 128), bf16),
            pltpu.VMEM((16, ROWS // BLOCKS, channels), bf16),
            pltpu.VMEM((BLOCKS, HELD, ROWS), bf16),
            pltpu.VMEM((BLOCKS, HELD, ROWS), bf16),
            pltpu.VMEM((BLOCKS, HELD, BLOCKS * send_rows), bf16),
            pltpu.VMEM((8, 128), jnp.int32),
            pltpu.VMEM((BLOCKS, 8, 128), jnp.int32),
            pltpu.VMEM((ROWS, channels), bf16),
            dma((17,)), dma((2,)), dma((2,)), one, dma((2, 2)), one, dma((2, 2)),
            one, one, one, one, one, one, dma((2,)), dma((2,)), one, one,
            one, one, one, one, one, one,
        ],
        compiler_params=pltpu.CompilerParams(
            collective_id=0, has_side_effects=True, vmem_limit_bytes=67043328
        ),
    )(*operands)
    gate_grad, filter_grad, grad_rows = finish(gate_grad, filter_grad, grad_rows.reshape(channels, -1))
    grid = (BLOCKS, ROWS // BLOCKS, channels)
    return (gate_grad, filter_grad.reshape(grid), grad_rows)


def solution(mesh):
    return jax.shard_map(
        shards,
        mesh=mesh,
        in_specs=(
            P("bins", "chan"),
            P("bins", "chan"),
            P("bins", "chan"),
            P("chan"),
            P("bins", "chan"),
            P("chan", None),
            P(None, "bins"),
            P(None, "bins"),
        ),
        out_specs=(P(None, "bins", "chan"), P(None, "bins", "chan"), P("bins", "chan")),
        check_vma=False,
    )
```
